32 devices in a mesh: seq: 8 (over z, y), tensor: 4 (over x, core).
Axes of the slice: x: 2, y: 2, z: 4, core: 2. Of those that a mesh axis runs over, the one named last changes fastest.
Arguments:
- hidden_in: bfloat16 [1024, 2048], P('seq'), may hold values from -6 to 6
- norm_gain: float32 [2048], replicated, may hold values from 0.1 to 1.9
- query_weight: bfloat16 [2048, 2048], P(None, 'tensor'), may hold values from -0.125 to 0.125
- key_weight: bfloat16 [2048, 1024], P(None, 'tensor'), may hold values from -0.375 to 0.375
- value_weight: bfloat16 [2048, 1024], P(None, 'tensor'), may hold values from -0.125 to 0.125
- out_weight: bfloat16 [2048, 2048], P('tensor'), may hold values from -0.125 to 0.125
- key_cache: bfloat16 [512, 128, 1024], P('seq', None, 'tensor'), may hold values from -102 to 102
- value_cache: bfloat16 [512, 128, 1024], P('seq', None, 'tensor'), may hold values from -6 to 6
- cached_lengths: int32 [2], replicated, may hold values from 16385 to 32768, as said below
- group_ids: int32 [2], replicated, may hold values from 0 to 1
- prompt_pages: int32 [2, 128], replicated, may hold values from 0 to 511, as said below
- own_pages: int32 [2, 128], replicated, may hold values from 0 to 511, as said below
Outputs:
- attention_out: bfloat16 [1024, 2048], P('seq', 'tensor')
The draws below stay inside these ranges and needn't reach their ends.
Inputs may be any that keep to these rules, and one draw needn't show every extreme that they name: `cached_lengths`: each request's cache holds the 16384 tokens of its group's prompt followed by its own tokens; some request holds the most in every draw. Slot s is page s % 64 of seq index s // 64; no slot is named twice in prompt_pages and own_pages together. `own_pages`: page p of request r holds its own cached tokens from p * 128 on; entries past a request's length name slots whose contents are not read.
All inputs are finite; a program needn't handle non-finite values.
Results may differ from the reference program's by a relative error of at most 0.0055.
The reference program's roundings to bfloat16 on the way count: a program that leaves them out, or rounds other values in their place, can miss the bound.
Values may be sent and summed in bfloat16 or wider, within the bound.
A program may use at most 64 MiB of HBM per device.

```python
import math
import jax
import jax.numpy as jnp
from jax import lax

D = 2048
Q_HEADS = 16
KV_HEADS = 8
HEAD_DIM = 128
PAGE_ROWS = 128
ADDED_TOKENS = 512
REQUESTS = 2
GROUPS = 2
PROMPT_PAGES = 128
OWN_PAGES_MAX = 128
TOKENS = 1024
TOK_DEV = 128
PAGES_DEV = 64
CACHE_SLOTS = 512
N_SEQ = 8


def page_order(key):
    return jax.random.permutation(jax.random.fold_in(key, 11), CACHE_SLOTS).astype(jnp.int32)


def draw_prompt_pages(key, part):
    slot_order = page_order(key)
    return slot_order[:GROUPS * PROMPT_PAGES].reshape(GROUPS, PROMPT_PAGES)


def draw_own_pages(key, part):
    slot_order = page_order(key)
    first_own = GROUPS * PROMPT_PAGES
    return slot_order[first_own:first_own + REQUESTS * OWN_PAGES_MAX].reshape(REQUESTS, OWN_PAGES_MAX)


def draw_cached_lengths(key, part):
    own_tokens = jax.random.randint(jax.random.fold_in(key, 21), (REQUESTS,), 1, OWN_PAGES_MAX * PAGE_ROWS + 1, dtype=jnp.int32)
    longest = jax.random.randint(jax.random.fold_in(key, 22), (), 0, REQUESTS, dtype=jnp.int32)
    own_tokens = jnp.where(jnp.arange(REQUESTS, dtype=jnp.int32) == longest, OWN_PAGES_MAX * PAGE_ROWS, own_tokens)
    return (PROMPT_PAGES * PAGE_ROWS + own_tokens).astype(jnp.int32)


def draw_key_cache(key, part):
    shape = (CACHE_SLOTS, PAGE_ROWS, KV_HEADS * HEAD_DIM)
    cached = jnp.clip(jax.random.normal(jax.random.fold_in(key, 35), shape, jnp.float32) * 3.0, -12.0, 12.0)
    return cached.astype(jnp.bfloat16)


def block_scale(key, extent, split, low, top_value):
    gain, own = 1.0, jax.random.fold_in(key, 6)
    for position, parts in split:
        steps = jnp.exp(jax.random.uniform(jax.random.fold_in(own, position), (parts,), jnp.float32, low / len(split), top_value / len(split)))
        gain = gain * jnp.repeat(steps, extent[position] // parts).reshape([-1 if axis == position else 1 for axis in range(len(extent))])
    return gain


def centred(stream_key, dims, deviation, limit, cuts=(), kind=jnp.bfloat16):
    drawn = jax.random.normal(stream_key, dims, jnp.float32) * deviation
    if len(cuts) > 0:
        drawn = block_scale(stream_key, dims, cuts, -0.22, 0.18) * drawn
    return jnp.clip(drawn, min=-limit, max=limit).astype(kind)


def setup_inputs(seed: int = 0) -> dict:
    keys = jax.random.split(jax.random.key(seed), 13)
    hidden_in = centred(keys[0], (TOKENS, D), 1.0, 6.0, ((0, 8),))
    norm_gain = jnp.clip(1.0 + 0.18 * jax.random.normal(keys[1], (D,), jnp.float32), 0.1, 1.9)
    query_weight = centred(keys[2], (D, Q_HEADS * HEAD_DIM), D ** -0.5, 0.125, ((1, 4),))
    key_weight = centred(keys[3], (D, KV_HEADS * HEAD_DIM), (D // 9) ** -0.5, 0.375, ((1, 4),))
    value_weight = centred(keys[4], (D, KV_HEADS * HEAD_DIM), D ** -0.5, 0.125, ((1, 4),))
    out_weight = centred(keys[5], (Q_HEADS * HEAD_DIM, D), (Q_HEADS * HEAD_DIM) ** -0.5, 0.125, ((0, 4),))
    key_cache = draw_key_cache(jax.random.fold_in(keys[12], 71), 0)
    value_cache = centred(keys[7], (CACHE_SLOTS, PAGE_ROWS, KV_HEADS * HEAD_DIM), 1.0, 6.0, ((0, 8), (2, 4)))
    cached_lengths = draw_cached_lengths(jax.random.fold_in(keys[12], 71), 0)
    group_ids = jax.random.randint(keys[9], (REQUESTS,), 0, GROUPS).astype(jnp.int32)
    prompt_pages = draw_prompt_pages(jax.random.fold_in(keys[12], 71), 0)
    own_pages = draw_own_pages(jax.random.fold_in(keys[12], 71), 0)
    return {"hidden_in": hidden_in, "norm_gain": norm_gain, "query_weight": query_weight, "key_weight": key_weight, "value_weight": value_weight, "out_weight": out_weight, "key_cache": key_cache, "value_cache": value_cache, "cached_lengths": cached_lengths, "group_ids": group_ids, "prompt_pages": prompt_pages, "own_pages": own_pages}


def block_terms(query_grid, key_grid, value_grid, live_mask, score_scale):
    scores = jnp.einsum('qkgd,pkd->qkgp', query_grid, key_grid) * score_scale
    live_grid = live_mask[:, None, None, :]
    block_max = lax.optimization_barrier(jnp.max(jnp.where(live_grid, scores, -1e+30), axis=-1))
    weights = jnp.exp(jnp.where(live_grid, scores - block_max[..., None], -1e+30)).astype(jnp.bfloat16)
    weights_wide = lax.optimization_barrier(weights).astype(jnp.float32)
    block_sum = lax.optimization_barrier(jnp.sum(weights_wide, axis=-1))
    block_out = jnp.einsum('qkgp,pkd->qkgd', weights_wide, value_grid)
    return (block_max, block_out, block_sum)

def combine_terms(running, terms):
    run_max, run_num, run_den = running
    part_max, part_num, part_den = terms
    new_max = jnp.maximum(run_max, part_max)
    keep_scale = jnp.exp(run_max - new_max)
    add_scale = jnp.exp(part_max - new_max)
    return (new_max, run_num * keep_scale[..., None] + part_num * add_scale[..., None], run_den * keep_scale + part_den * add_scale)

def reference(hidden_in, norm_gain, query_weight, key_weight, value_weight, out_weight, key_cache, value_cache, cached_lengths, group_ids, prompt_pages, own_pages):
    floats = hidden_in.astype(jnp.float32)
    normed = (floats * lax.rsqrt(lax.optimization_barrier(jnp.mean(floats * floats, axis=-1, keepdims=True)) + 1e-05) * norm_gain).astype(jnp.bfloat16)
    queries = jnp.dot(normed, query_weight, preferred_element_type=jnp.float32).astype(jnp.bfloat16)
    keys_new = jnp.dot(normed, key_weight, preferred_element_type=jnp.float32).astype(jnp.bfloat16)
    values_new = jnp.dot(normed, value_weight, preferred_element_type=jnp.float32).astype(jnp.bfloat16)
    per_kv = Q_HEADS // KV_HEADS
    score_scale = 1.0 / math.sqrt(HEAD_DIM)
    new_blocks = ADDED_TOKENS // PAGE_ROWS
    key_pos = jnp.arange(PAGE_ROWS, dtype=jnp.int32)
    query_pos = jnp.arange(ADDED_TOKENS, dtype=jnp.int32)
    seq_ids = jnp.arange(N_SEQ, dtype=jnp.int32)

    def one_request(request):
        row_start = request * ADDED_TOKENS
        query_grid = lax.dynamic_slice_in_dim(queries, row_start, ADDED_TOKENS, 0).astype(jnp.float32)
        query_grid = query_grid.reshape(ADDED_TOKENS, KV_HEADS, per_kv, HEAD_DIM)
        group_id = lax.dynamic_index_in_dim(group_ids, request, 0, keepdims=False)
        prompt_row = lax.dynamic_index_in_dim(prompt_pages, group_id, 0, keepdims=False)
        own_row = lax.dynamic_index_in_dim(own_pages, request, 0, keepdims=False)
        own_len = lax.dynamic_index_in_dim(cached_lengths, request, 0, keepdims=False) - PROMPT_PAGES * PAGE_ROWS
        slot_ids = jnp.concatenate([prompt_row, own_row]).astype(jnp.int32)
        block_pos = jnp.arange(PROMPT_PAGES + OWN_PAGES_MAX, dtype=jnp.int32)
        live_counts = jnp.where(block_pos < PROMPT_PAGES, PAGE_ROWS, jnp.clip(own_len - (block_pos - PROMPT_PAGES) * PAGE_ROWS, 0, PAGE_ROWS)).astype(jnp.int32)
        initial = (jnp.full((N_SEQ, ADDED_TOKENS, KV_HEADS, per_kv), -1e+30, jnp.float32), jnp.zeros((N_SEQ, ADDED_TOKENS, KV_HEADS, per_kv, HEAD_DIM), jnp.float32), jnp.zeros((N_SEQ, ADDED_TOKENS, KV_HEADS, per_kv), jnp.float32))

        def cache_step(running, entry_data):
            slot_id, live_count = entry_data
            owner = (slot_id // PAGES_DEV).astype(jnp.int32)
            page_keys = lax.dynamic_index_in_dim(key_cache, slot_id, 0, keepdims=False).astype(jnp.float32)
            page_values = lax.dynamic_index_in_dim(value_cache, slot_id, 0, keepdims=False).astype(jnp.float32)
            live_mask = jnp.broadcast_to((key_pos < live_count)[None, :], (ADDED_TOKENS, PAGE_ROWS))
            terms = block_terms(query_grid, page_keys.reshape(PAGE_ROWS, KV_HEADS, HEAD_DIM), page_values.reshape(PAGE_ROWS, KV_HEADS, HEAD_DIM), live_mask, score_scale)
            current = tuple((lax.dynamic_index_in_dim(member, owner, 0, keepdims=False) for member in running))
            merged = combine_terms(current, terms)
            return (tuple((lax.dynamic_update_index_in_dim(member, updated, owner, 0) for member, updated in zip(running, merged))), None)
        running, _ = lax.scan(cache_step, initial, (slot_ids, live_counts))
        block_keys = lax.dynamic_slice_in_dim(keys_new, row_start, ADDED_TOKENS, 0).astype(jnp.float32)
        block_values = lax.dynamic_slice_in_dim(values_new, row_start, ADDED_TOKENS, 0).astype(jnp.float32)
        block_keys = block_keys.reshape(new_blocks, PAGE_ROWS, KV_HEADS, HEAD_DIM)
        block_values = block_values.reshape(new_blocks, PAGE_ROWS, KV_HEADS, HEAD_DIM)
        fresh = (jnp.full((ADDED_TOKENS, KV_HEADS, per_kv), -1e+30, jnp.float32), jnp.zeros((ADDED_TOKENS, KV_HEADS, per_kv, HEAD_DIM), jnp.float32), jnp.zeros((ADDED_TOKENS, KV_HEADS, per_kv), jnp.float32))
        for block_index in range(new_blocks):
            live_mask = (block_index * PAGE_ROWS + key_pos)[None, :] <= query_pos[:, None]
            terms = block_terms(query_grid, block_keys[block_index], block_values[block_index], live_mask, score_scale)
            fresh = combine_terms(fresh, terms)
        home = ((row_start + query_pos) // TOK_DEV).astype(jnp.int32)
        match = (home[None, :] == seq_ids[:, None])[:, :, None, None]
        placed = (jnp.where(match, fresh[0][None], -1e+30), jnp.where(match[..., None], fresh[1][None], 0.0), jnp.where(match, fresh[2][None], 0.0))
        run_max, run_num, run_den = combine_terms(running, placed)
        den_safe = jnp.maximum(run_den, 1.0)
        partial_value = (run_num / den_safe[..., None]).astype(jnp.bfloat16)
        partial_wide = lax.optimization_barrier(partial_value).astype(jnp.float32)
        log_scale = run_max + jnp.log(den_safe)
        peak = lax.optimization_barrier(jnp.max(log_scale, axis=0))
        scale_weights = jnp.exp(log_scale - peak[None])
        result = lax.optimization_barrier(jnp.sum(scale_weights[..., None] * partial_wide, axis=0)) / lax.optimization_barrier(jnp.sum(scale_weights, axis=0))[..., None]
        return result.reshape(ADDED_TOKENS, Q_HEADS * HEAD_DIM)
    attention = lax.map(one_request, jnp.arange(REQUESTS, dtype=jnp.int32))
    attention = attention.reshape(TOKENS, Q_HEADS * HEAD_DIM).astype(jnp.bfloat16)
    return jnp.dot(attention, out_weight, preferred_element_type=jnp.float32).astype(jnp.bfloat16)
```

```python
import functools
import math

import jax
import jax.numpy as jnp
from jax import lax
from jax.experimental import pallas as pl
from jax.experimental.pallas import tpu as pltpu
from jax.sharding import PartitionSpec as P

HEAD_DIM = 128
PAGE_ROWS = 128
ADDED_TOKENS = 512
GROUPS = 2
PROMPT_PAGES = 128
STEP_PAGES = 8
TAIL_PAGES = 4
BLOCK = 128
EXTRA = 16
REQUESTS = 2
LIMIT = 1e30
SCORE_SCALE = 1.0 / math.sqrt(HEAD_DIM)
EXP2_SCALE = SCORE_SCALE * math.log2(math.e)
EMPTY = -1e30
LINES = 8
MESH = pl.DeviceIdType.MESH


def in_hbm(array):
    return pltpu.with_memory_space_constraint(array, pltpu.HBM)


def dot_nt(left, right):
    return lax.dot_general(
        left, right, (((1,), (1,)), ((), ())), preferred_element_type=jnp.float32
    )


def attend_kernel(
    per_kv,
    tok_rows,
    packed_ref,
    qt_ref,
    fk_ref,
    fv_ref,
    kc_ref,
    vc_ref,
    o_ref,
    ls_ref,
    lists,
    m_ref,
    acc_ref,
    list_sem,
):
    fetch = pltpu.make_async_copy(packed_ref, lists, list_sem)
    fetch.start()
    requests, kv_count = acc_ref.shape[:2]
    heads = kv_count * per_kv
    blocks = ADDED_TOKENS // BLOCK
    width = per_kv * ADDED_TOKENS
    acc_ref[...] = jnp.zeros_like(acc_ref)
    ls_ref[...] = jnp.zeros_like(ls_ref)

    def cols(index):
        return slice(index * HEAD_DIM, (index + 1) * HEAD_DIM)

    def pieces(kv):
        return [(kv * per_kv + sub, block) for sub in range(per_kv) for block in range(blocks)]

    def queries(request, kv):
        return jnp.concatenate(
            [qt_ref[request * blocks + block, cols(head), :] for head, block in pieces(kv)], axis=1
        )

    def set_marks(request):
        for kv in range(kv_count):
            rows = [
                qt_ref[request * blocks + block, heads * HEAD_DIM :, :].astype(jnp.float32)[
                    head : head + 1
                ]
                for head, block in pieces(kv)
            ]
            m_ref[request, kv, 0:1, :] = jnp.concatenate(rows, axis=1)

    for request in range(requests):
        set_marks(request)

    def values_t(values):
        ones = jnp.ones((EXTRA, values.shape[0]), jnp.bfloat16)
        return jnp.concatenate([values.T, ones], axis=0)

    def add(request, kv, keys, values, bias):
        scores = jnp.dot(keys, queries(request, kv), preferred_element_type=jnp.float32)
        if bias is not None:
            scores = scores + bias
        weights = jnp.exp2((scores - m_ref[request, kv, 0:1, :]) * EXP2_SCALE)
        acc_ref[request, kv] += jnp.dot(
            values_t(values), weights.astype(jnp.bfloat16), preferred_element_type=jnp.float32
        )

    def add_running(request, kv, keys, values, bias):
        scores = jnp.dot(keys, queries(request, kv), preferred_element_type=jnp.float32) + bias
        old = m_ref[request, kv, 0:1, :]
        new = jnp.maximum(old, jnp.max(scores, axis=0, keepdims=True))
        m_ref[request, kv, 0:1, :] = new
        weights = jnp.exp2((scores - new) * EXP2_SCALE)
        acc_ref[request, kv] = acc_ref[request, kv] * jnp.exp2((old - new) * EXP2_SCALE) + jnp.dot(
            values_t(values), weights.astype(jnp.bfloat16), preferred_element_type=jnp.float32
        )

    first = lax.axis_index("seq") * tok_rows
    home = first // ADDED_TOKENS

    def add_fresh(update):
        row = lax.broadcasted_iota(jnp.int32, (tok_rows, width), 0) + (first - home * ADDED_TOKENS)
        col = lax.broadcasted_iota(jnp.int32, (tok_rows, width), 1) % ADDED_TOKENS
        bias = jnp.where(row <= col, 0.0, EMPTY)
        for kv in range(kv_count):
            update(home, kv, fk_ref[:, cols(kv)], fv_ref[:, cols(kv)], bias)

    def add_pages(update, request, start, pages, masked):
        picked = [lists[request, start + page] for page in range(pages)]
        bias = None
        if masked:
            place = lax.broadcasted_iota(jnp.int32, (PAGE_ROWS, 1), 0)
            bias = jnp.concatenate(
                [jnp.where(place < (item & 255), 0.0, EMPTY) for item in picked], axis=0
            )
        slots = [item >> 8 for item in picked]
        for kv in range(kv_count):
            keys = jnp.concatenate([kc_ref[slot, :, cols(kv)] for slot in slots], axis=0)
            values = jnp.concatenate([vc_ref[slot, :, cols(kv)] for slot in slots], axis=0)
            update(request, kv, keys, values, bias)

    add_fresh(add)
    fetch.wait()

    def attend_request(request, carry):
        count = lists[requests + request, 0]
        whole = jnp.maximum(count - 1, 0) // STEP_PAGES

        def step(index, carry):
            add_pages(add, request, index * STEP_PAGES, STEP_PAGES, False)
            return carry

        lax.fori_loop(0, whole, step, 0)
        done = whole * STEP_PAGES
        rest = count - done

        @pl.when((rest > 0) & (rest <= TAIL_PAGES))
        def _():
            add_pages(add, request, done, TAIL_PAGES, True)

        @pl.when(rest > TAIL_PAGES)
        def _():
            add_pages(add, request, done, STEP_PAGES, True)

        sums = jnp.concatenate(
            [acc_ref[request, kv, HEAD_DIM : HEAD_DIM + 1, :] for kv in range(kv_count)], axis=0
        )
        unsafe = jnp.max(jnp.where(sums < LIMIT, 0.0, 1.0))

        @pl.when(unsafe > 0.0)
        def _():
            acc_ref[request] = jnp.zeros_like(acc_ref[request])
            m_ref[request] = jnp.full_like(m_ref[request], EMPTY)

            @pl.when(request == home)
            def _():
                add_fresh(add_running)

            def step(index, carry):
                add_pages(add_running, request, index * TAIL_PAGES, TAIL_PAGES, True)
                return carry

            lax.fori_loop(0, (count + TAIL_PAGES - 1) // TAIL_PAGES, step, 0)

        for kv in range(kv_count):
            top = m_ref[request, kv, 0:1, :]
            den = acc_ref[request, kv, HEAD_DIM : HEAD_DIM + 1, :]
            alive = (den > 0.0) & (top > 0.5 * EMPTY)
            den = jnp.where(alive, den, 1.0)
            scale = jnp.where(alive, top * SCORE_SCALE + jnp.log(den), EMPTY)
            parts = acc_ref[request, kv, :HEAD_DIM, :] * jnp.where(alive, 1.0 / den, 0.0)
            parts = parts.astype(jnp.bfloat16)
            for place, (head, block) in enumerate(pieces(kv)):
                span = slice(place * BLOCK, (place + 1) * BLOCK)
                o_ref[request * blocks + block, cols(head), :] = parts[:, span]
                ls_ref[request * blocks + block, head : head + 1, :] = scale[:, span]
        return carry

    lax.fori_loop(0, requests, attend_request, 0)


def attend(packed, queries_t, fresh_k, fresh_v, key_cache, value_cache, per_kv):
    blocks, q_rows, _ = queries_t.shape
    q_cols = q_rows - EXTRA
    pages, _, kv_cols = key_cache.shape
    tok_rows = fresh_k.shape[0]
    kv_count = kv_cols // HEAD_DIM
    requests = blocks * BLOCK // ADDED_TOKENS
    width = per_kv * ADDED_TOKENS
    vmem = pl.BlockSpec(memory_space=pltpu.VMEM)
    return pl.pallas_call(
        functools.partial(attend_kernel, per_kv, tok_rows),
        out_shape=(
            jax.ShapeDtypeStruct((blocks, q_cols, BLOCK), jnp.bfloat16),
            jax.ShapeDtypeStruct((blocks, LINES, BLOCK), jnp.float32),
        ),
        in_specs=[vmem] * 6,
        out_specs=(vmem, vmem),
        scratch_shapes=[
            pltpu.SMEM(packed.shape, packed.dtype),
            pltpu.VMEM((requests, kv_count, LINES, width), jnp.float32),
            pltpu.VMEM((requests, kv_count, HEAD_DIM + EXTRA, width), jnp.float32),
            pltpu.SemaphoreType.DMA(()),
        ],
        compiler_params=pltpu.CompilerParams(vmem_limit_bytes=32 << 20),
        cost_estimate=pl.CostEstimate(
            flops=4 * pages * PAGE_ROWS * ADDED_TOKENS * q_cols,
            bytes_accessed=4 * pages * PAGE_ROWS * kv_cols,
            transcendentals=pages * PAGE_ROWS * ADDED_TOKENS * (q_cols // HEAD_DIM),
        ),
    )(packed, queries_t, fresh_k, fresh_v, key_cache, value_cache)


def page_lists(lengths_ref, groups_ref, prompt_ref, own_ref, packed_ref, pages_dev, me):
    count = PROMPT_PAGES + own_ref.shape[1]
    position = lax.broadcasted_iota(jnp.int32, (1, count), 1)
    owned, pages, lives = [], [], []
    for request in range(REQUESTS):
        prompt = prompt_ref[0:1, :]
        for group in range(1, GROUPS):
            prompt = jnp.where(groups_ref[request] == group, prompt_ref[group : group + 1, :], prompt)
        slots = jnp.concatenate([prompt, own_ref[request : request + 1, :]], axis=1)
        own_len = lengths_ref[request] - PROMPT_PAGES * PAGE_ROWS
        live = jnp.clip(own_len - (position - PROMPT_PAGES) * PAGE_ROWS, 0, PAGE_ROWS)
        live = jnp.where(position < PROMPT_PAGES, PAGE_ROWS, live)
        page = slots - me * pages_dev
        owned.append((page >= 0) & (page < pages_dev) & (live > 0))
        pages.append(page)
        lives.append(live)
    earlier = lax.broadcasted_iota(jnp.int32, (count, count), 0)
    earlier = earlier < lax.broadcasted_iota(jnp.int32, (count, count), 1)
    earlier = jnp.where(earlier, 1.0, 0.0).astype(jnp.bfloat16)
    place = lax.broadcasted_iota(jnp.int32, (PAGE_ROWS, count), 0).astype(jnp.float32)
    packed_ref[...] = jnp.zeros_like(packed_ref)
    for request in range(REQUESTS):
        mark = jnp.where(owned[request], 1.0, 0.0)
        marks = jnp.broadcast_to(mark, (EXTRA, count)).astype(jnp.bfloat16)
        before = jnp.dot(marks, earlier, preferred_element_type=jnp.float32)[0:1]
        before = jnp.where(owned[request], before, -1.0)
        onehot = jnp.where(before == place, 1.0, 0.0).astype(jnp.bfloat16)

        def pick(line):
            line = jnp.where(owned[request], line, 0).astype(jnp.float32)
            lines = jnp.broadcast_to(line, (EXTRA, count)).astype(jnp.bfloat16)
            return dot_nt(lines, onehot)[0:1]

        packed = pick(pages[request]) * 256.0 + pick(lives[request])
        packed_ref[request : request + 1, :] = packed.astype(jnp.int32)
        total = jnp.sum(mark, axis=1, keepdims=True)
        packed_ref[REQUESTS + request : REQUESTS + request + 1, :] = jnp.broadcast_to(
            total, (1, PAGE_ROWS)
        ).astype(jnp.int32)


def greet(peers):
    barrier = pltpu.get_barrier_semaphore()
    for peer in peers:
        pl.semaphore_signal(barrier, inc=1, device_id=peer, device_id_type=MESH)
    pl.semaphore_wait(barrier, len(peers))


def remote(source, target, send_sem, recv_sem, peer):
    return pltpu.make_async_remote_copy(
        src_ref=source,
        dst_ref=target,
        send_sem=send_sem,
        recv_sem=recv_sem,
        device_id=peer,
        device_id_type=MESH,
    )


def gather_kernel(
    seq_count,
    x_ref,
    gain_ref,
    wq_ref,
    wk_ref,
    wv_ref,
    kc_hbm,
    vc_hbm,
    lengths_ref,
    groups_ref,
    prompt_ref,
    own_ref,
    qt_ref,
    fk_ref,
    fv_ref,
    packed_ref,
    kc_ref,
    vc_ref,
    q_send,
    q_recv,
    qy_send,
    qy_recv,
    wq_buf,
    wk_buf,
    wv_buf,
    x_buf,
    load_sem,
):
    loads = [
        pltpu.make_async_copy(source, target, load_sem.at[index])
        for index, (source, target) in enumerate(
            (
                (x_ref, x_buf),
                (wk_ref, wk_buf),
                (wq_ref, wq_buf),
                (wv_ref, wv_buf),
                (kc_hbm, kc_ref),
                (vc_hbm, vc_ref),
            )
        )
    ]
    for load in loads:
        load.start()
    me = lax.axis_index("seq")
    tensor = lax.axis_index("tensor")
    outer = seq_count // 2
    place, side = me // 2, me % 2
    twin = (place * 2 + 1 - side, tensor)

    def line_peer(distance):
        return (place + distance) % outer * 2 + side

    greet([twin] + [(line_peer(distance), tensor) for distance in range(1, outer)])

    loads[0].wait()
    floats = x_buf[...].astype(jnp.float32)
    mean = jnp.mean(floats * floats, axis=-1, keepdims=True)
    normed = (floats * lax.rsqrt(mean + 1e-05) * gain_ref[...]).astype(jnp.bfloat16)

    def project(weight):
        return jnp.dot(normed, weight[...], preferred_element_type=jnp.float32)

    loads[1].wait()
    keys = project(wk_buf)
    loads[2].wait()
    queries = project(wq_buf)
    fk_ref[...] = keys.astype(jnp.bfloat16)
    keys_t = keys.T.astype(jnp.bfloat16)
    queries_t = queries.T.astype(jnp.bfloat16)
    heads = queries_t.shape[0] // HEAD_DIM
    per_kv = queries_t.shape[0] // keys_t.shape[0]
    qt_ref[me, : heads * HEAD_DIM, :] = queries_t
    marks = []
    for head in range(heads):
        kv = head // per_kv
        left = queries_t[head * HEAD_DIM : (head + 1) * HEAD_DIM].astype(jnp.float32)
        right = keys_t[kv * HEAD_DIM : (kv + 1) * HEAD_DIM].astype(jnp.float32)
        marks.append(jnp.sum(left * right, axis=0, keepdims=True))
    marks.append(jnp.zeros((EXTRA - heads, marks[0].shape[1]), jnp.float32))
    qt_ref[me, heads * HEAD_DIM :, :] = jnp.concatenate(marks, axis=0).astype(jnp.bfloat16)

    started = []
    own = qt_ref.at[me]
    copy = remote(own, own, qy_send.at[0], qy_recv.at[0], twin)
    copy.start()
    started.append(copy)
    for distance in range(1, outer):
        peer = (line_peer(distance), tensor)
        copy = remote(own, own, q_send.at[distance], q_recv.at[distance], peer)
        copy.start()
        started.append(copy)

    loads[3].wait()
    fv_ref[...] = project(wv_buf).astype(jnp.bfloat16)
    page_lists(lengths_ref, groups_ref, prompt_ref, own_ref, packed_ref, kc_ref.shape[0], me)

    for distance in range(1, outer):
        block = qt_ref.at[line_peer(outer - distance)]
        remote(block, block, q_send.at[distance], q_recv.at[distance], twin).wait_recv()
        copy = remote(block, block, qy_send.at[distance], qy_recv.at[distance], twin)
        copy.start()
        started.append(copy)
    for load in loads[4:]:
        load.wait()
    for distance in range(outer):
        block = qt_ref.at[(place + outer - distance) % outer * 2 + 1 - side]
        remote(block, block, qy_send.at[distance], qy_recv.at[distance], twin).wait_recv()
    for copy in started:
        copy.wait_send()


def gather(
    hidden_in,
    norm_gain,
    query_weight,
    key_weight,
    value_weight,
    key_cache,
    value_cache,
    cached_lengths,
    group_ids,
    prompt_pages,
    own_pages,
    seq_count,
):
    tok_rows = hidden_in.shape[0]
    q_cols, kv_cols = query_weight.shape[1], key_weight.shape[1]
    slots = pltpu.SemaphoreType.DMA((seq_count // 2,))
    vmem = pl.BlockSpec(memory_space=pltpu.VMEM)
    smem = pl.BlockSpec(memory_space=pltpu.SMEM)
    hbm = pl.BlockSpec(memory_space=pltpu.HBM)
    fresh = jax.ShapeDtypeStruct((tok_rows, kv_cols), jnp.bfloat16)
    return pl.pallas_call(
        functools.partial(gather_kernel, seq_count),
        out_shape=(
            jax.ShapeDtypeStruct((seq_count, q_cols + EXTRA, tok_rows), jnp.bfloat16),
            fresh,
            fresh,
            jax.ShapeDtypeStruct((LINES, PAGE_ROWS), jnp.int32),
            jax.ShapeDtypeStruct(key_cache.shape, key_cache.dtype),
            jax.ShapeDtypeStruct(value_cache.shape, value_cache.dtype),
        ),
        in_specs=[hbm, vmem, hbm, hbm, hbm, hbm, hbm, smem, smem, vmem, vmem],
        out_specs=(vmem,) * 6,
        scratch_shapes=[slots] * 4
        + [
            pltpu.VMEM(weight.shape, weight.dtype)
            for weight in (query_weight, key_weight, value_weight, hidden_in)
        ]
        + [pltpu.SemaphoreType.DMA((6,))],
        compiler_params=pltpu.CompilerParams(
            collective_id=0, has_side_effects=True, vmem_limit_bytes=40 << 20
        ),
    )(
        in_hbm(hidden_in),
        norm_gain.reshape(1, -1),
        in_hbm(query_weight),
        in_hbm(key_weight),
        in_hbm(value_weight),
        in_hbm(key_cache),
        in_hbm(value_cache),
        cached_lengths,
        group_ids,
        prompt_pages,
        own_pages,
    )


def finish_kernel(
    seq_count,
    tensor_count,
    part_ref,
    ls_ref,
    w_ref,
    out_ref,
    mix_ref,
    mix_got,
    mls_ref,
    side_got,
    sls_ref,
    gls_ref,
    near_ref,
    near_got,
    far_ref,
    far_got,
    side_send,
    side_recv,
    sls_send,
    sls_recv,
    mix_send,
    mix_recv,
    mls_send,
    mls_recv,
    near_send,
    near_recv,
    far_send,
    far_recv,
):
    tok_rows, out_cols = out_ref.shape
    heads = part_ref.shape[1] // HEAD_DIM
    me = lax.axis_index("seq")
    tensor = lax.axis_index("tensor")
    pair, core = tensor // 2, tensor % 2
    pairs = tensor_count // 2
    twin = (me, pair * 2 + 1 - core)
    outer = seq_count // 2
    place, side = me // 2, me % 2
    beside = (place * 2 + 1 - side, tensor)
    order = sorted(range(1, outer), key=lambda distance: -min(distance, outer - distance))

    def far_pair(distance):
        return (pair + distance) % pairs

    def line(distance, which):
        return (place + distance) % outer * 2 + which

    greet(
        [beside]
        + [(line(distance, side), tensor) for distance in range(1, outer)]
        + [twin]
        + [(me, far_pair(distance) * 2 + core) for distance in range(1, pairs)]
    )
    started = []
    scales, sides, mixes, mix_scales = {}, {}, {}, {}
    for distance in order + [0]:
        scales[distance] = remote(
            ls_ref.at[line(distance, 1 - side)],
            sls_ref.at[distance],
            sls_send.at[distance],
            sls_recv.at[distance],
            beside,
        )
        scales[distance].start()
    for distance in order + [0]:
        sides[distance] = remote(
            part_ref.at[line(distance, 1 - side)],
            side_got.at[distance],
            side_send.at[distance],
            side_recv.at[distance],
            beside,
        )
        sides[distance].start()
    for distance in order + [0]:
        scales[distance].wait_recv()

    def weighted(block, share):
        return [
            block[head * HEAD_DIM : (head + 1) * HEAD_DIM].astype(jnp.float32)
            * share[head : head + 1]
            for head in range(heads)
        ]

    def plus(left, right):
        return [one + other for one, other in zip(left, right)]

    own_lines = jnp.stack([ls_ref[line(distance, side)] for distance in range(outer)])
    side_lines = sls_ref[...]
    top = jnp.maximum(own_lines, side_lines)
    own_scale, side_scale = jnp.exp(own_lines - top), jnp.exp(side_lines - top)
    both = own_scale + side_scale
    mls_ref[...] = top + jnp.log(both)
    for distance in order:
        mix_scales[distance] = remote(
            mls_ref.at[distance],
            gls_ref.at[distance],
            mls_send.at[distance],
            mls_recv.at[distance],
            (line(distance, side), tensor),
        )
        mix_scales[distance].start()
    own_shares, side_shares = own_scale / both, side_scale / both

    def mixed(distance):
        return plus(
            weighted(part_ref[line(distance, side)], own_shares[distance]),
            weighted(side_got[distance], side_shares[distance]),
        )

    for distance in order:
        sides[distance].wait_recv()
        mix_ref[distance] = jnp.concatenate(mixed(distance), axis=0).astype(jnp.bfloat16)
        mixes[distance] = remote(
            mix_ref.at[distance],
            mix_got.at[distance],
            mix_send.at[distance],
            mix_recv.at[distance],
            (line(distance, side), tensor),
        )
        mixes[distance].start()
    gls_ref[0] = mls_ref[0]
    for distance in order:
        mix_scales[distance].wait_recv()
    lines = gls_ref[...]
    lines = jnp.exp(lines - jnp.max(lines, axis=0, keepdims=True))
    shares = lines / jnp.sum(lines, axis=0, keepdims=True)
    sides[0].wait_recv()
    total = [
        block * shares[0][head : head + 1] for head, block in enumerate(mixed(0))
    ]
    for distance in order:
        mixes[distance].wait_recv()
        total = plus(total, weighted(mix_got[distance], shares[distance]))
    for group in (scales, sides, mixes, mix_scales):
        started.extend(group.values())
    attention = jnp.concatenate(total, axis=0).astype(jnp.bfloat16)

    def terms_for(owner):
        start = pl.multiple_of(owner * out_cols, out_cols)
        return lax.dot_general(
            attention,
            w_ref[:, pl.ds(start, out_cols)],
            (((0,), (0,)), ((), ())),
            preferred_element_type=jnp.float32,
        )

    nears = []
    for distance in list(range(1, pairs)) + [0]:
        near_ref[distance] = terms_for(far_pair(distance) * 2 + 1 - core)
        copy = remote(
            near_ref.at[distance],
            near_got.at[distance],
            near_send.at[distance],
            near_recv.at[distance],
            twin,
        )
        copy.start()
        started.append(copy)
        nears.append((distance, copy))
    fars = []
    for distance, copy in nears[:-1]:
        owner = far_pair(distance) * 2 + core
        terms = terms_for(owner)
        copy.wait_recv()
        far_ref[distance] = (terms + near_got[distance]).astype(far_ref.dtype)
        copy = remote(
            far_ref.at[distance],
            far_got.at[distance],
            far_send.at[distance],
            far_recv.at[distance],
            (me, owner),
        )
        copy.start()
        started.append(copy)
        fars.append(copy)
    result = terms_for(tensor)
    nears[-1][1].wait_recv()
    result = result + near_got[0]
    for distance in range(1, pairs):
        fars[distance - 1].wait_recv()
        result = result + far_got[distance].astype(jnp.float32)
    out_ref[...] = result.astype(jnp.bfloat16)
    for copy in started:
        copy.wait_send()


def finish(partial_value, log_scale, out_weight, seq_count, tensor_count):
    tok_rows = partial_value.shape[2]
    out_cols = out_weight.shape[1] // tensor_count
    pairs = tensor_count // 2
    vmem = pl.BlockSpec(memory_space=pltpu.VMEM)
    block = pltpu.VMEM((pairs, tok_rows, out_cols), jnp.float32)
    far_block = pltpu.VMEM((pairs, tok_rows, out_cols), jnp.bfloat16)
    outer = seq_count // 2
    parts = pltpu.VMEM((outer,) + partial_value.shape[1:], jnp.bfloat16)
    scales = pltpu.VMEM((outer, LINES, tok_rows), jnp.float32)
    line_sems = pltpu.SemaphoreType.DMA((outer,))
    pair_sems = pltpu.SemaphoreType.DMA((pairs,))
    return pl.pallas_call(
        functools.partial(finish_kernel, seq_count, tensor_count),
        out_shape=jax.ShapeDtypeStruct((tok_rows, out_cols), jnp.bfloat16),
        in_specs=[vmem] * 3,
        out_specs=vmem,
        scratch_shapes=[
            parts,
            parts,
            scales,
            parts,
            scales,
            scales,
            block,
            block,
            far_block,
            far_block,
        ]
        + [line_sems] * 8
        + [pair_sems] * 4,
        compiler_params=pltpu.CompilerParams(
            collective_id=1, has_side_effects=True, vmem_limit_bytes=24 << 20
        ),
    )(partial_value, log_scale, out_weight)


def regroup(array, rows):
    count, lines, width = array.shape
    if width == rows:
        return array
    array = jnp.transpose(array, (1, 0, 2)).reshape(lines, count * width // rows, rows)
    return jnp.transpose(array, (1, 0, 2))


def body(
    hidden_in,
    norm_gain,
    query_weight,
    key_weight,
    value_weight,
    out_weight,
    key_cache,
    value_cache,
    cached_lengths,
    group_ids,
    prompt_pages,
    own_pages,
):
    tok_rows = hidden_in.shape[0]
    seq_count = lax.axis_size("seq")
    queries_t, fresh_k, fresh_v, packed, keys, values = gather(
        hidden_in,
        norm_gain,
        query_weight,
        key_weight,
        value_weight,
        key_cache,
        value_cache,
        cached_lengths,
        group_ids,
        prompt_pages,
        own_pages,
        seq_count,
    )
    partial_value, log_scale = attend(
        packed,
        regroup(queries_t, BLOCK),
        fresh_k,
        fresh_v,
        keys,
        values,
        query_weight.shape[1] // key_weight.shape[1],
    )
    return finish(
        regroup(partial_value, tok_rows),
        regroup(log_scale, tok_rows),
        out_weight,
        seq_count,
        lax.axis_size("tensor"),
    )


def solution(mesh):
    in_specs = (
        P("seq", None),
        P(),
        P(None, "tensor"),
        P(None, "tensor"),
        P(None, "tensor"),
        P("tensor", None),
        P("seq", None, "tensor"),
        P("seq", None, "tensor"),
        P(),
        P(),
        P(),
        P(),
    )
    out_specs = P("seq", "tensor")
    return jax.shard_map(body, mesh=mesh, in_specs=in_specs, out_specs=out_specs, check_vma=False)
```

```python
import functools
import math

import jax
import jax.numpy as jnp
from jax import lax
from jax.experimental import pallas as pl
from jax.experimental.pallas import tpu as pltpu
from jax.sharding import PartitionSpec as P

HEAD_DIM = 128
PAGE_ROWS = 128
ADDED_TOKENS = 512
GROUPS = 2
PROMPT_PAGES = 128
STEP_PAGES = 8
TAIL_PAGES = 4
BLOCK = 128
EXTRA = 16
REQUESTS = 2
LIMIT = 1e30
EARLY_STEPS = 2
SAFE_POWER = 100.0
SCORE_SCALE = 1.0 / math.sqrt(HEAD_DIM)
EXP2_SCALE = SCORE_SCALE * math.log2(math.e)
EMPTY = -1e30
SHIFT = 60.0 / EXP2_SCALE
BLOCKS = ADDED_TOKENS // BLOCK
LINES = 8
MESH = pl.DeviceIdType.MESH


def in_hbm(array):
    return pltpu.with_memory_space_constraint(array, pltpu.HBM)


def dot_nt(left, right):
    return lax.dot_general(
        left, right, (((1,), (1,)), ((), ())), preferred_element_type=jnp.float32
    )


def cols(index):
    return slice(index * HEAD_DIM, (index + 1) * HEAD_DIM)


def joined_queries(qt_ref, request, kv, per_kv):
    return jnp.concatenate(
        [
            qt_ref[request * BLOCKS + block, kv, cols(sub), :]
            for sub in range(per_kv)
            for block in range(BLOCKS)
        ],
        axis=1,
    )


def joined_marks(qt_ref, request, kv, per_kv):
    rows = [
        qt_ref[request * BLOCKS + block, kv, per_kv * HEAD_DIM :, :].astype(jnp.float32)[
            sub : sub + 1
        ]
        for sub in range(per_kv)
        for block in range(BLOCKS)
    ]
    return jnp.concatenate(rows, axis=1) + SHIFT


def values_t(values):
    ones = jnp.ones((EXTRA, values.shape[0]), jnp.bfloat16)
    return jnp.concatenate([values.T, ones], axis=0)


def page_group(lists, cache_ref, request, start, pages, kv):
    last = cache_ref.shape[0] - 1
    slots = [jnp.clip(lists[request, start + page] >> 8, 0, last) for page in range(pages)]
    return jnp.concatenate([cache_ref[slot, :, cols(kv)] for slot in slots], axis=0)


def page_bias(lists, request, start, pages):
    place = lax.broadcasted_iota(jnp.int32, (PAGE_ROWS, 1), 0)
    return jnp.concatenate(
        [
            jnp.where(place < (lists[request, start + page] & 255), 0.0, EMPTY)
            for page in range(pages)
        ],
        axis=0,
    )


def terms(queries, mark, keys, values, bias):
    scores = jnp.dot(keys, queries, preferred_element_type=jnp.float32)
    if bias is not None:
        scores = scores + bias
    weights = jnp.exp2((scores - mark) * EXP2_SCALE).astype(jnp.bfloat16)
    return jnp.dot(values_t(values), weights, preferred_element_type=jnp.float32)


def early_terms(lists, qt_ref, kc_ref, vc_ref, mark, request, step, kv, per_kv):
    start = step * STEP_PAGES
    return terms(
        joined_queries(qt_ref, request, kv, per_kv),
        mark,
        page_group(lists, kc_ref, request, start, STEP_PAGES, kv),
        page_group(lists, vc_ref, request, start, STEP_PAGES, kv),
        page_bias(lists, request, start, STEP_PAGES),
    )


def settle(sums, top, request, part_ref, ls_ref, per_kv):
    den = sums[HEAD_DIM : HEAD_DIM + 1]
    alive = (den > 0.0) & (top > 0.5 * EMPTY)
    den = jnp.where(alive, den, 1.0)
    scale = jnp.where(alive, top * SCORE_SCALE + jnp.log(den), EMPTY)
    parts = (sums[:HEAD_DIM] * jnp.where(alive, 1.0 / den, 0.0)).astype(jnp.bfloat16)
    for sub in range(per_kv):
        for block in range(BLOCKS):
            place = sub * BLOCKS + block
            span = slice(place * BLOCK, (place + 1) * BLOCK)
            part_ref[request * BLOCKS + block, cols(sub), :] = parts[:, span]
            ls_ref[request * BLOCKS + block, sub : sub + 1, :] = scale[:, span]


def attend_kernel(per_kv, tok_rows, late, early, *refs):
    refs = list(refs)
    packed_ref, qt_ref, fk_ref, fv_ref, kc_ref, vc_ref = refs[:6]
    del refs[:6]
    if late:
        start_ref, peak_ref = refs[:2]
        del refs[:2]
    kv_count = kc_ref.shape[2] // HEAD_DIM
    done_kv = kv_count - 1 if late else kv_count
    part_refs, ls_refs = refs[:done_kv], refs[done_kv : 2 * done_kv]
    del refs[: 2 * done_kv]
    if late:
        left_ref, left_m_ref, left_list_ref = refs[:3]
        del refs[:3]
    lists, m_ref, acc_ref, list_sem = refs
    fetch = pltpu.make_async_copy(packed_ref, lists, list_sem)
    fetch.start()
    requests = acc_ref.shape[0]
    width = per_kv * ADDED_TOKENS
    for ls_ref in ls_refs:
        ls_ref[...] = jnp.zeros_like(ls_ref)
    for kv in range(kv_count):
        for request in range(requests):
            if late and kv == 0:
                acc_ref[request, kv] = start_ref[request]
            else:
                acc_ref[request, kv] = jnp.zeros_like(acc_ref[request, kv])
            m_ref[request, kv, 0:1, :] = joined_marks(qt_ref, request, kv, per_kv)
    if late:
        left_list_ref[...] = packed_ref[...]

    def add(request, kv, keys, values, bias):
        queries = joined_queries(qt_ref, request, kv, per_kv)
        acc_ref[request, kv] += terms(queries, m_ref[request, kv, 0:1, :], keys, values, bias)

    def add_running(request, kv, keys, values, bias):
        queries = joined_queries(qt_ref, request, kv, per_kv)
        scores = jnp.dot(keys, queries, preferred_element_type=jnp.float32) + bias
        old = m_ref[request, kv, 0:1, :]
        new = jnp.maximum(old, jnp.max(scores, axis=0, keepdims=True))
        m_ref[request, kv, 0:1, :] = new
        weights = jnp.exp2((scores - new) * EXP2_SCALE)
        acc_ref[request, kv] = acc_ref[request, kv] * jnp.exp2((old - new) * EXP2_SCALE) + jnp.dot(
            values_t(values), weights.astype(jnp.bfloat16), preferred_element_type=jnp.float32
        )

    first = lax.axis_index("seq") * tok_rows
    home = first // ADDED_TOKENS

    def add_fresh(update):
        row = lax.broadcasted_iota(jnp.int32, (tok_rows, width), 0) + (first - home * ADDED_TOKENS)
        col = lax.broadcasted_iota(jnp.int32, (tok_rows, width), 1) % ADDED_TOKENS
        bias = jnp.where(row <= col, 0.0, EMPTY)
        for kv in range(kv_count):
            update(home, kv, fk_ref[:, cols(kv)], fv_ref[:, cols(kv)], bias)

    def add_pages(update, request, start, pages, masked):
        bias = page_bias(lists, request, start, pages) if masked else None
        for kv in range(kv_count):
            keys = page_group(lists, kc_ref, request, start, pages, kv)
            values = page_group(lists, vc_ref, request, start, pages, kv)
            update(request, kv, keys, values, bias)

    add_fresh(add)
    fetch.wait()

    def attend_request(request, carry):
        total = lists[requests + request, 0]
        count = jnp.maximum(total - early, 0)
        whole = jnp.maximum(count - 1, 0) // STEP_PAGES

        def step(index, carry):
            add_pages(add, request, early + index * STEP_PAGES, STEP_PAGES, False)
            return carry

        lax.fori_loop(0, whole, step, 0)
        done = whole * STEP_PAGES
        rest = count - done

        @pl.when((rest > 0) & (rest <= TAIL_PAGES))
        def _():
            add_pages(add, request, early + done, TAIL_PAGES, True)

        @pl.when(rest > TAIL_PAGES)
        def _():
            add_pages(add, request, early + done, STEP_PAGES, True)

        safe = [
            acc_ref[request, kv, HEAD_DIM : HEAD_DIM + 1, :] < LIMIT for kv in range(kv_count)
        ]
        if late:
            floats = joined_queries(qt_ref, request, kv_count - 1, per_kv).astype(jnp.float32)
            norms = jnp.sum(floats * floats, axis=0, keepdims=True) * jnp.max(peak_ref[...])
            power = (jnp.sqrt(norms) - m_ref[request, kv_count - 1, 0:1, :]) * EXP2_SCALE
            safe.append(power < SAFE_POWER)
        unsafe = jnp.max(
            jnp.concatenate([jnp.where(flags, 0.0, 1.0) for flags in safe], axis=0)
        )

        @pl.when(unsafe > 0.0)
        def _():
            acc_ref[request] = jnp.zeros_like(acc_ref[request])
            m_ref[request] = jnp.full_like(m_ref[request], EMPTY)

            @pl.when(request == home)
            def _():
                add_fresh(add_running)

            def step(index, carry):
                add_pages(add_running, request, index * TAIL_PAGES, TAIL_PAGES, True)
                return carry

            lax.fori_loop(0, (total + TAIL_PAGES - 1) // TAIL_PAGES, step, 0)
            if late:
                row = lax.broadcasted_iota(jnp.int32, left_list_ref.shape, 0)
                left_list_ref[...] = jnp.where(row == request, 0, left_list_ref[...])

        for kv in range(done_kv):
            settle(
                acc_ref[request, kv],
                m_ref[request, kv, 0:1, :],
                request,
                part_refs[kv],
                ls_refs[kv],
                per_kv,
            )
        if late:
            left_ref[request] = acc_ref[request, done_kv]
            left_m_ref[request] = m_ref[request, done_kv]
        return carry

    lax.fori_loop(0, requests, attend_request, 0)


def attend(packed, queries_t, fresh_k, fresh_v, key_cache, value_cache, early_sums, peak, early):
    blocks, kv_count, q_rows, _ = queries_t.shape
    late = early > 0
    done_kv = kv_count - 1 if late else kv_count
    q_rows -= EXTRA
    per_kv = q_rows // HEAD_DIM
    pages, _, kv_cols = key_cache.shape
    tok_rows = fresh_k.shape[0]
    requests = blocks // BLOCKS
    width = per_kv * ADDED_TOKENS
    vmem = pl.BlockSpec(memory_space=pltpu.VMEM)
    out_shape = [jax.ShapeDtypeStruct((blocks, q_rows, BLOCK), jnp.bfloat16)] * done_kv
    out_shape += [jax.ShapeDtypeStruct((blocks, LINES, BLOCK), jnp.float32)] * done_kv
    operands = [packed, queries_t, fresh_k, fresh_v, key_cache, value_cache]
    if late:
        out_shape += [
            jax.ShapeDtypeStruct((requests, HEAD_DIM + EXTRA, width), jnp.float32),
            jax.ShapeDtypeStruct((requests, LINES, width), jnp.float32),
            jax.ShapeDtypeStruct(packed.shape, packed.dtype),
        ]
        operands += [early_sums, peak]
    return pl.pallas_call(
        functools.partial(attend_kernel, per_kv, tok_rows, late, early),
        out_shape=tuple(out_shape),
        in_specs=[vmem] * len(operands),
        out_specs=(vmem,) * len(out_shape),
        scratch_shapes=[
            pltpu.SMEM(packed.shape, packed.dtype),
            pltpu.VMEM((requests, kv_count, LINES, width), jnp.float32),
            pltpu.VMEM((requests, kv_count, HEAD_DIM + EXTRA, width), jnp.float32),
            pltpu.SemaphoreType.DMA(()),
        ],
        compiler_params=pltpu.CompilerParams(vmem_limit_bytes=28 << 20),
        cost_estimate=pl.CostEstimate(
            flops=4 * pages * PAGE_ROWS * ADDED_TOKENS * q_rows * kv_count,
            bytes_accessed=4 * pages * PAGE_ROWS * kv_cols,
            transcendentals=pages * PAGE_ROWS * ADDED_TOKENS * per_kv * kv_count,
        ),
    )(*operands)


def page_lists(lengths_ref, groups_ref, prompt_ref, own_ref, packed_ref, pages_dev, me):
    count = PROMPT_PAGES + own_ref.shape[1]
    position = lax.broadcasted_iota(jnp.int32, (1, count), 1)
    owned, pages, lives = [], [], []
    for request in range(REQUESTS):
        prompt = prompt_ref[0:1, :]
        for group in range(1, GROUPS):
            prompt = jnp.where(groups_ref[request] == group, prompt_ref[group : group + 1, :], prompt)
        slots = jnp.concatenate([prompt, own_ref[request : request + 1, :]], axis=1)
        own_len = lengths_ref[request] - PROMPT_PAGES * PAGE_ROWS
        live = jnp.clip(own_len - (position - PROMPT_PAGES) * PAGE_ROWS, 0, PAGE_ROWS)
        live = jnp.where(position < PROMPT_PAGES, PAGE_ROWS, live)
        page = slots - me * pages_dev
        owned.append((page >= 0) & (page < pages_dev) & (live > 0))
        pages.append(page)
        lives.append(live)
    earlier = lax.broadcasted_iota(jnp.int32, (count, count), 0)
    earlier = earlier < lax.broadcasted_iota(jnp.int32, (count, count), 1)
    earlier = jnp.where(earlier, 1.0, 0.0).astype(jnp.bfloat16)
    place = lax.broadcasted_iota(jnp.int32, (PAGE_ROWS, count), 0).astype(jnp.float32)
    packed_ref[...] = jnp.zeros_like(packed_ref)
    for request in range(REQUESTS):
        mark = jnp.where(owned[request], 1.0, 0.0)
        marks = jnp.broadcast_to(mark, (EXTRA, count)).astype(jnp.bfloat16)
        before = jnp.dot(marks, earlier, preferred_element_type=jnp.float32)[0:1]
        before = jnp.where(owned[request], before, -1.0)
        onehot = jnp.where(before == place, 1.0, 0.0).astype(jnp.bfloat16)

        def pick(line):
            line = jnp.where(owned[request], line, 0).astype(jnp.float32)
            lines = jnp.broadcast_to(line, (EXTRA, count)).astype(jnp.bfloat16)
            return dot_nt(lines, onehot)[0:1]

        packed = pick(pages[request]) * 256.0 + pick(lives[request])
        packed_ref[request : request + 1, :] = packed.astype(jnp.int32)
        total = jnp.sum(mark, axis=1, keepdims=True)
        packed_ref[REQUESTS + request : REQUESTS + request + 1, :] = jnp.broadcast_to(
            total, (1, PAGE_ROWS)
        ).astype(jnp.int32)


def greet(peers):
    barrier = pltpu.get_barrier_semaphore()
    for peer in peers:
        pl.semaphore_signal(barrier, inc=1, device_id=peer, device_id_type=MESH)


def greeted(count):
    pl.semaphore_wait(pltpu.get_barrier_semaphore(), count)


def remote(source, target, send_sem, recv_sem, peer):
    return pltpu.make_async_remote_copy(
        src_ref=source,
        dst_ref=target,
        send_sem=send_sem,
        recv_sem=recv_sem,
        device_id=peer,
        device_id_type=MESH,
    )


def gather_kernel(seq_count, early, *refs):
    refs = list(refs)
    x_ref, gain_ref, wq_ref, wk_ref, wv_ref, kc_hbm, vc_hbm = refs[:7]
    lengths_ref, groups_ref, prompt_ref, own_ref = refs[7:11]
    qt_ref, fk_ref, fv_ref, packed_ref, kc_ref, vc_ref = refs[11:17]
    del refs[:17]
    if early:
        sums_ref, peak_ref = refs[:2]
        del refs[:2]
    q_send, q_recv, qy_send, qy_recv, wq_buf, wk_buf, wv_buf, x_buf, load_sem, lists = refs
    loads = [
        pltpu.make_async_copy(source, target, load_sem.at[index])
        for index, (source, target) in enumerate(
            (
                (x_ref, x_buf),
                (wk_ref, wk_buf),
                (wq_ref, wq_buf),
                (wv_ref, wv_buf),
                (kc_hbm, kc_ref),
                (vc_hbm, vc_ref),
            )
        )
    ]
    for load in loads[:4]:
        load.start()
    me = lax.axis_index("seq")
    tensor = lax.axis_index("tensor")
    outer = seq_count // 2
    place, side = me // 2, me % 2
    twin = (place * 2 + 1 - side, tensor)
    kv_count = qt_ref.shape[1]
    per_kv = (qt_ref.shape[2] - EXTRA) // HEAD_DIM
    order = sorted(range(1, outer), key=lambda distance: -min(distance, outer - distance))

    def line_peer(distance):
        return (place + distance) % outer * 2 + side

    greet([twin] + [(line_peer(distance), tensor) for distance in range(1, outer)])

    loads[0].wait()
    floats = x_buf[...].astype(jnp.float32)
    mean = jnp.mean(floats * floats, axis=-1, keepdims=True)
    normed = (floats * lax.rsqrt(mean + 1e-05) * gain_ref[...]).astype(jnp.bfloat16)

    def project(weight):
        return jnp.dot(normed, weight, preferred_element_type=jnp.float32)

    loads[1].wait()
    keys = project(wk_buf[...])
    fk_ref[...] = keys.astype(jnp.bfloat16)
    keys_t = keys.T.astype(jnp.bfloat16)
    loads[2].wait()
    started = []

    def make(kv):
        span = per_kv * HEAD_DIM
        queries_t = project(wq_buf[:, kv * span : (kv + 1) * span]).T.astype(jnp.bfloat16)
        qt_ref[me, kv, :span, :] = queries_t
        right = keys_t[cols(kv)].astype(jnp.float32)
        marks = [
            jnp.sum(queries_t[cols(sub)].astype(jnp.float32) * right, axis=0, keepdims=True)
            for sub in range(per_kv)
        ]
        marks.append(jnp.zeros((EXTRA - per_kv, marks[0].shape[1]), jnp.float32))
        qt_ref[me, kv, span:, :] = jnp.concatenate(marks, axis=0).astype(jnp.bfloat16)

    def launch(kv):
        own = qt_ref.at[me, kv]
        copy = remote(own, own, qy_send.at[kv, 0], qy_recv.at[kv, 0], twin)
        copy.start()
        started.append(copy)
        for distance in order:
            peer = (line_peer(distance), tensor)
            copy = remote(own, own, q_send.at[kv, distance], q_recv.at[kv, distance], peer)
            copy.start()
            started.append(copy)

    def relay(kv, distance):
        block = qt_ref.at[line_peer(outer - distance), kv]
        remote(block, block, q_send.at[kv, distance], q_recv.at[kv, distance], twin).wait_recv()
        copy = remote(block, block, qy_send.at[kv, distance], qy_recv.at[kv, distance], twin)
        copy.start()
        started.append(copy)

    def arrive(kv):
        for distance in [0] + order:
            block = qt_ref.at[(place + outer - distance) % outer * 2 + 1 - side, kv]
            remote(block, block, qy_send.at[kv, distance], qy_recv.at[kv, distance], twin).wait_recv()

    make(0)
    greeted(outer)
    launch(0)
    for load in loads[4:]:
        load.start()
    for kv in range(1, kv_count):
        make(kv)
    loads[3].wait()
    fv_ref[...] = project(wv_buf[...]).astype(jnp.bfloat16)
    page_lists(lengths_ref, groups_ref, prompt_ref, own_ref, packed_ref, kc_ref.shape[0], me)
    for distance in order[: len(order) // 2 + 1]:
        relay(0, distance)
    for kv in range(1, kv_count):
        launch(kv)
    for distance in order[len(order) // 2 + 1 :]:
        relay(0, distance)
    fetch = pltpu.make_async_copy(packed_ref, lists, load_sem.at[6])
    fetch.start()
    for load in loads[4:]:
        load.wait()
    fetch.wait()
    waiting = [(kv, distance) for kv in range(1, kv_count) for distance in order]
    if early:
        peak = jnp.zeros((PAGE_ROWS, 1), jnp.float32)
        for page in range(kc_ref.shape[0]):
            floats = kc_ref[page, :, cols(kv_count - 1)].astype(jnp.float32)
            peak = jnp.maximum(peak, jnp.sum(floats * floats, axis=1, keepdims=True))
        peak_ref[...] = jnp.broadcast_to(peak, peak_ref.shape)
        arrive(0)
        marks = [joined_marks(qt_ref, request, 0, per_kv) for request in range(REQUESTS)]
        for step in range(early // STEP_PAGES):
            for request in range(REQUESTS):
                fresh = early_terms(
                    lists, qt_ref, kc_ref, vc_ref, marks[request], request, step, 0, per_kv
                )
                if step == 0:
                    sums_ref[request] = fresh
                else:
                    sums_ref[request] += fresh
                if waiting:
                    relay(*waiting.pop(0))
    else:
        arrive(0)
    for kv, distance in waiting:
        relay(kv, distance)
    for kv in range(1, kv_count):
        arrive(kv)
    for copy in started:
        copy.wait_send()


def gather(
    hidden_in,
    norm_gain,
    query_weight,
    key_weight,
    value_weight,
    key_cache,
    value_cache,
    cached_lengths,
    group_ids,
    prompt_pages,
    own_pages,
    seq_count,
    early,
):
    tok_rows = hidden_in.shape[0]
    q_cols, kv_cols = query_weight.shape[1], key_weight.shape[1]
    kv_count = kv_cols // HEAD_DIM
    per_kv = q_cols // kv_cols
    slots = pltpu.SemaphoreType.DMA((kv_count, seq_count // 2))
    vmem = pl.BlockSpec(memory_space=pltpu.VMEM)
    smem = pl.BlockSpec(memory_space=pltpu.SMEM)
    hbm = pl.BlockSpec(memory_space=pltpu.HBM)
    fresh = jax.ShapeDtypeStruct((tok_rows, kv_cols), jnp.bfloat16)
    rows = per_kv * HEAD_DIM + EXTRA
    out_shape = [
        jax.ShapeDtypeStruct((seq_count, kv_count, rows, tok_rows), jnp.bfloat16),
        fresh,
        fresh,
        jax.ShapeDtypeStruct((LINES, PAGE_ROWS), jnp.int32),
        jax.ShapeDtypeStruct(key_cache.shape, key_cache.dtype),
        jax.ShapeDtypeStruct(value_cache.shape, value_cache.dtype),
    ]
    if early:
        sums = (REQUESTS, HEAD_DIM + EXTRA, per_kv * ADDED_TOKENS)
        out_shape += [
            jax.ShapeDtypeStruct(sums, jnp.float32),
            jax.ShapeDtypeStruct((PAGE_ROWS, HEAD_DIM), jnp.float32),
        ]
    return pl.pallas_call(
        functools.partial(gather_kernel, seq_count, early),
        out_shape=tuple(out_shape),
        in_specs=[hbm, vmem, hbm, hbm, hbm, hbm, hbm, smem, smem, vmem, vmem],
        out_specs=(vmem,) * len(out_shape),
        scratch_shapes=[slots] * 4
        + [
            pltpu.VMEM(weight.shape, weight.dtype)
            for weight in (query_weight, key_weight, value_weight, hidden_in)
        ]
        + [pltpu.SemaphoreType.DMA((7,)), pltpu.SMEM((LINES, PAGE_ROWS), jnp.int32)],
        compiler_params=pltpu.CompilerParams(
            collective_id=0, has_side_effects=True, vmem_limit_bytes=40 << 20
        ),
    )(
        in_hbm(hidden_in),
        norm_gain.reshape(1, -1),
        in_hbm(query_weight),
        in_hbm(key_weight),
        in_hbm(value_weight),
        in_hbm(key_cache),
        in_hbm(value_cache),
        cached_lengths,
        group_ids,
        prompt_pages,
        own_pages,
    )


def finish_kernel(seq_count, tensor_count, kv_count, early, *refs):
    refs = list(refs)
    known = kv_count - 1 if early else kv_count
    part_refs, ls_refs = refs[:known], refs[known : 2 * known]
    del refs[: 2 * known]
    if early:
        left_ref, left_m_ref, packed_ref, qt_ref, kc_ref, vc_ref = refs[:6]
        del refs[:6]
    w_ref, out_ref = refs[:2]
    mix_ref, mix_got, mls_ref, side_got, sls_ref, gls_ref = refs[2:8]
    terms_ref, near_ref, near_got, far_ref, far_got = refs[8:13]
    side_send, side_recv, sls_send, sls_recv, mix_send, mix_recv, mls_send, mls_recv = refs[13:21]
    near_send, near_recv, far_send, far_recv = refs[21:25]
    del refs[:25]
    if early:
        late_ref, lists, list_sem = refs[2:]
        part_refs = part_refs + refs[:1]
        ls_refs = ls_refs + refs[1:2]
        fetch = pltpu.make_async_copy(packed_ref, lists, list_sem)
        fetch.start()
    tok_rows, out_cols = out_ref.shape
    per_kv = part_refs[0].shape[1] // HEAD_DIM
    me = lax.axis_index("seq")
    tensor = lax.axis_index("tensor")
    pair, core = tensor // 2, tensor % 2
    pairs = tensor_count // 2
    twin = (me, pair * 2 + 1 - core)
    outer = seq_count // 2
    place, side = me // 2, me % 2
    beside = (place * 2 + 1 - side, tensor)
    order = sorted(range(1, outer), key=lambda distance: -min(distance, outer - distance))

    def far_pair(distance):
        return (pair + distance) % pairs

    def line(distance, which):
        return (place + distance) % outer * 2 + which

    greet(
        [beside]
        + [(line(distance, side), tensor) for distance in range(1, outer)]
        + [twin]
        + [(me, far_pair(distance) * 2 + core) for distance in range(1, pairs)]
    )
    greeted(outer + pairs)
    started = []
    scales, sides, mixes, mix_scales, shares = {}, {}, {}, {}, {}

    def begin(table, key, *rest):
        table[key] = remote(*rest)
        table[key].start()
        started.append(table[key])

    def send_sides(kv):
        for distance in order + [0]:
            begin(
                scales,
                (kv, distance),
                ls_refs[kv].at[line(distance, 1 - side)],
                sls_ref.at[kv, distance],
                sls_send.at[kv, distance],
                sls_recv.at[kv, distance],
                beside,
            )
        for distance in order + [0]:
            begin(
                sides,
                (kv, distance),
                part_refs[kv].at[line(distance, 1 - side)],
                side_got.at[kv, distance],
                side_send.at[kv, distance],
                side_recv.at[kv, distance],
                beside,
            )

    def weighted(block, share):
        return [
            block[cols(sub)].astype(jnp.float32) * share[sub : sub + 1] for sub in range(per_kv)
        ]

    def plus(left, right):
        return [one + other for one, other in zip(left, right)]

    def weigh(kv):
        for distance in order + [0]:
            scales[kv, distance].wait_recv()
        own_lines = jnp.stack([ls_refs[kv][line(distance, side)] for distance in range(outer)])
        side_lines = sls_ref[kv]
        top = jnp.maximum(own_lines, side_lines)
        own_scale, side_scale = jnp.exp(own_lines - top), jnp.exp(side_lines - top)
        both = own_scale + side_scale
        mls_ref[kv] = top + jnp.log(both)
        for distance in order:
            begin(
                mix_scales,
                (kv, distance),
                mls_ref.at[kv, distance],
                gls_ref.at[kv, distance],
                mls_send.at[kv, distance],
                mls_recv.at[kv, distance],
                (line(distance, side), tensor),
            )
        shares[kv] = own_scale / both, side_scale / both

    def mixed(kv, distance):
        sides[kv, distance].wait_recv()
        own_shares, side_shares = shares[kv]
        return plus(
            weighted(part_refs[kv][line(distance, side)], own_shares[distance]),
            weighted(side_got[kv, distance], side_shares[distance]),
        )

    def send_mix(kv, distance):
        mix_ref[kv, distance] = jnp.concatenate(mixed(kv, distance), axis=0).astype(jnp.bfloat16)
        begin(
            mixes,
            (kv, distance),
            mix_ref.at[kv, distance],
            mix_got.at[kv, distance],
            mix_send.at[kv, distance],
            mix_recv.at[kv, distance],
            (line(distance, side), tensor),
        )

    def merged(kv):
        gls_ref[kv, 0] = mls_ref[kv, 0]
        for distance in order:
            mix_scales[kv, distance].wait_recv()
        lines = gls_ref[kv]
        lines = jnp.exp(lines - jnp.max(lines, axis=0, keepdims=True))
        share = lines / jnp.sum(lines, axis=0, keepdims=True)
        total = [block * share[0][sub : sub + 1] for sub, block in enumerate(mixed(kv, 0))]
        for distance in order:
            mixes[kv, distance].wait_recv()
            total = plus(total, weighted(mix_got[kv, distance], share[distance]))
        return jnp.concatenate(total, axis=0).astype(jnp.bfloat16)

    def terms_for(kv, attention, owner):
        start = pl.multiple_of(owner * out_cols, out_cols)
        span = per_kv * HEAD_DIM
        return lax.dot_general(
            attention,
            w_ref[kv * span : (kv + 1) * span, pl.ds(start, out_cols)],
            (((0,), (0,)), ((), ())),
            preferred_element_type=jnp.float32,
        )

    last = kv_count - 1
    for kv in range(known):
        send_sides(kv)
    if early:
        fetch.wait()
        ls_refs[last][...] = jnp.zeros_like(ls_refs[last])
        steps = [
            (step, request)
            for step in range(early // STEP_PAGES)
            for request in range(REQUESTS)
        ]
        tasks = [(weigh, (kv,)) for kv in range(known)]
        tasks += [(send_mix, (kv, distance)) for kv in range(known) for distance in order]
        share_of = -(-len(tasks) // len(steps))
        for step, request in steps:
            late_ref[request] = (left_ref if step == 0 else late_ref)[request] + early_terms(
                lists,
                qt_ref,
                kc_ref,
                vc_ref,
                left_m_ref[request, 0:1, :],
                request,
                step,
                last,
                per_kv,
            )
            for run, given in tasks[:share_of]:
                run(*given)
            del tasks[:share_of]
        for request in range(REQUESTS):
            settle(
                late_ref[request],
                left_m_ref[request, 0:1, :],
                request,
                part_refs[last],
                ls_refs[last],
                per_kv,
            )
        send_sides(last)
        ready = known
    else:
        ready = 0
    for kv in range(ready, kv_count):
        weigh(kv)
        for distance in order:
            send_mix(kv, distance)
    for kv in range(last):
        attention = merged(kv)
        for owner in range(tensor_count):
            if kv == 0:
                terms_ref[owner] = terms_for(kv, attention, owner)
            else:
                terms_ref[owner] += terms_for(kv, attention, owner)
    attention = merged(last)

    def all_terms(owner):
        return terms_ref[owner] + terms_for(last, attention, owner)

    nears = []
    for distance in list(range(1, pairs)) + [0]:
        near_ref[distance] = all_terms(far_pair(distance) * 2 + 1 - core)
        copy = remote(
            near_ref.at[distance],
            near_got.at[distance],
            near_send.at[distance],
            near_recv.at[distance],
            twin,
        )
        copy.start()
        started.append(copy)
        nears.append((distance, copy))
    fars = []
    for distance, copy in nears[:-1]:
        owner = far_pair(distance) * 2 + core
        own_terms = all_terms(owner)
        copy.wait_recv()
        far_ref[distance] = (own_terms + near_got[distance]).astype(far_ref.dtype)
        copy = remote(
            far_ref.at[distance],
            far_got.at[distance],
            far_send.at[distance],
            far_recv.at[distance],
            (me, owner),
        )
        copy.start()
        started.append(copy)
        fars.append(copy)
    result = all_terms(tensor)
    nears[-1][1].wait_recv()
    result = result + near_got[0]
    for distance in range(1, pairs):
        fars[distance - 1].wait_recv()
        result = result + far_got[distance].astype(jnp.float32)
    out_ref[...] = result.astype(jnp.bfloat16)
    for copy in started:
        copy.wait_send()


def finish(parts, scales, leftovers, out_weight, seq_count, tensor_count, early):
    q_rows, tok_rows = parts[0].shape[1:]
    kv_count = len(parts) + (1 if early else 0)
    out_cols = out_weight.shape[1] // tensor_count
    pairs = tensor_count // 2
    outer = seq_count // 2
    vmem = pl.BlockSpec(memory_space=pltpu.VMEM)
    block = pltpu.VMEM((pairs, tok_rows, out_cols), jnp.float32)
    far_block = pltpu.VMEM((pairs, tok_rows, out_cols), jnp.bfloat16)
    part_buf = pltpu.VMEM((kv_count, outer, q_rows, tok_rows), jnp.bfloat16)
    scale_buf = pltpu.VMEM((kv_count, outer, LINES, tok_rows), jnp.float32)
    line_sems = pltpu.SemaphoreType.DMA((kv_count, outer))
    pair_sems = pltpu.SemaphoreType.DMA((pairs,))
    operands = list(parts) + list(scales) + list(leftovers) + [out_weight]
    scratch = [part_buf, part_buf, scale_buf, part_buf, scale_buf, scale_buf]
    scratch += [pltpu.VMEM((tensor_count, tok_rows, out_cols), jnp.float32)]
    scratch += [block, block, far_block, far_block] + [line_sems] * 8 + [pair_sems] * 4
    if early:
        scratch += [
            pltpu.VMEM(parts[0].shape, parts[0].dtype),
            pltpu.VMEM(scales[0].shape, scales[0].dtype),
            pltpu.VMEM(leftovers[0].shape, leftovers[0].dtype),
            pltpu.SMEM(leftovers[2].shape, leftovers[2].dtype),
            pltpu.SemaphoreType.DMA(()),
        ]
    return pl.pallas_call(
        functools.partial(finish_kernel, seq_count, tensor_count, kv_count, early),
        out_shape=jax.ShapeDtypeStruct((tok_rows, out_cols), jnp.bfloat16),
        in_specs=[vmem] * len(operands),
        out_specs=vmem,
        scratch_shapes=scratch,
        compiler_params=pltpu.CompilerParams(
            collective_id=1, has_side_effects=True, vmem_limit_bytes=32 << 20
        ),
    )(*operands)


def regroup(array, rows):
    count, width = array.shape[0], array.shape[-1]
    if width == rows:
        return array
    array = jnp.moveaxis(array, 0, -2)
    array = array.reshape(array.shape[:-2] + (count * width // rows, rows))
    return jnp.moveaxis(array, -2, 0)


def body(
    hidden_in,
    norm_gain,
    query_weight,
    key_weight,
    value_weight,
    out_weight,
    key_cache,
    value_cache,
    cached_lengths,
    group_ids,
    prompt_pages,
    own_pages,
):
    tok_rows = hidden_in.shape[0]
    seq_count = lax.axis_size("seq")
    kv_count = key_weight.shape[1] // HEAD_DIM
    early = EARLY_STEPS * STEP_PAGES if tok_rows == BLOCK and kv_count > 1 else 0
    queries_t, fresh_k, fresh_v, packed, keys, values, *rest = gather(
        hidden_in,
        norm_gain,
        query_weight,
        key_weight,
        value_weight,
        key_cache,
        value_cache,
        cached_lengths,
        group_ids,
        prompt_pages,
        own_pages,
        seq_count,
        early,
    )
    queries_t = regroup(queries_t, BLOCK)
    sums, peak = rest if early else (None, None)
    found = attend(packed, queries_t, fresh_k, fresh_v, keys, values, sums, peak, early)
    known = kv_count - 1 if early else kv_count
    parts = [regroup(array, tok_rows) for array in found[:known]]
    scales = [regroup(array, tok_rows) for array in found[known : 2 * known]]
    leftovers = list(found[2 * known :])
    if early:
        leftovers += [queries_t, keys, values]
    return finish(
        parts, scales, leftovers, out_weight, seq_count, lax.axis_size("tensor"), early
    )


def solution(mesh):
    in_specs = (
        P("seq", None),
        P(),
        P(None, "tensor"),
        P(None, "tensor"),
        P(None, "tensor"),
        P("tensor", None),
        P("seq", None, "tensor"),
        P("seq", None, "tensor"),
        P(),
        P(),
        P(),
        P(),
    )
    out_specs = P("seq", "tensor")
    return jax.shard_map(body, mesh=mesh, in_specs=in_specs, out_specs=out_specs, check_vma=False)
```

```python
import functools
import math

import jax
import jax.numpy as jnp
from jax import lax
from jax.experimental import pallas as pl
from jax.experimental.pallas import tpu as pltpu
from jax.sharding import PartitionSpec as P

HEAD_DIM = 128
PAGE_ROWS = 128
ADDED_TOKENS = 512
GROUPS = 2
PROMPT_PAGES = 128
STEP_PAGES = 8
TAIL_PAGES = 4
BLOCK = 128
EXTRA = 16
REQUESTS = 2
LIMIT = 1e30
EARLY_STEPS = 2
SAFE_POWER = 100.0
SCORE_SCALE = 1.0 / math.sqrt(HEAD_DIM)
EXP2_SCALE = SCORE_SCALE * math.log2(math.e)
EMPTY = -1e30
SHIFT = 60.0 / EXP2_SCALE
BLOCKS = ADDED_TOKENS // BLOCK
LINES = 8
MESH = pl.DeviceIdType.MESH


def in_hbm(array):
    return pltpu.with_memory_space_constraint(array, pltpu.HBM)


def dot_nt(left, right):
    return lax.dot_general(
        left, right, (((1,), (1,)), ((), ())), preferred_element_type=jnp.float32
    )


def cols(index):
    return slice(index * HEAD_DIM, (index + 1) * HEAD_DIM)


def joined_queries(qt_ref, request, kv, per_kv):
    return jnp.concatenate(
        [
            qt_ref[request * BLOCKS + block, kv, cols(sub), :]
            for sub in range(per_kv)
            for block in range(BLOCKS)
        ],
        axis=1,
    )


def joined_marks(qt_ref, request, kv, per_kv):
    rows = [
        qt_ref[request * BLOCKS + block, kv, per_kv * HEAD_DIM :, :].astype(jnp.float32)[
            sub : sub + 1
        ]
        for sub in range(per_kv)
        for block in range(BLOCKS)
    ]
    return jnp.concatenate(rows, axis=1) + SHIFT


def values_t(values):
    ones = jnp.ones((EXTRA, values.shape[0]), jnp.bfloat16)
    return jnp.concatenate([values.T, ones], axis=0)


def page_group(lists, cache_ref, request, start, pages, kv):
    last = cache_ref.shape[0] - 1
    slots = [jnp.clip(lists[request, start + page] >> 8, 0, last) for page in range(pages)]
    return jnp.concatenate([cache_ref[slot, :, cols(kv)] for slot in slots], axis=0)


def page_bias(lists, request, start, pages):
    place = lax.broadcasted_iota(jnp.int32, (PAGE_ROWS, 1), 0)
    return jnp.concatenate(
        [
            jnp.where(place < (lists[request, start + page] & 255), 0.0, EMPTY)
            for page in range(pages)
        ],
        axis=0,
    )


def terms(queries, mark, keys, values, bias):
    scores = jnp.dot(keys, queries, preferred_element_type=jnp.float32)
    if bias is not None:
        scores = scores + bias
    weights = jnp.exp2((scores - mark) * EXP2_SCALE).astype(jnp.bfloat16)
    return jnp.dot(values_t(values), weights, preferred_element_type=jnp.float32)


def early_terms(lists, qt_ref, kc_ref, vc_ref, mark, request, step, kv, per_kv):
    start = step * STEP_PAGES
    return terms(
        joined_queries(qt_ref, request, kv, per_kv),
        mark,
        page_group(lists, kc_ref, request, start, STEP_PAGES, kv),
        page_group(lists, vc_ref, request, start, STEP_PAGES, kv),
        page_bias(lists, request, start, STEP_PAGES),
    )


def settle(sums, top, request, part_ref, ls_ref, per_kv):
    den = sums[HEAD_DIM : HEAD_DIM + 1]
    alive = (den > 0.0) & (top > 0.5 * EMPTY)
    den = jnp.where(alive, den, 1.0)
    scale = jnp.where(alive, top * SCORE_SCALE + jnp.log(den), EMPTY)
    parts = (sums[:HEAD_DIM] * jnp.where(alive, 1.0 / den, 0.0)).astype(jnp.bfloat16)
    for sub in range(per_kv):
        for block in range(BLOCKS):
            place = sub * BLOCKS + block
            span = slice(place * BLOCK, (place + 1) * BLOCK)
            part_ref[request * BLOCKS + block, cols(sub), :] = parts[:, span]
            ls_ref[request * BLOCKS + block, sub : sub + 1, :] = scale[:, span]


def attend_kernel(per_kv, tok_rows, late, early, *refs):
    refs = list(refs)
    packed_ref, qt_ref, fk_ref, fv_ref, kc_ref, vc_ref = refs[:6]
    del refs[:6]
    if late:
        start_ref, peak_ref = refs[:2]
        del refs[:2]
    kv_count = kc_ref.shape[2] // HEAD_DIM
    done_kv = kv_count - 1 if late else kv_count
    part_refs, ls_refs = refs[:done_kv], refs[done_kv : 2 * done_kv]
    del refs[: 2 * done_kv]
    if late:
        left_ref, left_m_ref, left_list_ref = refs[:3]
        del refs[:3]
    lists, m_ref, acc_ref, list_sem = refs
    fetch = pltpu.make_async_copy(packed_ref, lists, list_sem)
    fetch.start()
    requests = acc_ref.shape[0]
    width = per_kv * ADDED_TOKENS
    for ls_ref in ls_refs:
        ls_ref[...] = jnp.zeros_like(ls_ref)
    for kv in range(kv_count):
        for request in range(requests):
            if late and kv == 0:
                acc_ref[request, kv] = start_ref[request]
            else:
                acc_ref[request, kv] = jnp.zeros_like(acc_ref[request, kv])
            m_ref[request, kv, 0:1, :] = joined_marks(qt_ref, request, kv, per_kv)
    if late:
        left_list_ref[...] = packed_ref[...]

    def add(request, kv, keys, values, bias):
        queries = joined_queries(qt_ref, request, kv, per_kv)
        acc_ref[request, kv] += terms(queries, m_ref[request, kv, 0:1, :], keys, values, bias)

    def add_running(request, kv, keys, values, bias):
        queries = joined_queries(qt_ref, request, kv, per_kv)
        scores = jnp.dot(keys, queries, preferred_element_type=jnp.float32) + bias
        old = m_ref[request, kv, 0:1, :]
        new = jnp.maximum(old, jnp.max(scores, axis=0, keepdims=True))
        m_ref[request, kv, 0:1, :] = new
        weights = jnp.exp2((scores - new) * EXP2_SCALE)
        acc_ref[request, kv] = acc_ref[request, kv] * jnp.exp2((old - new) * EXP2_SCALE) + jnp.dot(
            values_t(values), weights.astype(jnp.bfloat16), preferred_element_type=jnp.float32
        )

    first = lax.axis_index("seq") * tok_rows
    home = first // ADDED_TOKENS

    def add_fresh(update):
        row = lax.broadcasted_iota(jnp.int32, (tok_rows, width), 0) + (first - home * ADDED_TOKENS)
        col = lax.broadcasted_iota(jnp.int32, (tok_rows, width), 1) % ADDED_TOKENS
        bias = jnp.where(row <= col, 0.0, EMPTY)
        for kv in range(kv_count):
            update(home, kv, fk_ref[:, cols(kv)], fv_ref[:, cols(kv)], bias)

    def add_pages(update, request, start, pages, masked):
        bias = page_bias(lists, request, start, pages) if masked else None
        for kv in range(kv_count):
            keys = page_group(lists, kc_ref, request, start, pages, kv)
            values = page_group(lists, vc_ref, request, start, pages, kv)
            update(request, kv, keys, values, bias)

    add_fresh(add)
    fetch.wait()

    def attend_request(request, carry):
        total = lists[requests + request, 0]
        count = jnp.maximum(total - early, 0)
        whole = jnp.maximum(count - 1, 0) // STEP_PAGES

        def step(index, carry):
            add_pages(add, request, early + index * STEP_PAGES, STEP_PAGES, False)
            return carry

        lax.fori_loop(0, whole, step, 0)
        done = whole * STEP_PAGES
        rest = count - done

        @pl.when((rest > 0) & (rest <= TAIL_PAGES))
        def _():
            add_pages(add, request, early + done, TAIL_PAGES, True)

        @pl.when(rest > TAIL_PAGES)
        def _():
            add_pages(add, request, early + done, STEP_PAGES, True)

        safe = [
            acc_ref[request, kv, HEAD_DIM : HEAD_DIM + 1, :] < LIMIT for kv in range(kv_count)
        ]
        if late:
            floats = joined_queries(qt_ref, request, kv_count - 1, per_kv).astype(jnp.float32)
            norms = jnp.sum(floats * floats, axis=0, keepdims=True) * jnp.max(peak_ref[...])
            power = (jnp.sqrt(norms) - m_ref[request, kv_count - 1, 0:1, :]) * EXP2_SCALE
            safe.append(power < SAFE_POWER)
        unsafe = jnp.max(
            jnp.concatenate([jnp.where(flags, 0.0, 1.0) for flags in safe], axis=0)
        )

        @pl.when(unsafe > 0.0)
        def _():
            acc_ref[request] = jnp.zeros_like(acc_ref[request])
            m_ref[request] = jnp.full_like(m_ref[request], EMPTY)

            @pl.when(request == home)
            def _():
                add_fresh(add_running)

            def step(index, carry):
                add_pages(add_running, request, index * TAIL_PAGES, TAIL_PAGES, True)
                return carry

            lax.fori_loop(0, (total + TAIL_PAGES - 1) // TAIL_PAGES, step, 0)
            if late:
                row = lax.broadcasted_iota(jnp.int32, left_list_ref.shape, 0)
                left_list_ref[...] = jnp.where(row == request, 0, left_list_ref[...])

        for kv in range(done_kv):
            settle(
                acc_ref[request, kv],
                m_ref[request, kv, 0:1, :],
                request,
                part_refs[kv],
                ls_refs[kv],
                per_kv,
            )
        if late:
            left_ref[request] = acc_ref[request, done_kv]
            left_m_ref[request] = m_ref[request, done_kv]
        return carry

    lax.fori_loop(0, requests, attend_request, 0)


def attend(packed, queries_t, fresh_k, fresh_v, key_cache, value_cache, early_sums, peak, early):
    blocks, kv_count, q_rows, _ = queries_t.shape
    late = early > 0
    done_kv = kv_count - 1 if late else kv_count
    q_rows -= EXTRA
    per_kv = q_rows // HEAD_DIM
    pages, _, kv_cols = key_cache.shape
    tok_rows = fresh_k.shape[0]
    requests = blocks // BLOCKS
    width = per_kv * ADDED_TOKENS
    vmem = pl.BlockSpec(memory_space=pltpu.VMEM)
    out_shape = [jax.ShapeDtypeStruct((blocks, q_rows, BLOCK), jnp.bfloat16)] * done_kv
    out_shape += [jax.ShapeDtypeStruct((blocks, LINES, BLOCK), jnp.float32)] * done_kv
    operands = [packed, queries_t, fresh_k, fresh_v, key_cache, value_cache]
    if late:
        out_shape += [
            jax.ShapeDtypeStruct((requests, HEAD_DIM + EXTRA, width), jnp.float32),
            jax.ShapeDtypeStruct((requests, LINES, width), jnp.float32),
            jax.ShapeDtypeStruct(packed.shape, packed.dtype),
        ]
        operands += [early_sums, peak]
    return pl.pallas_call(
        functools.partial(attend_kernel, per_kv, tok_rows, late, early),
        out_shape=tuple(out_shape),
        in_specs=[vmem] * len(operands),
        out_specs=(vmem,) * len(out_shape),
        scratch_shapes=[
            pltpu.SMEM(packed.shape, packed.dtype),
            pltpu.VMEM((requests, kv_count, LINES, width), jnp.float32),
            pltpu.VMEM((requests, kv_count, HEAD_DIM + EXTRA, width), jnp.float32),
            pltpu.SemaphoreType.DMA(()),
        ],
        compiler_params=pltpu.CompilerParams(vmem_limit_bytes=28 << 20),
        cost_estimate=pl.CostEstimate(
            flops=4 * pages * PAGE_ROWS * ADDED_TOKENS * q_rows * kv_count,
            bytes_accessed=4 * pages * PAGE_ROWS * kv_cols,
            transcendentals=pages * PAGE_ROWS * ADDED_TOKENS * per_kv * kv_count,
        ),
    )(*operands)


def page_lists(lengths_ref, groups_ref, prompt_ref, own_ref, packed_ref, pages_dev, me):
    count = PROMPT_PAGES + own_ref.shape[1]
    position = lax.broadcasted_iota(jnp.int32, (1, count), 1)
    owned, pages, lives = [], [], []
    for request in range(REQUESTS):
        prompt = prompt_ref[0:1, :]
        for group in range(1, GROUPS):
            prompt = jnp.where(groups_ref[request] == group, prompt_ref[group : group + 1, :], prompt)
        slots = jnp.concatenate([prompt, own_ref[request : request + 1, :]], axis=1)
        own_len = lengths_ref[request] - PROMPT_PAGES * PAGE_ROWS
        live = jnp.clip(own_len - (position - PROMPT_PAGES) * PAGE_ROWS, 0, PAGE_ROWS)
        live = jnp.where(position < PROMPT_PAGES, PAGE_ROWS, live)
        page = slots - me * pages_dev
        owned.append((page >= 0) & (page < pages_dev) & (live > 0))
        pages.append(page)
        lives.append(live)
    earlier = lax.broadcasted_iota(jnp.int32, (count, count), 0)
    earlier = earlier < lax.broadcasted_iota(jnp.int32, (count, count), 1)
    earlier = jnp.where(earlier, 1.0, 0.0).astype(jnp.bfloat16)
    place = lax.broadcasted_iota(jnp.int32, (PAGE_ROWS, count), 0).astype(jnp.float32)
    packed_ref[...] = jnp.zeros_like(packed_ref)
    for request in range(REQUESTS):
        mark = jnp.where(owned[request], 1.0, 0.0)
        marks = jnp.broadcast_to(mark, (EXTRA, count)).astype(jnp.bfloat16)
        before = jnp.dot(marks, earlier, preferred_element_type=jnp.float32)[0:1]
        before = jnp.where(owned[request], before, -1.0)
        onehot = jnp.where(before == place, 1.0, 0.0).astype(jnp.bfloat16)

        def pick(line):
            line = jnp.where(owned[request], line, 0).astype(jnp.float32)
            lines = jnp.broadcast_to(line, (EXTRA, count)).astype(jnp.bfloat16)
            return dot_nt(lines, onehot)[0:1]

        packed = pick(pages[request]) * 256.0 + pick(lives[request])
        packed_ref[request : request + 1, :] = packed.astype(jnp.int32)
        total = jnp.sum(mark, axis=1, keepdims=True)
        packed_ref[REQUESTS + request : REQUESTS + request + 1, :] = jnp.broadcast_to(
            total, (1, PAGE_ROWS)
        ).astype(jnp.int32)


def greet(peers):
    barrier = pltpu.get_barrier_semaphore()
    for peer in peers:
        pl.semaphore_signal(barrier, inc=1, device_id=peer, device_id_type=MESH)


def greeted(count):
    pl.semaphore_wait(pltpu.get_barrier_semaphore(), count)


def remote(source, target, send_sem, recv_sem, peer):
    return pltpu.make_async_remote_copy(
        src_ref=source,
        dst_ref=target,
        send_sem=send_sem,
        recv_sem=recv_sem,
        device_id=peer,
        device_id_type=MESH,
    )


def spread_columns(w_hbm, start, target, tensor_count, send_sem, recv_sem):
    me = lax.axis_index("seq")
    tensor = lax.axis_index("tensor")
    rows, columns = target.shape[1:]

    def block(owner):
        first = pl.multiple_of(owner * columns, columns)
        return w_hbm.at[pl.ds(start, rows), pl.ds(first, columns)]

    copies = [pltpu.make_async_copy(block(tensor), target.at[tensor], send_sem.at[0])]
    for distance in range(1, tensor_count):
        owner = (tensor + distance) % tensor_count
        copies.append(
            remote(
                block(owner),
                target.at[tensor],
                send_sem.at[distance],
                recv_sem.at[distance],
                (me, owner),
            )
        )
    return copies


def gather_kernel(seq_count, early, *refs):
    refs = list(refs)
    x_ref, gain_hbm, wq_ref, wk_ref, wv_ref, kc_hbm, vc_hbm, w_hbm = refs[:8]
    small_hbm = refs[8:12]
    qt_ref, fk_ref, fv_ref, packed_ref, kc_ref, vc_ref, w_cols = refs[12:19]
    del refs[:19]
    if early:
        sums_ref, peak_ref = refs[:2]
        del refs[:2]
    q_send, q_recv, qy_send, qy_recv, wq_buf, wk_buf, wv_buf, x_buf = refs[:8]
    load_sem, lists, gain_ref, lengths_ref, groups_ref, prompt_ref, own_ref = refs[8:15]
    w_send, w_recv = refs[15:]
    loads = [
        pltpu.make_async_copy(source, target, load_sem.at[index])
        for index, (source, target) in enumerate(
            (
                (x_ref, x_buf),
                (wk_ref, wk_buf),
                (wq_ref, wq_buf),
                (wv_ref, wv_buf),
                (kc_hbm, kc_ref),
                (vc_hbm, vc_ref),
                (packed_ref, lists),
                (gain_hbm, gain_ref),
                (small_hbm[0], lengths_ref),
                (small_hbm[1], groups_ref),
                (small_hbm[2], prompt_ref),
                (small_hbm[3], own_ref),
            )
        )
    ]
    small = loads[7:]
    for load in loads[:1] + small + loads[1:4]:
        load.start()
    me = lax.axis_index("seq")
    tensor = lax.axis_index("tensor")
    tensor_count = w_cols.shape[0]
    outer = seq_count // 2
    place, side = me // 2, me % 2
    twin = (place * 2 + 1 - side, tensor)
    kv_count = qt_ref.shape[1]
    per_kv = (qt_ref.shape[2] - EXTRA) // HEAD_DIM
    order = sorted(range(1, outer), key=lambda distance: -min(distance, outer - distance))

    def line_peer(distance):
        return (place + distance) % outer * 2 + side

    others = [(me, (tensor + distance) % tensor_count) for distance in range(1, tensor_count)]
    greet([twin] + [(line_peer(distance), tensor) for distance in range(1, outer)] + others)

    loads[0].wait()
    small[0].wait()
    floats = x_buf[...].astype(jnp.float32)
    mean = jnp.mean(floats * floats, axis=-1, keepdims=True)
    normed = (floats * lax.rsqrt(mean + 1e-05) * gain_ref[...]).astype(jnp.bfloat16)

    def project(weight):
        return jnp.dot(normed, weight, preferred_element_type=jnp.float32)

    loads[1].wait()
    keys = project(wk_buf[...])
    fk_ref[...] = keys.astype(jnp.bfloat16)
    keys_t = keys.T.astype(jnp.bfloat16)
    loads[2].wait()
    started = []

    def make(kv):
        span = per_kv * HEAD_DIM
        queries_t = project(wq_buf[:, kv * span : (kv + 1) * span]).T.astype(jnp.bfloat16)
        qt_ref[me, kv, :span, :] = queries_t
        right = keys_t[cols(kv)].astype(jnp.float32)
        marks = [
            jnp.sum(queries_t[cols(sub)].astype(jnp.float32) * right, axis=0, keepdims=True)
            for sub in range(per_kv)
        ]
        marks.append(jnp.zeros((EXTRA - per_kv, marks[0].shape[1]), jnp.float32))
        qt_ref[me, kv, span:, :] = jnp.concatenate(marks, axis=0).astype(jnp.bfloat16)

    def launch(kv):
        own = qt_ref.at[me, kv]
        copy = remote(own, own, qy_send.at[kv, 0], qy_recv.at[kv, 0], twin)
        copy.start()
        started.append(copy)
        for distance in order:
            peer = (line_peer(distance), tensor)
            copy = remote(own, own, q_send.at[kv, distance], q_recv.at[kv, distance], peer)
            copy.start()
            started.append(copy)

    def relay(kv, distance):
        block = qt_ref.at[line_peer(outer - distance), kv]
        remote(block, block, q_send.at[kv, distance], q_recv.at[kv, distance], twin).wait_recv()
        copy = remote(block, block, qy_send.at[kv, distance], qy_recv.at[kv, distance], twin)
        copy.start()
        started.append(copy)

    def arrive(kv):
        for distance in [0] + order:
            block = qt_ref.at[(place + outer - distance) % outer * 2 + 1 - side, kv]
            remote(block, block, qy_send.at[kv, distance], qy_recv.at[kv, distance], twin).wait_recv()

    make(0)
    greeted(outer + tensor_count - 1)
    launch(0)
    for load in loads[4:6]:
        load.start()
    spread = spread_columns(w_hbm, 0, w_cols, tensor_count, w_send, w_recv)
    for copy in spread:
        copy.start()
    for kv in range(1, kv_count):
        make(kv)
    loads[3].wait()
    fv_ref[...] = project(wv_buf[...]).astype(jnp.bfloat16)
    for load in small[1:]:
        load.wait()
    page_lists(lengths_ref, groups_ref, prompt_ref, own_ref, packed_ref, kc_ref.shape[0], me)
    for distance in order[: len(order) // 2 + 1]:
        relay(0, distance)
    for kv in range(1, kv_count):
        launch(kv)
    for distance in order[len(order) // 2 + 1 :]:
        relay(0, distance)
    loads[6].start()
    for load in loads[4:7]:
        load.wait()
    waiting = [(kv, distance) for kv in range(1, kv_count) for distance in order]
    if early:
        peak = jnp.zeros((PAGE_ROWS, 1), jnp.float32)
        for page in range(kc_ref.shape[0]):
            floats = kc_ref[page, :, cols(kv_count - 1)].astype(jnp.float32)
            peak = jnp.maximum(peak, jnp.sum(floats * floats, axis=1, keepdims=True))
        peak_ref[...] = jnp.broadcast_to(peak, peak_ref.shape)
        arrive(0)
        marks = [joined_marks(qt_ref, request, 0, per_kv) for request in range(REQUESTS)]
        for step in range(early // STEP_PAGES):
            for request in range(REQUESTS):
                fresh = early_terms(
                    lists, qt_ref, kc_ref, vc_ref, marks[request], request, step, 0, per_kv
                )
                if step == 0:
                    sums_ref[request] = fresh
                else:
                    sums_ref[request] += fresh
                if waiting:
                    relay(*waiting.pop(0))
    else:
        arrive(0)
    for kv, distance in waiting:
        relay(kv, distance)
    for kv in range(1, kv_count):
        arrive(kv)
    for copy in spread:
        copy.wait()
    for copy in started:
        copy.wait_send()


def gather(
    hidden_in,
    norm_gain,
    query_weight,
    key_weight,
    value_weight,
    key_cache,
    value_cache,
    cached_lengths,
    group_ids,
    prompt_pages,
    own_pages,
    out_weight,
    seq_count,
    tensor_count,
    early,
):
    tok_rows = hidden_in.shape[0]
    q_cols, kv_cols = query_weight.shape[1], key_weight.shape[1]
    kv_count = kv_cols // HEAD_DIM
    per_kv = q_cols // kv_cols
    slots = pltpu.SemaphoreType.DMA((kv_count, seq_count // 2))
    vmem = pl.BlockSpec(memory_space=pltpu.VMEM)
    hbm = pl.BlockSpec(memory_space=pltpu.HBM)
    fresh = jax.ShapeDtypeStruct((tok_rows, kv_cols), jnp.bfloat16)
    rows = per_kv * HEAD_DIM + EXTRA
    out_shape = [
        jax.ShapeDtypeStruct((seq_count, kv_count, rows, tok_rows), jnp.bfloat16),
        fresh,
        fresh,
        jax.ShapeDtypeStruct((LINES, PAGE_ROWS), jnp.int32),
        jax.ShapeDtypeStruct(key_cache.shape, key_cache.dtype),
        jax.ShapeDtypeStruct(value_cache.shape, value_cache.dtype),
        jax.ShapeDtypeStruct(
            (tensor_count, per_kv * HEAD_DIM, out_weight.shape[1] // tensor_count), jnp.bfloat16
        ),
    ]
    if early:
        sums = (REQUESTS, HEAD_DIM + EXTRA, per_kv * ADDED_TOKENS)
        out_shape += [
            jax.ShapeDtypeStruct(sums, jnp.float32),
            jax.ShapeDtypeStruct((PAGE_ROWS, HEAD_DIM), jnp.float32),
        ]
    return pl.pallas_call(
        functools.partial(gather_kernel, seq_count, early),
        out_shape=tuple(out_shape),
        in_specs=[hbm] * 12,
        out_specs=(vmem,) * len(out_shape),
        scratch_shapes=[slots] * 4
        + [
            pltpu.VMEM(weight.shape, weight.dtype)
            for weight in (query_weight, key_weight, value_weight, hidden_in)
        ]
        + [
            pltpu.SemaphoreType.DMA((12,)),
            pltpu.SMEM((LINES, PAGE_ROWS), jnp.int32),
            pltpu.VMEM((1, norm_gain.shape[0]), norm_gain.dtype),
            pltpu.SMEM(cached_lengths.shape, jnp.int32),
            pltpu.SMEM(group_ids.shape, jnp.int32),
            pltpu.VMEM(prompt_pages.shape, jnp.int32),
            pltpu.VMEM(own_pages.shape, jnp.int32),
            pltpu.SemaphoreType.DMA((tensor_count,)),
            pltpu.SemaphoreType.DMA((tensor_count,)),
        ],
        compiler_params=pltpu.CompilerParams(
            collective_id=0, has_side_effects=True, vmem_limit_bytes=40 << 20
        ),
    )(
        in_hbm(hidden_in),
        in_hbm(norm_gain.reshape(1, -1)),
        in_hbm(query_weight),
        in_hbm(key_weight),
        in_hbm(value_weight),
        in_hbm(key_cache),
        in_hbm(value_cache),
        in_hbm(out_weight),
        in_hbm(cached_lengths),
        in_hbm(group_ids),
        in_hbm(prompt_pages),
        in_hbm(own_pages),
    )


def finish_kernel(seq_count, tensor_count, kv_count, early, *refs):
    refs = list(refs)
    known = kv_count - 1 if early else kv_count
    part_refs, ls_refs = refs[:known], refs[known : 2 * known]
    del refs[: 2 * known]
    if early:
        left_ref, left_m_ref, packed_ref, qt_ref, kc_ref, vc_ref = refs[:6]
        del refs[:6]
    w_early, w_hbm, out_ref = refs[:3]
    mix_ref, mix_got, mls_ref, side_got, sls_ref, gls_ref = refs[3:9]
    w_late, att_ref = refs[9:11]
    side_send, side_recv, sls_send, sls_recv, mix_send, mix_recv, mls_send, mls_recv = refs[11:19]
    w_send, w_recv, far_send, far_recv, near_send, near_recv = refs[19:25]
    del refs[:25]
    if early:
        late_ref, lists, list_sem = refs[2:]
        part_refs = part_refs + refs[:1]
        ls_refs = ls_refs + refs[1:2]
        fetch = pltpu.make_async_copy(packed_ref, lists, list_sem)
        fetch.start()
    tok_rows, out_cols = out_ref.shape
    per_kv = part_refs[0].shape[1] // HEAD_DIM
    me = lax.axis_index("seq")
    tensor = lax.axis_index("tensor")
    pair, core = tensor // 2, tensor % 2
    pairs = tensor_count // 2
    twin = (me, pair * 2 + 1 - core)
    outer = seq_count // 2
    place, side = me // 2, me % 2
    beside = (place * 2 + 1 - side, tensor)
    order = sorted(range(1, outer), key=lambda distance: -min(distance, outer - distance))

    def far_pair(distance):
        return (pair + distance) % pairs

    def line(distance, which):
        return (place + distance) % outer * 2 + which

    greet(
        [beside]
        + [(line(distance, side), tensor) for distance in range(1, outer)]
        + [twin]
        + [(me, far_pair(distance) * 2 + core) for distance in range(1, pairs)]
        + [(me, far_pair(distance) * 2 + 1 - core) for distance in range(1, pairs)]
    )
    greeted(outer + tensor_count - 1)
    started = []
    scales, sides, mixes, mix_scales, shares = {}, {}, {}, {}, {}

    def begin(table, key, *rest):
        table[key] = remote(*rest)
        table[key].start()
        started.append(table[key])

    def send_sides(kv):
        for distance in order + [0]:
            begin(
                scales,
                (kv, distance),
                ls_refs[kv].at[line(distance, 1 - side)],
                sls_ref.at[kv, distance],
                sls_send.at[kv, distance],
                sls_recv.at[kv, distance],
                beside,
            )
        for distance in order + [0]:
            begin(
                sides,
                (kv, distance),
                part_refs[kv].at[line(distance, 1 - side)],
                side_got.at[kv, distance],
                side_send.at[kv, distance],
                side_recv.at[kv, distance],
                beside,
            )

    def weighted(block, share):
        return [
            block[cols(sub)].astype(jnp.float32) * share[sub : sub + 1] for sub in range(per_kv)
        ]

    def plus(left, right):
        return [one + other for one, other in zip(left, right)]

    def weigh(kv):
        for distance in order + [0]:
            scales[kv, distance].wait_recv()
        own_lines = jnp.stack([ls_refs[kv][line(distance, side)] for distance in range(outer)])
        side_lines = sls_ref[kv]
        top = jnp.maximum(own_lines, side_lines)
        own_scale, side_scale = jnp.exp(own_lines - top), jnp.exp(side_lines - top)
        both = own_scale + side_scale
        mls_ref[kv] = top + jnp.log(both)
        for distance in order:
            begin(
                mix_scales,
                (kv, distance),
                mls_ref.at[kv, distance],
                gls_ref.at[kv, distance],
                mls_send.at[kv, distance],
                mls_recv.at[kv, distance],
                (line(distance, side), tensor),
            )
        shares[kv] = own_scale / both, side_scale / both

    def mixed(kv, distance):
        sides[kv, distance].wait_recv()
        own_shares, side_shares = shares[kv]
        return plus(
            weighted(part_refs[kv][line(distance, side)], own_shares[distance]),
            weighted(side_got[kv, distance], side_shares[distance]),
        )

    def send_mix(kv, distance):
        mix_ref[kv, distance] = jnp.concatenate(mixed(kv, distance), axis=0).astype(jnp.bfloat16)
        begin(
            mixes,
            (kv, distance),
            mix_ref.at[kv, distance],
            mix_got.at[kv, distance],
            mix_send.at[kv, distance],
            mix_recv.at[kv, distance],
            (line(distance, side), tensor),
        )

    def merged(kv):
        gls_ref[kv, 0] = mls_ref[kv, 0]
        for distance in order:
            mix_scales[kv, distance].wait_recv()
        lines = gls_ref[kv]
        lines = jnp.exp(lines - jnp.max(lines, axis=0, keepdims=True))
        share = lines / jnp.sum(lines, axis=0, keepdims=True)
        total = [block * share[0][sub : sub + 1] for sub, block in enumerate(mixed(kv, 0))]
        for distance in order:
            mixes[kv, distance].wait_recv()
            total = plus(total, weighted(mix_got[kv, distance], share[distance]))
        return jnp.concatenate(total, axis=0).astype(jnp.bfloat16)

    def twin_copy(kv, distance, which):
        block = att_ref.at[(pair + pairs - distance) % pairs * 2 + which, kv]
        return remote(block, block, near_send.at[kv, distance], near_recv.at[kv, distance], twin)

    def far_copy(kv, distance, source, target):
        block = att_ref.at[source, kv]
        return remote(
            block, block, far_send.at[kv, distance], far_recv.at[kv, distance], (me, target)
        )

    def share_out(kv, attention):
        att_ref[tensor, kv] = attention
        copies = [
            far_copy(kv, distance, tensor, far_pair(distance) * 2 + core)
            for distance in range(1, pairs)
        ]
        copies.append(twin_copy(kv, 0, core))
        for copy in copies:
            copy.start()
            started.append(copy)

    def pass_on(kv):
        for distance in range(1, pairs):
            source = far_pair(pairs - distance) * 2 + core
            far_copy(kv, distance, source, source).wait_recv()
            copy = twin_copy(kv, distance, core)
            copy.start()
            started.append(copy)

    def terms_of(kv, source):
        rest = (kv - 1) * per_kv * HEAD_DIM
        if kv == 0:
            weight = w_early[source]
        else:
            weight = w_late[source, rest : rest + per_kv * HEAD_DIM, :]
        return lax.dot_general(
            att_ref[source, kv],
            weight,
            (((0,), (0,)), ((), ())),
            preferred_element_type=jnp.float32,
        )

    def near_terms(kv):
        total = terms_of(kv, tensor)
        for distance in range(1, pairs):
            total = total + terms_of(kv, far_pair(distance) * 2 + core)
        return total

    def twin_terms(kv):
        total = None
        for distance in range(pairs):
            twin_copy(kv, distance, 1 - core).wait_recv()
            fresh = terms_of(kv, (pair + pairs - distance) % pairs * 2 + 1 - core)
            total = fresh if total is None else total + fresh
        return total

    last = kv_count - 1
    for kv in range(known):
        send_sides(kv)
    spread = spread_columns(w_hbm, per_kv * HEAD_DIM, w_late, tensor_count, w_send, w_recv)
    for copy in spread:
        copy.start()
    if early:
        fetch.wait()
        ls_refs[last][...] = jnp.zeros_like(ls_refs[last])
        steps = [
            (step, request)
            for step in range(early // STEP_PAGES)
            for request in range(REQUESTS)
        ]
        tasks = [(weigh, (kv,)) for kv in range(known)]
        tasks += [(send_mix, (kv, distance)) for kv in range(known) for distance in order]
        share_of = -(-len(tasks) // len(steps))
        for step, request in steps:
            late_ref[request] = (left_ref if step == 0 else late_ref)[request] + early_terms(
                lists,
                qt_ref,
                kc_ref,
                vc_ref,
                left_m_ref[request, 0:1, :],
                request,
                step,
                last,
                per_kv,
            )
            for run, given in tasks[:share_of]:
                run(*given)
            del tasks[:share_of]
        for request in range(REQUESTS):
            settle(
                late_ref[request],
                left_m_ref[request, 0:1, :],
                request,
                part_refs[last],
                ls_refs[last],
                per_kv,
            )
        send_sides(last)
        ready = known
    else:
        ready = 0
    for kv in range(ready, kv_count):
        weigh(kv)
        for distance in order:
            send_mix(kv, distance)
    result = None
    for kv in range(kv_count):
        share_out(kv, merged(kv))
        if kv == 1:
            for copy in spread:
                copy.wait()
        pass_on(kv)
        fresh = near_terms(kv) + twin_terms(kv)
        result = fresh if result is None else result + fresh
    out_ref[...] = result.astype(jnp.bfloat16)
    for copy in started:
        copy.wait_send()


def finish(parts, scales, leftovers, w_cols, out_weight, seq_count, tensor_count, early):
    q_rows, tok_rows = parts[0].shape[1:]
    kv_count = len(parts) + (1 if early else 0)
    out_cols = out_weight.shape[1] // tensor_count
    pairs = tensor_count // 2
    outer = seq_count // 2
    vmem = pl.BlockSpec(memory_space=pltpu.VMEM)
    w_block = (tensor_count, out_weight.shape[0] - w_cols.shape[1], out_cols)
    att_block = (tensor_count, kv_count, q_rows, tok_rows)
    part_buf = pltpu.VMEM((kv_count, outer, q_rows, tok_rows), jnp.bfloat16)
    scale_buf = pltpu.VMEM((kv_count, outer, LINES, tok_rows), jnp.float32)
    line_sems = pltpu.SemaphoreType.DMA((kv_count, outer))
    pair_sems = pltpu.SemaphoreType.DMA((kv_count, pairs))
    w_sems = pltpu.SemaphoreType.DMA((tensor_count,))
    operands = list(parts) + list(scales) + list(leftovers) + [w_cols, in_hbm(out_weight)]
    scratch = [part_buf, part_buf, scale_buf, part_buf, scale_buf, scale_buf]
    scratch += [pltpu.VMEM(w_block, jnp.bfloat16), pltpu.VMEM(att_block, jnp.bfloat16)]
    scratch += [line_sems] * 8 + [w_sems] * 2 + [pair_sems] * 4
    if early:
        scratch += [
            pltpu.VMEM(parts[0].shape, parts[0].dtype),
            pltpu.VMEM(scales[0].shape, scales[0].dtype),
            pltpu.VMEM(leftovers[0].shape, leftovers[0].dtype),
            pltpu.SMEM(leftovers[2].shape, leftovers[2].dtype),
            pltpu.SemaphoreType.DMA(()),
        ]
    return pl.pallas_call(
        functools.partial(finish_kernel, seq_count, tensor_count, kv_count, early),
        out_shape=jax.ShapeDtypeStruct((tok_rows, out_cols), jnp.bfloat16),
        in_specs=[vmem] * (len(operands) - 1) + [pl.BlockSpec(memory_space=pltpu.HBM)],
        out_specs=vmem,
        scratch_shapes=scratch,
        compiler_params=pltpu.CompilerParams(
            collective_id=1, has_side_effects=True, vmem_limit_bytes=32 << 20
        ),
    )(*operands)


def regroup(array, rows):
    count, width = array.shape[0], array.shape[-1]
    if width == rows:
        return array
    array = jnp.moveaxis(array, 0, -2)
    array = array.reshape(array.shape[:-2] + (count * width // rows, rows))
    return jnp.moveaxis(array, -2, 0)


def body(
    hidden_in,
    norm_gain,
    query_weight,
    key_weight,
    value_weight,
    out_weight,
    key_cache,
    value_cache,
    cached_lengths,
    group_ids,
    prompt_pages,
    own_pages,
):
    tok_rows = hidden_in.shape[0]
    seq_count = lax.axis_size("seq")
    kv_count = key_weight.shape[1] // HEAD_DIM
    early = EARLY_STEPS * STEP_PAGES if tok_rows == BLOCK and kv_count > 1 else 0
    tensor_count = lax.axis_size("tensor")
    queries_t, fresh_k, fresh_v, packed, keys, values, w_cols, *rest = gather(
        hidden_in,
        norm_gain,
        query_weight,
        key_weight,
        value_weight,
        key_cache,
        value_cache,
        cached_lengths,
        group_ids,
        prompt_pages,
        own_pages,
        out_weight,
        seq_count,
        tensor_count,
        early,
    )
    queries_t = regroup(queries_t, BLOCK)
    sums, peak = rest if early else (None, None)
    found = attend(packed, queries_t, fresh_k, fresh_v, keys, values, sums, peak, early)
    known = kv_count - 1 if early else kv_count
    parts = [regroup(array, tok_rows) for array in found[:known]]
    scales = [regroup(array, tok_rows) for array in found[known : 2 * known]]
    leftovers = list(found[2 * known :])
    if early:
        leftovers += [queries_t, keys, values]
    return finish(
        parts, scales, leftovers, w_cols, out_weight, seq_count, tensor_count, early
    )


def solution(mesh):
    in_specs = (
        P("seq", None),
        P(),
        P(None, "tensor"),
        P(None, "tensor"),
        P(None, "tensor"),
        P("tensor", None),
        P("seq", None, "tensor"),
        P("seq", None, "tensor"),
        P(),
        P(),
        P(),
        P(),
    )
    out_specs = P("seq", "tensor")
    return jax.shard_map(body, mesh=mesh, in_specs=in_specs, out_specs=out_specs, check_vma=False)
```

```python
import functools
import math

import jax
import jax.numpy as jnp
from jax import lax
from jax.experimental import pallas as pl
from jax.experimental.pallas import tpu as pltpu
from jax.sharding import PartitionSpec as P

HEAD_DIM = 128
PAGE_ROWS = 128
ADDED_TOKENS = 512
GROUPS = 2
PROMPT_PAGES = 128
STEP_PAGES = 8
TAIL_PAGES = 4
BLOCK = 128
EXTRA = 16
REQUESTS = 2
LIMIT = 1e30
EARLY_STEPS = 3
LATE_STEPS = 2
SAFE_POWER = 100.0
SCORE_SCALE = 1.0 / math.sqrt(HEAD_DIM)
EXP2_SCALE = SCORE_SCALE * math.log2(math.e)
EMPTY = -1e30
SHIFT = 60.0 / EXP2_SCALE
BLOCKS = ADDED_TOKENS // BLOCK
LINES = 8
MESH = pl.DeviceIdType.MESH


def in_hbm(array):
    return pltpu.with_memory_space_constraint(array, pltpu.HBM)


def dot_nt(left, right):
    return lax.dot_general(
        left, right, (((1,), (1,)), ((), ())), preferred_element_type=jnp.float32
    )


def cols(index):
    return slice(index * HEAD_DIM, (index + 1) * HEAD_DIM)


def joined_queries(qt_ref, request, kv, per_kv):
    return jnp.concatenate(
        [
            qt_ref[request * BLOCKS + block, kv, cols(sub), :]
            for sub in range(per_kv)
            for block in range(BLOCKS)
        ],
        axis=1,
    )


def joined_marks(qt_ref, request, kv, per_kv):
    rows = [
        qt_ref[request * BLOCKS + block, kv, per_kv * HEAD_DIM :, :].astype(jnp.float32)[
            sub : sub + 1
        ]
        for sub in range(per_kv)
        for block in range(BLOCKS)
    ]
    return jnp.concatenate(rows, axis=1) + SHIFT


def values_t(values):
    ones = jnp.ones((EXTRA, values.shape[0]), jnp.bfloat16)
    return jnp.concatenate([values.T, ones], axis=0)


def page_group(lists, cache_ref, request, start, pages, kv):
    last = cache_ref.shape[0] - 1
    slots = [jnp.clip(lists[request, start + page] >> 8, 0, last) for page in range(pages)]
    return jnp.concatenate([cache_ref[slot, :, cols(kv)] for slot in slots], axis=0)


def page_bias(lists, request, start, pages):
    place = lax.broadcasted_iota(jnp.int32, (PAGE_ROWS, 1), 0)
    return jnp.concatenate(
        [
            jnp.where(place < (lists[request, start + page] & 255), 0.0, EMPTY)
            for page in range(pages)
        ],
        axis=0,
    )


def terms(queries, mark, keys, values, bias):
    scores = jnp.dot(keys, queries, preferred_element_type=jnp.float32)
    if bias is not None:
        scores = scores + bias
    weights = jnp.exp2((scores - mark) * EXP2_SCALE).astype(jnp.bfloat16)
    return jnp.dot(values_t(values), weights, preferred_element_type=jnp.float32)


def early_terms(lists, qt_ref, kc_ref, vc_ref, mark, request, step, kv, per_kv):
    start = step * STEP_PAGES
    return terms(
        joined_queries(qt_ref, request, kv, per_kv),
        mark,
        page_group(lists, kc_ref, request, start, STEP_PAGES, kv),
        page_group(lists, vc_ref, request, start, STEP_PAGES, kv),
        page_bias(lists, request, start, STEP_PAGES),
    )


def settle(sums, top, request, part_ref, ls_ref, per_kv):
    den = sums[HEAD_DIM : HEAD_DIM + 1]
    alive = (den > 0.0) & (top > 0.5 * EMPTY)
    den = jnp.where(alive, den, 1.0)
    scale = jnp.where(alive, top * SCORE_SCALE + jnp.log(den), EMPTY)
    parts = (sums[:HEAD_DIM] * jnp.where(alive, 1.0 / den, 0.0)).astype(jnp.bfloat16)
    for sub in range(per_kv):
        for block in range(BLOCKS):
            place = sub * BLOCKS + block
            span = slice(place * BLOCK, (place + 1) * BLOCK)
            part_ref[request * BLOCKS + block, cols(sub), :] = parts[:, span]
            ls_ref[request * BLOCKS + block, sub : sub + 1, :] = scale[:, span]


def attend_kernel(per_kv, tok_rows, late, early, later, *refs):
    refs = list(refs)
    packed_ref, qt_ref, fk_ref, fv_ref, kc_ref, vc_ref = refs[:6]
    del refs[:6]
    if late:
        start_ref, peak_ref = refs[:2]
        del refs[:2]
    kv_count = kc_ref.shape[2] // HEAD_DIM
    done_kv = kv_count - 1 if late else kv_count
    part_refs, ls_refs = refs[:done_kv], refs[done_kv : 2 * done_kv]
    del refs[: 2 * done_kv]
    if late:
        left_ref, left_m_ref, left_list_ref = refs[:3]
        del refs[:3]
    lists, m_ref, acc_ref, list_sem = refs
    fetch = pltpu.make_async_copy(packed_ref, lists, list_sem)
    fetch.start()
    requests = acc_ref.shape[0]
    width = per_kv * ADDED_TOKENS
    for ls_ref in ls_refs:
        ls_ref[...] = jnp.zeros_like(ls_ref)
    for kv in range(kv_count):
        for request in range(requests):
            if late and kv == 0:
                acc_ref[request, kv] = start_ref[request]
            else:
                acc_ref[request, kv] = jnp.zeros_like(acc_ref[request, kv])
            m_ref[request, kv, 0:1, :] = joined_marks(qt_ref, request, kv, per_kv)
    if late:
        left_list_ref[...] = packed_ref[...]

    def add(request, kv, keys, values, bias):
        queries = joined_queries(qt_ref, request, kv, per_kv)
        acc_ref[request, kv] += terms(queries, m_ref[request, kv, 0:1, :], keys, values, bias)

    def add_running(request, kv, keys, values, bias):
        queries = joined_queries(qt_ref, request, kv, per_kv)
        scores = jnp.dot(keys, queries, preferred_element_type=jnp.float32) + bias
        old = m_ref[request, kv, 0:1, :]
        new = jnp.maximum(old, jnp.max(scores, axis=0, keepdims=True))
        m_ref[request, kv, 0:1, :] = new
        weights = jnp.exp2((scores - new) * EXP2_SCALE)
        acc_ref[request, kv] = acc_ref[request, kv] * jnp.exp2((old - new) * EXP2_SCALE) + jnp.dot(
            values_t(values), weights.astype(jnp.bfloat16), preferred_element_type=jnp.float32
        )

    first = lax.axis_index("seq") * tok_rows
    home = first // ADDED_TOKENS

    def add_fresh(update):
        row = lax.broadcasted_iota(jnp.int32, (tok_rows, width), 0) + (first - home * ADDED_TOKENS)
        col = lax.broadcasted_iota(jnp.int32, (tok_rows, width), 1) % ADDED_TOKENS
        bias = jnp.where(row <= col, 0.0, EMPTY)
        for kv in range(kv_count):
            update(home, kv, fk_ref[:, cols(kv)], fv_ref[:, cols(kv)], bias)

    def add_pages(update, request, start, pages, masked, kvs=range(kv_count)):
        bias = page_bias(lists, request, start, pages) if masked else None
        for kv in kvs:
            keys = page_group(lists, kc_ref, request, start, pages, kv)
            values = page_group(lists, vc_ref, request, start, pages, kv)
            update(request, kv, keys, values, bias)

    add_fresh(add)
    fetch.wait()

    def attend_request(request, carry):
        total = lists[requests + request, 0]
        count = jnp.maximum(total - early, 0)
        whole = jnp.maximum(count - 1, 0) // STEP_PAGES

        def step(index, carry):
            add_pages(add, request, early + index * STEP_PAGES, STEP_PAGES, False)
            return carry

        for start in range(later, early, STEP_PAGES):

            @pl.when(total > start)
            def _():
                add_pages(add, request, start, STEP_PAGES, True, range(done_kv, kv_count))

        lax.fori_loop(0, whole, step, 0)
        done = whole * STEP_PAGES
        rest = count - done

        @pl.when((rest > 0) & (rest <= TAIL_PAGES))
        def _():
            add_pages(add, request, early + done, TAIL_PAGES, True)

        @pl.when(rest > TAIL_PAGES)
        def _():
            add_pages(add, request, early + done, STEP_PAGES, True)

        safe = [
            acc_ref[request, kv, HEAD_DIM : HEAD_DIM + 1, :] < LIMIT for kv in range(kv_count)
        ]
        if late:
            floats = joined_queries(qt_ref, request, kv_count - 1, per_kv).astype(jnp.float32)
            norms = jnp.sum(floats * floats, axis=0, keepdims=True) * jnp.max(peak_ref[...])
            power = (jnp.sqrt(norms) - m_ref[request, kv_count - 1, 0:1, :]) * EXP2_SCALE
            safe.append(power < SAFE_POWER)
        unsafe = jnp.max(
            jnp.concatenate([jnp.where(flags, 0.0, 1.0) for flags in safe], axis=0)
        )

        @pl.when(unsafe > 0.0)
        def _():
            acc_ref[request] = jnp.zeros_like(acc_ref[request])
            m_ref[request] = jnp.full_like(m_ref[request], EMPTY)

            @pl.when(request == home)
            def _():
                add_fresh(add_running)

            def step(index, carry):
                add_pages(add_running, request, index * TAIL_PAGES, TAIL_PAGES, True)
                return carry

            lax.fori_loop(0, (total + TAIL_PAGES - 1) // TAIL_PAGES, step, 0)
            if late:
                row = lax.broadcasted_iota(jnp.int32, left_list_ref.shape, 0)
                left_list_ref[...] = jnp.where(row == request, 0, left_list_ref[...])

        for kv in range(done_kv):
            settle(
                acc_ref[request, kv],
                m_ref[request, kv, 0:1, :],
                request,
                part_refs[kv],
                ls_refs[kv],
                per_kv,
            )
        if late:
            left_ref[request] = acc_ref[request, done_kv]
            left_m_ref[request] = m_ref[request, done_kv]
        return carry

    lax.fori_loop(0, requests, attend_request, 0)


def attend(
    packed, queries_t, fresh_k, fresh_v, key_cache, value_cache, early_sums, peak, early, later
):
    blocks, kv_count, q_rows, _ = queries_t.shape
    late = early > 0
    done_kv = kv_count - 1 if late else kv_count
    q_rows -= EXTRA
    per_kv = q_rows // HEAD_DIM
    pages, _, kv_cols = key_cache.shape
    tok_rows = fresh_k.shape[0]
    requests = blocks // BLOCKS
    width = per_kv * ADDED_TOKENS
    vmem = pl.BlockSpec(memory_space=pltpu.VMEM)
    out_shape = [jax.ShapeDtypeStruct((blocks, q_rows, BLOCK), jnp.bfloat16)] * done_kv
    out_shape += [jax.ShapeDtypeStruct((blocks, LINES, BLOCK), jnp.float32)] * done_kv
    operands = [packed, queries_t, fresh_k, fresh_v, key_cache, value_cache]
    if late:
        out_shape += [
            jax.ShapeDtypeStruct((requests, HEAD_DIM + EXTRA, width), jnp.float32),
            jax.ShapeDtypeStruct((requests, LINES, width), jnp.float32),
            jax.ShapeDtypeStruct(packed.shape, packed.dtype),
        ]
        operands += [early_sums, peak]
    return pl.pallas_call(
        functools.partial(attend_kernel, per_kv, tok_rows, late, early, later),
        out_shape=tuple(out_shape),
        in_specs=[vmem] * len(operands),
        out_specs=(vmem,) * len(out_shape),
        scratch_shapes=[
            pltpu.SMEM(packed.shape, packed.dtype),
            pltpu.VMEM((requests, kv_count, LINES, width), jnp.float32),
            pltpu.VMEM((requests, kv_count, HEAD_DIM + EXTRA, width), jnp.float32),
            pltpu.SemaphoreType.DMA(()),
        ],
        compiler_params=pltpu.CompilerParams(vmem_limit_bytes=28 << 20),
        cost_estimate=pl.CostEstimate(
            flops=4 * pages * PAGE_ROWS * ADDED_TOKENS * q_rows * kv_count,
            bytes_accessed=4 * pages * PAGE_ROWS * kv_cols,
            transcendentals=pages * PAGE_ROWS * ADDED_TOKENS * per_kv * kv_count,
        ),
    )(*operands)


def page_lists(lengths_ref, groups_ref, prompt_ref, own_ref, packed_ref, pages_dev, me):
    count = PROMPT_PAGES + own_ref.shape[1]
    position = lax.broadcasted_iota(jnp.int32, (1, count), 1)
    owned, pages, lives = [], [], []
    for request in range(REQUESTS):
        prompt = prompt_ref[0:1, :]
        for group in range(1, GROUPS):
            prompt = jnp.where(groups_ref[request] == group, prompt_ref[group : group + 1, :], prompt)
        slots = jnp.concatenate([prompt, own_ref[request : request + 1, :]], axis=1)
        own_len = lengths_ref[request] - PROMPT_PAGES * PAGE_ROWS
        live = jnp.clip(own_len - (position - PROMPT_PAGES) * PAGE_ROWS, 0, PAGE_ROWS)
        live = jnp.where(position < PROMPT_PAGES, PAGE_ROWS, live)
        page = slots - me * pages_dev
        owned.append((page >= 0) & (page < pages_dev) & (live > 0))
        pages.append(page)
        lives.append(live)
    earlier = lax.broadcasted_iota(jnp.int32, (count, count), 0)
    earlier = earlier < lax.broadcasted_iota(jnp.int32, (count, count), 1)
    earlier = jnp.where(earlier, 1.0, 0.0).astype(jnp.bfloat16)
    place = lax.broadcasted_iota(jnp.int32, (PAGE_ROWS, count), 0).astype(jnp.float32)
    packed_ref[...] = jnp.zeros_like(packed_ref)
    for request in range(REQUESTS):
        mark = jnp.where(owned[request], 1.0, 0.0)
        marks = jnp.broadcast_to(mark, (EXTRA, count)).astype(jnp.bfloat16)
        before = jnp.dot(marks, earlier, preferred_element_type=jnp.float32)[0:1]
        before = jnp.where(owned[request], before, -1.0)
        onehot = jnp.where(before == place, 1.0, 0.0).astype(jnp.bfloat16)

        def pick(line):
            line = jnp.where(owned[request], line, 0).astype(jnp.float32)
            lines = jnp.broadcast_to(line, (EXTRA, count)).astype(jnp.bfloat16)
            return dot_nt(lines, onehot)[0:1]

        packed = pick(pages[request]) * 256.0 + pick(lives[request])
        packed_ref[request : request + 1, :] = packed.astype(jnp.int32)
        total = jnp.sum(mark, axis=1, keepdims=True)
        packed_ref[REQUESTS + request : REQUESTS + request + 1, :] = jnp.broadcast_to(
            total, (1, PAGE_ROWS)
        ).astype(jnp.int32)


def greet(peers):
    barrier = pltpu.get_barrier_semaphore()
    for peer in peers:
        pl.semaphore_signal(barrier, inc=1, device_id=peer, device_id_type=MESH)


def greeted(count):
    pl.semaphore_wait(pltpu.get_barrier_semaphore(), count)


def remote(source, target, send_sem, recv_sem, peer):
    return pltpu.make_async_remote_copy(
        src_ref=source,
        dst_ref=target,
        send_sem=send_sem,
        recv_sem=recv_sem,
        device_id=peer,
        device_id_type=MESH,
    )


def spread_columns(w_hbm, start, target, tensor_count, send_sem, recv_sem):
    me = lax.axis_index("seq")
    tensor = lax.axis_index("tensor")
    rows, columns = target.shape[1:]

    def block(owner):
        first = pl.multiple_of(owner * columns, columns)
        return w_hbm.at[pl.ds(start, rows), pl.ds(first, columns)]

    copies = [pltpu.make_async_copy(block(tensor), target.at[tensor], send_sem.at[0])]
    for distance in range(1, tensor_count):
        owner = (tensor + distance) % tensor_count
        copies.append(
            remote(
                block(owner),
                target.at[tensor],
                send_sem.at[distance],
                recv_sem.at[distance],
                (me, owner),
            )
        )
    return copies


def gather_kernel(seq_count, early, *refs):
    refs = list(refs)
    x_ref, gain_hbm, wq_ref, wk_ref, wv_ref, kc_hbm, vc_hbm, w_hbm = refs[:8]
    small_hbm = refs[8:12]
    qt_ref, fk_ref, fv_ref, packed_ref, kc_ref, vc_ref, w_cols = refs[12:19]
    del refs[:19]
    if early:
        sums_ref, peak_ref = refs[:2]
        del refs[:2]
    q_send, q_recv, qy_send, qy_recv, wq_buf, wk_buf, wv_buf, x_buf = refs[:8]
    load_sem, lists, gain_ref, lengths_ref, groups_ref, prompt_ref, own_ref = refs[8:15]
    w_send, w_recv = refs[15:]
    loads = [
        pltpu.make_async_copy(source, target, load_sem.at[index])
        for index, (source, target) in enumerate(
            (
                (x_ref, x_buf),
                (wk_ref, wk_buf),
                (wq_ref, wq_buf),
                (wv_ref, wv_buf),
                (kc_hbm, kc_ref),
                (vc_hbm, vc_ref),
                (packed_ref, lists),
                (gain_hbm, gain_ref),
                (small_hbm[0], lengths_ref),
                (small_hbm[1], groups_ref),
                (small_hbm[2], prompt_ref),
                (small_hbm[3], own_ref),
            )
        )
    ]
    small = loads[7:]
    for load in loads[:1] + small + loads[1:4]:
        load.start()
    me = lax.axis_index("seq")
    tensor = lax.axis_index("tensor")
    tensor_count = w_cols.shape[0]
    outer = seq_count // 2
    place, side = me // 2, me % 2
    twin = (place * 2 + 1 - side, tensor)
    kv_count = qt_ref.shape[1]
    per_kv = (qt_ref.shape[2] - EXTRA) // HEAD_DIM
    order = sorted(range(1, outer), key=lambda distance: -min(distance, outer - distance))

    def line_peer(distance):
        return (place + distance) % outer * 2 + side

    others = [(me, (tensor + distance) % tensor_count) for distance in range(1, tensor_count)]
    greet([twin] + [(line_peer(distance), tensor) for distance in range(1, outer)] + others)

    loads[0].wait()
    small[0].wait()
    floats = x_buf[...].astype(jnp.float32)
    mean = jnp.mean(floats * floats, axis=-1, keepdims=True)
    normed = (floats * lax.rsqrt(mean + 1e-05) * gain_ref[...]).astype(jnp.bfloat16)

    def project(weight):
        return jnp.dot(normed, weight, preferred_element_type=jnp.float32)

    loads[1].wait()
    keys = project(wk_buf[...])
    fk_ref[...] = keys.astype(jnp.bfloat16)
    keys_t = keys.T.astype(jnp.bfloat16)
    loads[2].wait()
    started = []

    def make(kv):
        span = per_kv * HEAD_DIM
        queries_t = project(wq_buf[:, kv * span : (kv + 1) * span]).T.astype(jnp.bfloat16)
        qt_ref[me, kv, :span, :] = queries_t
        right = keys_t[cols(kv)].astype(jnp.float32)
        marks = [
            jnp.sum(queries_t[cols(sub)].astype(jnp.float32) * right, axis=0, keepdims=True)
            for sub in range(per_kv)
        ]
        marks.append(jnp.zeros((EXTRA - per_kv, marks[0].shape[1]), jnp.float32))
        qt_ref[me, kv, span:, :] = jnp.concatenate(marks, axis=0).astype(jnp.bfloat16)

    def launch(kv):
        own = qt_ref.at[me, kv]
        copy = remote(own, own, qy_send.at[kv, 0], qy_recv.at[kv, 0], twin)
        copy.start()
        started.append(copy)
        for distance in order:
            peer = (line_peer(distance), tensor)
            copy = remote(own, own, q_send.at[kv, distance], q_recv.at[kv, distance], peer)
            copy.start()
            started.append(copy)

    def relay(kv, distance):
        block = qt_ref.at[line_peer(outer - distance), kv]
        remote(block, block, q_send.at[kv, distance], q_recv.at[kv, distance], twin).wait_recv()
        copy = remote(block, block, qy_send.at[kv, distance], qy_recv.at[kv, distance], twin)
        copy.start()
        started.append(copy)

    def arrive(kv):
        for distance in [0] + order:
            block = qt_ref.at[(place + outer - distance) % outer * 2 + 1 - side, kv]
            remote(block, block, qy_send.at[kv, distance], qy_recv.at[kv, distance], twin).wait_recv()

    make(0)
    greeted(outer + tensor_count - 1)
    launch(0)
    for load in loads[4:6]:
        load.start()
    spread = spread_columns(w_hbm, 0, w_cols, tensor_count, w_send, w_recv)
    for copy in spread:
        copy.start()
    for kv in range(1, kv_count):
        make(kv)
    loads[3].wait()
    fv_ref[...] = project(wv_buf[...]).astype(jnp.bfloat16)
    for load in small[1:]:
        load.wait()
    page_lists(lengths_ref, groups_ref, prompt_ref, own_ref, packed_ref, kc_ref.shape[0], me)
    for distance in order[: len(order) // 2 + 1]:
        relay(0, distance)
    for kv in range(1, kv_count):
        launch(kv)
    for distance in order[len(order) // 2 + 1 :]:
        relay(0, distance)
    loads[6].start()
    for load in loads[4:7]:
        load.wait()
    waiting = [(kv, distance) for kv in range(1, kv_count) for distance in order]
    if early:
        peak = jnp.zeros((PAGE_ROWS, 1), jnp.float32)
        for page in range(kc_ref.shape[0]):
            floats = kc_ref[page, :, cols(kv_count - 1)].astype(jnp.float32)
            peak = jnp.maximum(peak, jnp.sum(floats * floats, axis=1, keepdims=True))
        peak_ref[...] = jnp.broadcast_to(peak, peak_ref.shape)
        arrive(0)
        marks = [joined_marks(qt_ref, request, 0, per_kv) for request in range(REQUESTS)]
        for step in range(early // STEP_PAGES):
            for request in range(REQUESTS):
                fresh = early_terms(
                    lists, qt_ref, kc_ref, vc_ref, marks[request], request, step, 0, per_kv
                )
                if step == 0:
                    sums_ref[request] = fresh
                else:
                    sums_ref[request] += fresh
                if waiting:
                    relay(*waiting.pop(0))
    else:
        arrive(0)
    for kv, distance in waiting:
        relay(kv, distance)
    for kv in range(1, kv_count):
        arrive(kv)
    for copy in spread:
        copy.wait()
    for copy in started:
        copy.wait_send()


def gather(
    hidden_in,
    norm_gain,
    query_weight,
    key_weight,
    value_weight,
    key_cache,
    value_cache,
    cached_lengths,
    group_ids,
    prompt_pages,
    own_pages,
    out_weight,
    seq_count,
    tensor_count,
    early,
):
    tok_rows = hidden_in.shape[0]
    q_cols, kv_cols = query_weight.shape[1], key_weight.shape[1]
    kv_count = kv_cols // HEAD_DIM
    per_kv = q_cols // kv_cols
    slots = pltpu.SemaphoreType.DMA((kv_count, seq_count // 2))
    vmem = pl.BlockSpec(memory_space=pltpu.VMEM)
    hbm = pl.BlockSpec(memory_space=pltpu.HBM)
    fresh = jax.ShapeDtypeStruct((tok_rows, kv_cols), jnp.bfloat16)
    rows = per_kv * HEAD_DIM + EXTRA
    out_shape = [
        jax.ShapeDtypeStruct((seq_count, kv_count, rows, tok_rows), jnp.bfloat16),
        fresh,
        fresh,
        jax.ShapeDtypeStruct((LINES, PAGE_ROWS), jnp.int32),
        jax.ShapeDtypeStruct(key_cache.shape, key_cache.dtype),
        jax.ShapeDtypeStruct(value_cache.shape, value_cache.dtype),
        jax.ShapeDtypeStruct(
            (tensor_count, per_kv * HEAD_DIM, out_weight.shape[1] // tensor_count), jnp.bfloat16
        ),
    ]
    if early:
        sums = (REQUESTS, HEAD_DIM + EXTRA, per_kv * ADDED_TOKENS)
        out_shape += [
            jax.ShapeDtypeStruct(sums, jnp.float32),
            jax.ShapeDtypeStruct((PAGE_ROWS, HEAD_DIM), jnp.float32),
        ]
    return pl.pallas_call(
        functools.partial(gather_kernel, seq_count, early),
        out_shape=tuple(out_shape),
        in_specs=[hbm] * 12,
        out_specs=(vmem,) * len(out_shape),
        scratch_shapes=[slots] * 4
        + [
            pltpu.VMEM(weight.shape, weight.dtype)
            for weight in (query_weight, key_weight, value_weight, hidden_in)
        ]
        + [
            pltpu.SemaphoreType.DMA((12,)),
            pltpu.SMEM((LINES, PAGE_ROWS), jnp.int32),
            pltpu.VMEM((1, norm_gain.shape[0]), norm_gain.dtype),
            pltpu.SMEM(cached_lengths.shape, jnp.int32),
            pltpu.SMEM(group_ids.shape, jnp.int32),
            pltpu.VMEM(prompt_pages.shape, jnp.int32),
            pltpu.VMEM(own_pages.shape, jnp.int32),
            pltpu.SemaphoreType.DMA((tensor_count,)),
            pltpu.SemaphoreType.DMA((tensor_count,)),
        ],
        compiler_params=pltpu.CompilerParams(
            collective_id=0, has_side_effects=True, vmem_limit_bytes=40 << 20
        ),
    )(
        in_hbm(hidden_in),
        in_hbm(norm_gain.reshape(1, -1)),
        in_hbm(query_weight),
        in_hbm(key_weight),
        in_hbm(value_weight),
        in_hbm(key_cache),
        in_hbm(value_cache),
        in_hbm(out_weight),
        in_hbm(cached_lengths),
        in_hbm(group_ids),
        in_hbm(prompt_pages),
        in_hbm(own_pages),
    )


def finish_kernel(seq_count, tensor_count, kv_count, early, *refs):
    refs = list(refs)
    known = kv_count - 1 if early else kv_count
    part_refs, ls_refs = refs[:known], refs[known : 2 * known]
    del refs[: 2 * known]
    if early:
        left_ref, left_m_ref, packed_ref, qt_ref, kc_ref, vc_ref = refs[:6]
        del refs[:6]
    w_early, w_hbm, out_ref = refs[:3]
    mix_ref, mix_got, mls_ref, side_got, sls_ref, gls_ref = refs[3:9]
    w_late, att_ref = refs[9:11]
    side_send, side_recv, sls_send, sls_recv, mix_send, mix_recv, mls_send, mls_recv = refs[11:19]
    w_send, w_recv, att_send, att_recv = refs[19:23]
    del refs[:23]
    if early:
        late_ref, lists, list_sem = refs[2:]
        part_refs = part_refs + refs[:1]
        ls_refs = ls_refs + refs[1:2]
        fetch = pltpu.make_async_copy(packed_ref, lists, list_sem)
        fetch.start()
    tok_rows, out_cols = out_ref.shape
    per_kv = part_refs[0].shape[1] // HEAD_DIM
    me = lax.axis_index("seq")
    tensor = lax.axis_index("tensor")
    hops = range(1, tensor_count)
    outer = seq_count // 2
    place, side = me // 2, me % 2
    beside = (place * 2 + 1 - side, tensor)
    order = sorted(range(1, outer), key=lambda distance: -min(distance, outer - distance))

    def line(distance, which):
        return (place + distance) % outer * 2 + which

    greet(
        [beside]
        + [(line(distance, side), tensor) for distance in range(1, outer)]
        + [(me, (tensor + distance) % tensor_count) for distance in range(1, tensor_count)]
    )
    greeted(outer + tensor_count - 1)
    started = []
    scales, sides, mixes, mix_scales, shares = {}, {}, {}, {}, {}

    def begin(table, key, *rest):
        table[key] = remote(*rest)
        table[key].start()
        started.append(table[key])

    def send_sides(kv):
        for distance in order + [0]:
            begin(
                scales,
                (kv, distance),
                ls_refs[kv].at[line(distance, 1 - side)],
                sls_ref.at[kv, distance],
                sls_send.at[kv, distance],
                sls_recv.at[kv, distance],
                beside,
            )
        for sub in range(per_kv):
            for distance in order + [0]:
                begin(
                    sides,
                    (kv, sub, distance),
                    part_refs[kv].at[line(distance, 1 - side), cols(sub)],
                    side_got.at[kv, distance, cols(sub)],
                    side_send.at[kv, sub, distance],
                    side_recv.at[kv, sub, distance],
                    beside,
                )

    def weighted(block, share, sub):
        return block.astype(jnp.float32) * share[sub : sub + 1]

    def weigh(kv):
        for distance in order + [0]:
            scales[kv, distance].wait_recv()
        own_lines = jnp.stack([ls_refs[kv][line(distance, side)] for distance in range(outer)])
        side_lines = sls_ref[kv]
        top = jnp.maximum(own_lines, side_lines)
        own_scale, side_scale = jnp.exp(own_lines - top), jnp.exp(side_lines - top)
        both = own_scale + side_scale
        mls_ref[kv] = top + jnp.log(both)
        for distance in order:
            begin(
                mix_scales,
                (kv, distance),
                mls_ref.at[kv, distance],
                gls_ref.at[kv, distance],
                mls_send.at[kv, distance],
                mls_recv.at[kv, distance],
                (line(distance, side), tensor),
            )
        shares[kv] = own_scale / both, side_scale / both

    def mixed(kv, sub, distance):
        sides[kv, sub, distance].wait_recv()
        own_shares, side_shares = shares[kv]
        own = part_refs[kv][line(distance, side), cols(sub), :]
        return weighted(own, own_shares[distance], sub) + weighted(
            side_got[kv, distance, cols(sub), :], side_shares[distance], sub
        )

    def send_mix(kv, sub, distance):
        mix_ref[kv, distance, cols(sub), :] = mixed(kv, sub, distance).astype(jnp.bfloat16)
        begin(
            mixes,
            (kv, sub, distance),
            mix_ref.at[kv, distance, cols(sub)],
            mix_got.at[kv, distance, cols(sub)],
            mix_send.at[kv, sub, distance],
            mix_recv.at[kv, sub, distance],
            (line(distance, side), tensor),
        )

    def owner_shares(kv):
        gls_ref[kv, 0] = mls_ref[kv, 0]
        for distance in order:
            mix_scales[kv, distance].wait_recv()
        lines = gls_ref[kv]
        lines = jnp.exp(lines - jnp.max(lines, axis=0, keepdims=True))
        return lines / jnp.sum(lines, axis=0, keepdims=True)

    def merged(kv, sub, share):
        total = mixed(kv, sub, 0) * share[0][sub : sub + 1]
        for distance in order:
            mixes[kv, sub, distance].wait_recv()
            total = total + weighted(
                mix_got[kv, distance, cols(sub), :], share[distance], sub
            )
        return total.astype(jnp.bfloat16)

    def tensor_copy(kv, sub, distance, source):
        block = att_ref.at[source, kv, cols(sub)]
        return remote(
            block,
            block,
            att_send.at[kv, sub, distance],
            att_recv.at[kv, sub, distance],
            (me, (tensor + distance) % tensor_count),
        )

    def share_out(kv, sub, attention):
        att_ref[tensor, kv, cols(sub), :] = attention
        for distance in range(1, tensor_count):
            copy = tensor_copy(kv, sub, distance, tensor)
            copy.start()
            started.append(copy)

    def terms_of(kv, sub, source):
        first = ((kv - 1) * per_kv + sub) * HEAD_DIM
        if kv == 0:
            weight = w_early[source, cols(sub), :]
        else:
            weight = w_late[source, first : first + HEAD_DIM, :]
        return lax.dot_general(
            att_ref[source, kv, cols(sub), :],
            weight,
            (((0,), (0,)), ((), ())),
            preferred_element_type=jnp.float32,
        )

    def out_terms(kv, sub):
        total = terms_of(kv, sub, tensor)
        for distance in hops:
            source = (tensor + tensor_count - distance) % tensor_count
            tensor_copy(kv, sub, distance, source).wait_recv()
            total = total + terms_of(kv, sub, source)
        return total

    last = kv_count - 1
    for kv in range(known):
        send_sides(kv)
    spread = spread_columns(w_hbm, per_kv * HEAD_DIM, w_late, tensor_count, w_send, w_recv)
    for copy in spread:
        copy.start()
    if early:
        fetch.wait()
        ls_refs[last][...] = jnp.zeros_like(ls_refs[last])
        steps = [
            (step, request)
            for step in range(early // STEP_PAGES)
            for request in range(REQUESTS)
        ]
        tasks = [(weigh, (kv,)) for kv in range(known)]
        tasks += [
            (send_mix, (kv, sub, distance))
            for kv in range(known)
            for sub in range(per_kv)
            for distance in order
        ]
        share_of = -(-len(tasks) // len(steps))
        for step, request in steps:
            late_ref[request] = (left_ref if step == 0 else late_ref)[request] + early_terms(
                lists,
                qt_ref,
                kc_ref,
                vc_ref,
                left_m_ref[request, 0:1, :],
                request,
                step,
                last,
                per_kv,
            )
            for run, given in tasks[:share_of]:
                run(*given)
            del tasks[:share_of]
        for request in range(REQUESTS):
            settle(
                late_ref[request],
                left_m_ref[request, 0:1, :],
                request,
                part_refs[last],
                ls_refs[last],
                per_kv,
            )
        send_sides(last)
        ready = known
    else:
        ready = 0
    for kv in range(ready, kv_count):
        weigh(kv)
        for sub in range(per_kv):
            for distance in order:
                send_mix(kv, sub, distance)
    result = None
    for kv in range(kv_count):
        share = owner_shares(kv)
        for sub in range(per_kv):
            share_out(kv, sub, merged(kv, sub, share))
        if kv == 1:
            for copy in spread:
                copy.wait()
        for sub in range(per_kv):
            fresh = out_terms(kv, sub)
            result = fresh if result is None else result + fresh
    out_ref[...] = result.astype(jnp.bfloat16)
    for copy in started:
        copy.wait_send()


def finish(parts, scales, leftovers, w_cols, out_weight, seq_count, tensor_count, early):
    q_rows, tok_rows = parts[0].shape[1:]
    kv_count = len(parts) + (1 if early else 0)
    out_cols = out_weight.shape[1] // tensor_count
    per_kv = q_rows // HEAD_DIM
    outer = seq_count // 2
    vmem = pl.BlockSpec(memory_space=pltpu.VMEM)
    w_block = (tensor_count, out_weight.shape[0] - w_cols.shape[1], out_cols)
    att_block = (tensor_count, kv_count, q_rows, tok_rows)
    part_buf = pltpu.VMEM((kv_count, outer, q_rows, tok_rows), jnp.bfloat16)
    scale_buf = pltpu.VMEM((kv_count, outer, LINES, tok_rows), jnp.float32)
    line_sems = pltpu.SemaphoreType.DMA((kv_count, outer))
    head_sems = pltpu.SemaphoreType.DMA((kv_count, per_kv, outer))
    att_sems = pltpu.SemaphoreType.DMA((kv_count, per_kv, tensor_count))
    w_sems = pltpu.SemaphoreType.DMA((tensor_count,))
    operands = list(parts) + list(scales) + list(leftovers) + [w_cols, in_hbm(out_weight)]
    scratch = [part_buf, part_buf, scale_buf, part_buf, scale_buf, scale_buf]
    scratch += [pltpu.VMEM(w_block, jnp.bfloat16), pltpu.VMEM(att_block, jnp.bfloat16)]
    scratch += [head_sems] * 2 + [line_sems] * 2 + [head_sems] * 2 + [line_sems] * 2
    scratch += [w_sems] * 2 + [att_sems] * 2
    if early:
        scratch += [
            pltpu.VMEM(parts[0].shape, parts[0].dtype),
            pltpu.VMEM(scales[0].shape, scales[0].dtype),
            pltpu.VMEM(leftovers[0].shape, leftovers[0].dtype),
            pltpu.SMEM(leftovers[2].shape, leftovers[2].dtype),
            pltpu.SemaphoreType.DMA(()),
        ]
    return pl.pallas_call(
        functools.partial(finish_kernel, seq_count, tensor_count, kv_count, early),
        out_shape=jax.ShapeDtypeStruct((tok_rows, out_cols), jnp.bfloat16),
        in_specs=[vmem] * (len(operands) - 1) + [pl.BlockSpec(memory_space=pltpu.HBM)],
        out_specs=vmem,
        scratch_shapes=scratch,
        compiler_params=pltpu.CompilerParams(
            collective_id=1, has_side_effects=True, vmem_limit_bytes=32 << 20
        ),
    )(*operands)


def regroup(array, rows):
    count, width = array.shape[0], array.shape[-1]
    if width == rows:
        return array
    array = jnp.moveaxis(array, 0, -2)
    array = array.reshape(array.shape[:-2] + (count * width // rows, rows))
    return jnp.moveaxis(array, -2, 0)


def body(
    hidden_in,
    norm_gain,
    query_weight,
    key_weight,
    value_weight,
    out_weight,
    key_cache,
    value_cache,
    cached_lengths,
    group_ids,
    prompt_pages,
    own_pages,
):
    tok_rows = hidden_in.shape[0]
    seq_count = lax.axis_size("seq")
    kv_count = key_weight.shape[1] // HEAD_DIM
    split = tok_rows == BLOCK and kv_count > 1
    early = EARLY_STEPS * STEP_PAGES if split else 0
    later = LATE_STEPS * STEP_PAGES if split else 0
    tensor_count = lax.axis_size("tensor")
    queries_t, fresh_k, fresh_v, packed, keys, values, w_cols, *rest = gather(
        hidden_in,
        norm_gain,
        query_weight,
        key_weight,
        value_weight,
        key_cache,
        value_cache,
        cached_lengths,
        group_ids,
        prompt_pages,
        own_pages,
        out_weight,
        seq_count,
        tensor_count,
        early,
    )
    queries_t = regroup(queries_t, BLOCK)
    sums, peak = rest if early else (None, None)
    found = attend(
        packed, queries_t, fresh_k, fresh_v, keys, values, sums, peak, early, later
    )
    known = kv_count - 1 if early else kv_count
    parts = [regroup(array, tok_rows) for array in found[:known]]
    scales = [regroup(array, tok_rows) for array in found[known : 2 * known]]
    leftovers = list(found[2 * known :])
    if early:
        leftovers += [queries_t, keys, values]
    return finish(
        parts, scales, leftovers, w_cols, out_weight, seq_count, tensor_count, later
    )


def solution(mesh):
    in_specs = (
        P("seq", None),
        P(),
        P(None, "tensor"),
        P(None, "tensor"),
        P(None, "tensor"),
        P("tensor", None),
        P("seq", None, "tensor"),
        P("seq", None, "tensor"),
        P(),
        P(),
        P(),
        P(),
    )
    out_specs = P("seq", "tensor")
    return jax.shard_map(body, mesh=mesh, in_specs=in_specs, out_specs=out_specs, check_vma=False)
```

```python
import functools
import math

import jax
import jax.numpy as jnp
from jax import lax
from jax.experimental import pallas as pl
from jax.experimental.pallas import tpu as pltpu
from jax.sharding import PartitionSpec as P

HEAD_DIM = 128
PAGE_ROWS = 128
ADDED_TOKENS = 512
GROUPS = 2
PROMPT_PAGES = 128
STEP_PAGES = 8
TAIL_PAGES = 4
BLOCK = 128
EXTRA = 16
REQUESTS = 2
LIMIT = 1e30
EARLY_STEPS = 3
LATE_STEPS = 2
SAFE_POWER = 100.0
SCORE_SCALE = 1.0 / math.sqrt(HEAD_DIM)
EXP2_SCALE = SCORE_SCALE * math.log2(math.e)
EMPTY = -1e30
SHIFT = 60.0 / EXP2_SCALE
BLOCKS = ADDED_TOKENS // BLOCK
LINES = 8
MESH = pl.DeviceIdType.MESH


def in_hbm(array):
    return pltpu.with_memory_space_constraint(array, pltpu.HBM)


def dot_nt(left, right):
    return lax.dot_general(
        left, right, (((1,), (1,)), ((), ())), preferred_element_type=jnp.float32
    )


def cols(index):
    return slice(index * HEAD_DIM, (index + 1) * HEAD_DIM)


def joined_queries(qt_ref, request, kv, per_kv):
    return jnp.concatenate(
        [
            qt_ref[request * BLOCKS + block, kv, cols(sub), :]
            for sub in range(per_kv)
            for block in range(BLOCKS)
        ],
        axis=1,
    )


def joined_marks(qt_ref, request, kv, per_kv):
    rows = [
        qt_ref[request * BLOCKS + block, kv, per_kv * HEAD_DIM :, :].astype(jnp.float32)[
            sub : sub + 1
        ]
        for sub in range(per_kv)
        for block in range(BLOCKS)
    ]
    return jnp.concatenate(rows, axis=1) + SHIFT


def values_t(values):
    ones = jnp.ones((EXTRA, values.shape[0]), jnp.bfloat16)
    return jnp.concatenate([values.T, ones], axis=0)


def page_group(lists, cache_ref, request, start, pages, kv):
    last = cache_ref.shape[0] - 1
    slots = [jnp.clip(lists[request, start + page] >> 8, 0, last) for page in range(pages)]
    return jnp.concatenate([cache_ref[slot, :, cols(kv)] for slot in slots], axis=0)


def page_bias(lists, request, start, pages):
    place = lax.broadcasted_iota(jnp.int32, (PAGE_ROWS, 1), 0)
    return jnp.concatenate(
        [
            jnp.where(place < (lists[request, start + page] & 255), 0.0, EMPTY)
            for page in range(pages)
        ],
        axis=0,
    )


def terms(queries, mark, keys, values, bias):
    scores = jnp.dot(keys, queries, preferred_element_type=jnp.float32)
    if bias is not None:
        scores = scores + bias
    weights = jnp.exp2((scores - mark) * EXP2_SCALE).astype(jnp.bfloat16)
    return jnp.dot(values_t(values), weights, preferred_element_type=jnp.float32)


def early_terms(lists, qt_ref, kc_ref, vc_ref, mark, request, step, kv, per_kv):
    start = step * STEP_PAGES
    return terms(
        joined_queries(qt_ref, request, kv, per_kv),
        mark,
        page_group(lists, kc_ref, request, start, STEP_PAGES, kv),
        page_group(lists, vc_ref, request, start, STEP_PAGES, kv),
        page_bias(lists, request, start, STEP_PAGES),
    )


def settle(sums, top, request, part_ref, ls_ref, per_kv):
    den = sums[HEAD_DIM : HEAD_DIM + 1]
    alive = (den > 0.0) & (top > 0.5 * EMPTY)
    den = jnp.where(alive, den, 1.0)
    scale = jnp.where(alive, top * SCORE_SCALE + jnp.log(den), EMPTY)
    parts = (sums[:HEAD_DIM] * jnp.where(alive, 1.0 / den, 0.0)).astype(jnp.bfloat16)
    for sub in range(per_kv):
        for block in range(BLOCKS):
            place = sub * BLOCKS + block
            span = slice(place * BLOCK, (place + 1) * BLOCK)
            part_ref[request * BLOCKS + block, cols(sub), :] = parts[:, span]
            ls_ref[request * BLOCKS + block, sub : sub + 1, :] = scale[:, span]


def attend_kernel(per_kv, tok_rows, late, early, later, *refs):
    refs = list(refs)
    packed_ref, qt_ref, fk_ref, fv_ref, kc_ref, vc_ref = refs[:6]
    del refs[:6]
    if late:
        start_ref, peak_ref = refs[:2]
        del refs[:2]
    kv_count = kc_ref.shape[2] // HEAD_DIM
    done_kv = kv_count - 1 if late else kv_count
    part_refs, ls_refs = refs[:done_kv], refs[done_kv : 2 * done_kv]
    del refs[: 2 * done_kv]
    if late:
        left_ref, left_m_ref, left_list_ref = refs[:3]
        del refs[:3]
    lists, m_ref, acc_ref, list_sem = refs
    fetch = pltpu.make_async_copy(packed_ref, lists, list_sem)
    fetch.start()
    requests = acc_ref.shape[0]
    width = per_kv * ADDED_TOKENS
    for ls_ref in ls_refs:
        ls_ref[...] = jnp.zeros_like(ls_ref)
    for kv in range(kv_count):
        for request in range(requests):
            if late and kv == 0:
                acc_ref[request, kv] = start_ref[request]
            else:
                acc_ref[request, kv] = jnp.zeros_like(acc_ref[request, kv])
            m_ref[request, kv, 0:1, :] = joined_marks(qt_ref, request, kv, per_kv)
    if late:
        left_list_ref[...] = packed_ref[...]

    def add(request, kv, keys, values, bias):
        queries = joined_queries(qt_ref, request, kv, per_kv)
        acc_ref[request, kv] += terms(queries, m_ref[request, kv, 0:1, :], keys, values, bias)

    def add_running(request, kv, keys, values, bias):
        queries = joined_queries(qt_ref, request, kv, per_kv)
        scores = jnp.dot(keys, queries, preferred_element_type=jnp.float32) + bias
        old = m_ref[request, kv, 0:1, :]
        new = jnp.maximum(old, jnp.max(scores, axis=0, keepdims=True))
        m_ref[request, kv, 0:1, :] = new
        weights = jnp.exp2((scores - new) * EXP2_SCALE)
        acc_ref[request, kv] = acc_ref[request, kv] * jnp.exp2((old - new) * EXP2_SCALE) + jnp.dot(
            values_t(values), weights.astype(jnp.bfloat16), preferred_element_type=jnp.float32
        )

    first = lax.axis_index("seq") * tok_rows
    home = first // ADDED_TOKENS

    def add_fresh(update):
        row = lax.broadcasted_iota(jnp.int32, (tok_rows, width), 0) + (first - home * ADDED_TOKENS)
        col = lax.broadcasted_iota(jnp.int32, (tok_rows, width), 1) % ADDED_TOKENS
        bias = jnp.where(row <= col, 0.0, EMPTY)
        for kv in range(kv_count):
            update(home, kv, fk_ref[:, cols(kv)], fv_ref[:, cols(kv)], bias)

    def add_pages(update, request, start, pages, masked, kvs=range(kv_count)):
        bias = page_bias(lists, request, start, pages) if masked else None
        for kv in kvs:
            keys = page_group(lists, kc_ref, request, start, pages, kv)
            values = page_group(lists, vc_ref, request, start, pages, kv)
            update(request, kv, keys, values, bias)

    add_fresh(add)
    fetch.wait()

    def attend_request(request, carry):
        total = lists[requests + request, 0]
        count = jnp.maximum(total - early, 0)
        whole = jnp.maximum(count - 1, 0) // STEP_PAGES

        def step(index, carry):
            add_pages(add, request, early + index * STEP_PAGES, STEP_PAGES, False)
            return carry

        for start in range(later, early, STEP_PAGES):

            @pl.when(total > start)
            def _():
                add_pages(add, request, start, STEP_PAGES, True, range(done_kv, kv_count))

        lax.fori_loop(0, whole, step, 0)
        done = whole * STEP_PAGES
        rest = count - done

        @pl.when((rest > 0) & (rest <= TAIL_PAGES))
        def _():
            add_pages(add, request, early + done, TAIL_PAGES, True)

        @pl.when(rest > TAIL_PAGES)
        def _():
            add_pages(add, request, early + done, STEP_PAGES, True)

        safe = [
            acc_ref[request, kv, HEAD_DIM : HEAD_DIM + 1, :] < LIMIT for kv in range(kv_count)
        ]
        if late:
            floats = joined_queries(qt_ref, request, kv_count - 1, per_kv).astype(jnp.float32)
            norms = jnp.sum(floats * floats, axis=0, keepdims=True) * jnp.max(peak_ref[...])
            power = (jnp.sqrt(norms) - m_ref[request, kv_count - 1, 0:1, :]) * EXP2_SCALE
            safe.append(power < SAFE_POWER)
        unsafe = jnp.max(
            jnp.concatenate([jnp.where(flags, 0.0, 1.0) for flags in safe], axis=0)
        )

        @pl.when(unsafe > 0.0)
        def _():
            acc_ref[request] = jnp.zeros_like(acc_ref[request])
            m_ref[request] = jnp.full_like(m_ref[request], EMPTY)

            @pl.when(request == home)
            def _():
                add_fresh(add_running)

            def step(index, carry):
                add_pages(add_running, request, index * TAIL_PAGES, TAIL_PAGES, True)
                return carry

            lax.fori_loop(0, (total + TAIL_PAGES - 1) // TAIL_PAGES, step, 0)
            if late:
                row = lax.broadcasted_iota(jnp.int32, left_list_ref.shape, 0)
                left_list_ref[...] = jnp.where(row == request, 0, left_list_ref[...])

        for kv in range(done_kv):
            settle(
                acc_ref[request, kv],
                m_ref[request, kv, 0:1, :],
                request,
                part_refs[kv],
                ls_refs[kv],
                per_kv,
            )
        if late:
            left_ref[request] = acc_ref[request, done_kv]
            left_m_ref[request] = m_ref[request, done_kv]
        return carry

    lax.fori_loop(0, requests, attend_request, 0)


def attend(
    packed, queries_t, fresh_k, fresh_v, key_cache, value_cache, early_sums, peak, early, later
):
    blocks, kv_count, q_rows, _ = queries_t.shape
    late = early > 0
    done_kv = kv_count - 1 if late else kv_count
    q_rows -= EXTRA
    per_kv = q_rows // HEAD_DIM
    pages, _, kv_cols = key_cache.shape
    tok_rows = fresh_k.shape[0]
    requests = blocks // BLOCKS
    width = per_kv * ADDED_TOKENS
    vmem = pl.BlockSpec(memory_space=pltpu.VMEM)
    out_shape = [jax.ShapeDtypeStruct((blocks, q_rows, BLOCK), jnp.bfloat16)] * done_kv
    out_shape += [jax.ShapeDtypeStruct((blocks, LINES, BLOCK), jnp.float32)] * done_kv
    operands = [packed, queries_t, fresh_k, fresh_v, key_cache, value_cache]
    if late:
        out_shape += [
            jax.ShapeDtypeStruct((requests, HEAD_DIM + EXTRA, width), jnp.float32),
            jax.ShapeDtypeStruct((requests, LINES, width), jnp.float32),
            jax.ShapeDtypeStruct(packed.shape, packed.dtype),
        ]
        operands += [early_sums, peak]
    return pl.pallas_call(
        functools.partial(attend_kernel, per_kv, tok_rows, late, early, later),
        out_shape=tuple(out_shape),
        in_specs=[vmem] * len(operands),
        out_specs=(vmem,) * len(out_shape),
        scratch_shapes=[
            pltpu.SMEM(packed.shape, packed.dtype),
            pltpu.VMEM((requests, kv_count, LINES, width), jnp.float32),
            pltpu.VMEM((requests, kv_count, HEAD_DIM + EXTRA, width), jnp.float32),
            pltpu.SemaphoreType.DMA(()),
        ],
        compiler_params=pltpu.CompilerParams(vmem_limit_bytes=28 << 20),
        cost_estimate=pl.CostEstimate(
            flops=4 * pages * PAGE_ROWS * ADDED_TOKENS * q_rows * kv_count,
            bytes_accessed=4 * pages * PAGE_ROWS * kv_cols,
            transcendentals=pages * PAGE_ROWS * ADDED_TOKENS * per_kv * kv_count,
        ),
    )(*operands)


def page_lists(lengths_ref, groups_ref, prompt_ref, own_ref, packed_ref, pages_dev, me):
    count = PROMPT_PAGES + own_ref.shape[1]
    position = lax.broadcasted_iota(jnp.int32, (1, count), 1)
    owned, pages, lives = [], [], []
    for request in range(REQUESTS):
        prompt = prompt_ref[0:1, :]
        for group in range(1, GROUPS):
            prompt = jnp.where(groups_ref[request] == group, prompt_ref[group : group + 1, :], prompt)
        slots = jnp.concatenate([prompt, own_ref[request : request + 1, :]], axis=1)
        own_len = lengths_ref[request] - PROMPT_PAGES * PAGE_ROWS
        live = jnp.clip(own_len - (position - PROMPT_PAGES) * PAGE_ROWS, 0, PAGE_ROWS)
        live = jnp.where(position < PROMPT_PAGES, PAGE_ROWS, live)
        page = slots - me * pages_dev
        owned.append((page >= 0) & (page < pages_dev) & (live > 0))
        pages.append(page)
        lives.append(live)
    earlier = lax.broadcasted_iota(jnp.int32, (count, count), 0)
    earlier = earlier < lax.broadcasted_iota(jnp.int32, (count, count), 1)
    earlier = jnp.where(earlier, 1.0, 0.0).astype(jnp.bfloat16)
    place = lax.broadcasted_iota(jnp.int32, (PAGE_ROWS, count), 0).astype(jnp.float32)
    packed_ref[...] = jnp.zeros_like(packed_ref)
    for request in range(REQUESTS):
        mark = jnp.where(owned[request], 1.0, 0.0)
        marks = jnp.broadcast_to(mark, (EXTRA, count)).astype(jnp.bfloat16)
        before = jnp.dot(marks, earlier, preferred_element_type=jnp.float32)[0:1]
        before = jnp.where(owned[request], before, -1.0)
        onehot = jnp.where(before == place, 1.0, 0.0).astype(jnp.bfloat16)

        def pick(line):
            line = jnp.where(owned[request], line, 0).astype(jnp.float32)
            lines = jnp.broadcast_to(line, (EXTRA, count)).astype(jnp.bfloat16)
            return dot_nt(lines, onehot)[0:1]

        packed = pick(pages[request]) * 256.0 + pick(lives[request])
        packed_ref[request : request + 1, :] = packed.astype(jnp.int32)
        total = jnp.sum(mark, axis=1, keepdims=True)
        packed_ref[REQUESTS + request : REQUESTS + request + 1, :] = jnp.broadcast_to(
            total, (1, PAGE_ROWS)
        ).astype(jnp.int32)


def greet(peers):
    barrier = pltpu.get_barrier_semaphore()
    for peer in peers:
        pl.semaphore_signal(barrier, inc=1, device_id=peer, device_id_type=MESH)


def greeted(count):
    pl.semaphore_wait(pltpu.get_barrier_semaphore(), count)


def remote(source, target, send_sem, recv_sem, peer):
    return pltpu.make_async_remote_copy(
        src_ref=source,
        dst_ref=target,
        send_sem=send_sem,
        recv_sem=recv_sem,
        device_id=peer,
        device_id_type=MESH,
    )


def spread_columns(w_hbm, start, target, tensor_count, send_sem, recv_sem):
    me = lax.axis_index("seq")
    tensor = lax.axis_index("tensor")
    rows, columns = target.shape[1:]

    def block(owner):
        first = pl.multiple_of(owner * columns, columns)
        return w_hbm.at[pl.ds(start, rows), pl.ds(first, columns)]

    copies = [pltpu.make_async_copy(block(tensor), target.at[tensor], send_sem.at[0])]
    for distance in range(1, tensor_count):
        owner = (tensor + distance) % tensor_count
        copies.append(
            remote(
                block(owner),
                target.at[tensor],
                send_sem.at[distance],
                recv_sem.at[distance],
                (me, owner),
            )
        )
    return copies


def gather_kernel(seq_count, early, *refs):
    refs = list(refs)
    x_ref, gain_hbm, wq_ref, wk_ref, wv_ref, kc_hbm, vc_hbm, w_hbm = refs[:8]
    small_hbm = refs[8:12]
    qt_ref, fk_ref, fv_ref, packed_ref, kc_ref, vc_ref, w_cols = refs[12:19]
    del refs[:19]
    if early:
        sums_ref, peak_ref = refs[:2]
        del refs[:2]
    q_send, q_recv, qy_send, qy_recv, wq_buf, wk_buf, wv_buf, x_buf = refs[:8]
    load_sem, lists, gain_ref, lengths_ref, groups_ref, prompt_ref, own_ref = refs[8:15]
    w_send, w_recv = refs[15:]
    loads = [
        pltpu.make_async_copy(source, target, load_sem.at[index])
        for index, (source, target) in enumerate(
            (
                (x_ref, x_buf),
                (wk_ref, wk_buf),
                (wq_ref, wq_buf),
                (wv_ref, wv_buf),
                (kc_hbm, kc_ref),
                (vc_hbm, vc_ref),
                (packed_ref, lists),
                (gain_hbm, gain_ref),
                (small_hbm[0], lengths_ref),
                (small_hbm[1], groups_ref),
                (small_hbm[2], prompt_ref),
                (small_hbm[3], own_ref),
            )
        )
    ]
    small = loads[7:]
    for load in loads[:1] + small + loads[1:4]:
        load.start()
    me = lax.axis_index("seq")
    tensor = lax.axis_index("tensor")
    tensor_count = w_cols.shape[0]
    outer = seq_count // 2
    place, side = me // 2, me % 2
    twin = (place * 2 + 1 - side, tensor)
    kv_count = qt_ref.shape[1]
    per_kv = (qt_ref.shape[2] - EXTRA) // HEAD_DIM
    order = sorted(range(1, outer), key=lambda distance: -min(distance, outer - distance))

    def line_peer(distance):
        return (place + distance) % outer * 2 + side

    others = [(me, (tensor + distance) % tensor_count) for distance in range(1, tensor_count)]
    greet([twin] + [(line_peer(distance), tensor) for distance in range(1, outer)] + others)

    loads[0].wait()
    small[0].wait()
    floats = x_buf[...].astype(jnp.float32)
    mean = jnp.mean(floats * floats, axis=-1, keepdims=True)
    normed = (floats * lax.rsqrt(mean + 1e-05) * gain_ref[...]).astype(jnp.bfloat16)

    def project(weight):
        return jnp.dot(normed, weight, preferred_element_type=jnp.float32)

    loads[1].wait()
    keys = project(wk_buf[...])
    fk_ref[...] = keys.astype(jnp.bfloat16)
    keys_t = keys.T.astype(jnp.bfloat16)
    loads[2].wait()
    started = []

    def make(kv):
        span = per_kv * HEAD_DIM
        queries_t = project(wq_buf[:, kv * span : (kv + 1) * span]).T.astype(jnp.bfloat16)
        qt_ref[me, kv, :span, :] = queries_t
        right = keys_t[cols(kv)].astype(jnp.float32)
        marks = [
            jnp.sum(queries_t[cols(sub)].astype(jnp.float32) * right, axis=0, keepdims=True)
            for sub in range(per_kv)
        ]
        marks.append(jnp.zeros((EXTRA - per_kv, marks[0].shape[1]), jnp.float32))
        qt_ref[me, kv, span:, :] = jnp.concatenate(marks, axis=0).astype(jnp.bfloat16)

    def launch(kv):
        own = qt_ref.at[me, kv]
        copy = remote(own, own, qy_send.at[kv, 0], qy_recv.at[kv, 0], twin)
        copy.start()
        started.append(copy)
        for distance in order:
            peer = (line_peer(distance), tensor)
            copy = remote(own, own, q_send.at[kv, distance], q_recv.at[kv, distance], peer)
            copy.start()
            started.append(copy)

    def relay(kv, distance):
        block = qt_ref.at[line_peer(outer - distance), kv]
        remote(block, block, q_send.at[kv, distance], q_recv.at[kv, distance], twin).wait_recv()
        copy = remote(block, block, qy_send.at[kv, distance], qy_recv.at[kv, distance], twin)
        copy.start()
        started.append(copy)

    def arrive(kv):
        for distance in [0] + order:
            block = qt_ref.at[(place + outer - distance) % outer * 2 + 1 - side, kv]
            remote(block, block, qy_send.at[kv, distance], qy_recv.at[kv, distance], twin).wait_recv()

    make(0)
    greeted(outer + tensor_count - 1)
    launch(0)
    for load in loads[4:6]:
        load.start()
    spread = spread_columns(w_hbm, 0, w_cols, tensor_count, w_send, w_recv)
    for copy in spread:
        copy.start()
    for kv in range(1, kv_count):
        make(kv)
    loads[3].wait()
    fv_ref[...] = project(wv_buf[...]).astype(jnp.bfloat16)
    for load in small[1:]:
        load.wait()
    page_lists(lengths_ref, groups_ref, prompt_ref, own_ref, packed_ref, kc_ref.shape[0], me)
    for distance in order:
        relay(0, distance)
    for kv in range(1, kv_count):
        launch(kv)
    loads[6].start()
    for load in loads[4:7]:
        load.wait()
    waiting = [(kv, distance) for kv in range(1, kv_count) for distance in order]
    if early:
        peak = jnp.zeros((PAGE_ROWS, 1), jnp.float32)
        for page in range(kc_ref.shape[0]):
            floats = kc_ref[page, :, cols(kv_count - 1)].astype(jnp.float32)
            peak = jnp.maximum(peak, jnp.sum(floats * floats, axis=1, keepdims=True))
        peak_ref[...] = jnp.broadcast_to(peak, peak_ref.shape)
        arrive(0)
        marks = [joined_marks(qt_ref, request, 0, per_kv) for request in range(REQUESTS)]
        for step in range(early // STEP_PAGES):
            for request in range(REQUESTS):
                fresh = early_terms(
                    lists, qt_ref, kc_ref, vc_ref, marks[request], request, step, 0, per_kv
                )
                if step == 0:
                    sums_ref[request] = fresh
                else:
                    sums_ref[request] += fresh
                if waiting:
                    relay(*waiting.pop(0))
    else:
        arrive(0)
    for kv, distance in waiting:
        relay(kv, distance)
    for kv in range(1, kv_count):
        arrive(kv)
    for copy in spread:
        copy.wait()
    for copy in started:
        copy.wait_send()


def gather(
    hidden_in,
    norm_gain,
    query_weight,
    key_weight,
    value_weight,
    key_cache,
    value_cache,
    cached_lengths,
    group_ids,
    prompt_pages,
    own_pages,
    out_weight,
    seq_count,
    tensor_count,
    early,
):
    tok_rows = hidden_in.shape[0]
    q_cols, kv_cols = query_weight.shape[1], key_weight.shape[1]
    kv_count = kv_cols // HEAD_DIM
    per_kv = q_cols // kv_cols
    slots = pltpu.SemaphoreType.DMA((kv_count, seq_count // 2))
    vmem = pl.BlockSpec(memory_space=pltpu.VMEM)
    hbm = pl.BlockSpec(memory_space=pltpu.HBM)
    fresh = jax.ShapeDtypeStruct((tok_rows, kv_cols), jnp.bfloat16)
    rows = per_kv * HEAD_DIM + EXTRA
    out_shape = [
        jax.ShapeDtypeStruct((seq_count, kv_count, rows, tok_rows), jnp.bfloat16),
        fresh,
        fresh,
        jax.ShapeDtypeStruct((LINES, PAGE_ROWS), jnp.int32),
        jax.ShapeDtypeStruct(key_cache.shape, key_cache.dtype),
        jax.ShapeDtypeStruct(value_cache.shape, value_cache.dtype),
        jax.ShapeDtypeStruct(
            (tensor_count, per_kv * HEAD_DIM, out_weight.shape[1] // tensor_count), jnp.bfloat16
        ),
    ]
    if early:
        sums = (REQUESTS, HEAD_DIM + EXTRA, per_kv * ADDED_TOKENS)
        out_shape += [
            jax.ShapeDtypeStruct(sums, jnp.float32),
            jax.ShapeDtypeStruct((PAGE_ROWS, HEAD_DIM), jnp.float32),
        ]
    return pl.pallas_call(
        functools.partial(gather_kernel, seq_count, early),
        out_shape=tuple(out_shape),
        in_specs=[hbm] * 12,
        out_specs=(vmem,) * len(out_shape),
        scratch_shapes=[slots] * 4
        + [
            pltpu.VMEM(weight.shape, weight.dtype)
            for weight in (query_weight, key_weight, value_weight, hidden_in)
        ]
        + [
            pltpu.SemaphoreType.DMA((12,)),
            pltpu.SMEM((LINES, PAGE_ROWS), jnp.int32),
            pltpu.VMEM((1, norm_gain.shape[0]), norm_gain.dtype),
            pltpu.SMEM(cached_lengths.shape, jnp.int32),
            pltpu.SMEM(group_ids.shape, jnp.int32),
            pltpu.VMEM(prompt_pages.shape, jnp.int32),
            pltpu.VMEM(own_pages.shape, jnp.int32),
            pltpu.SemaphoreType.DMA((tensor_count,)),
            pltpu.SemaphoreType.DMA((tensor_count,)),
        ],
        compiler_params=pltpu.CompilerParams(
            collective_id=0, has_side_effects=True, vmem_limit_bytes=40 << 20
        ),
    )(
        in_hbm(hidden_in),
        in_hbm(norm_gain.reshape(1, -1)),
        in_hbm(query_weight),
        in_hbm(key_weight),
        in_hbm(value_weight),
        in_hbm(key_cache),
        in_hbm(value_cache),
        in_hbm(out_weight),
        in_hbm(cached_lengths),
        in_hbm(group_ids),
        in_hbm(prompt_pages),
        in_hbm(own_pages),
    )


def finish_kernel(seq_count, tensor_count, kv_count, early, *refs):
    refs = list(refs)
    known = kv_count - 1 if early else kv_count
    part_refs, ls_refs = refs[:known], refs[known : 2 * known]
    del refs[: 2 * known]
    if early:
        left_ref, left_m_ref, packed_ref, qt_ref, kc_ref, vc_ref = refs[:6]
        del refs[:6]
    w_early, w_hbm, out_ref = refs[:3]
    mix_ref, mix_got, mls_ref, side_got, sls_ref, gls_ref = refs[3:9]
    w_late, att_ref = refs[9:11]
    side_send, side_recv, sls_send, sls_recv, mix_send, mix_recv, mls_send, mls_recv = refs[11:19]
    w_send, w_recv, far_send, far_recv, near_send, near_recv = refs[19:25]
    del refs[:25]
    if early:
        late_ref, lists, list_sem = refs[2:]
        part_refs = part_refs + refs[:1]
        ls_refs = ls_refs + refs[1:2]
        fetch = pltpu.make_async_copy(packed_ref, lists, list_sem)
        fetch.start()
    tok_rows, out_cols = out_ref.shape
    per_kv = part_refs[0].shape[1] // HEAD_DIM
    me = lax.axis_index("seq")
    tensor = lax.axis_index("tensor")
    pair, core = tensor // 2, tensor % 2
    pairs = tensor_count // 2
    twin = (me, pair * 2 + 1 - core)
    outer = seq_count // 2
    place, side = me // 2, me % 2
    beside = (place * 2 + 1 - side, tensor)
    order = sorted(range(1, outer), key=lambda distance: -min(distance, outer - distance))

    def far_pair(distance):
        return (pair + distance) % pairs

    def line(distance, which):
        return (place + distance) % outer * 2 + which

    greet(
        [beside]
        + [(line(distance, side), tensor) for distance in range(1, outer)]
        + [twin]
        + [(me, far_pair(distance) * 2 + core) for distance in range(1, pairs)]
        + [(me, far_pair(distance) * 2 + 1 - core) for distance in range(1, pairs)]
    )
    greeted(outer + tensor_count - 1)
    started = []
    scales, sides, mixes, mix_scales, shares = {}, {}, {}, {}, {}

    def begin(table, key, *rest):
        table[key] = remote(*rest)
        table[key].start()
        started.append(table[key])

    def send_sides(kv):
        for distance in order + [0]:
            begin(
                scales,
                (kv, distance),
                ls_refs[kv].at[line(distance, 1 - side)],
                sls_ref.at[kv, distance],
                sls_send.at[kv, distance],
                sls_recv.at[kv, distance],
                beside,
            )
        for distance in order + [0]:
            begin(
                sides,
                (kv, distance),
                part_refs[kv].at[line(distance, 1 - side)],
                side_got.at[kv, distance],
                side_send.at[kv, distance],
                side_recv.at[kv, distance],
                beside,
            )

    def weighted(block, share):
        return [
            block[cols(sub)].astype(jnp.float32) * share[sub : sub + 1] for sub in range(per_kv)
        ]

    def plus(left, right):
        return [one + other for one, other in zip(left, right)]

    def weigh(kv):
        for distance in order + [0]:
            scales[kv, distance].wait_recv()
        own_lines = jnp.stack([ls_refs[kv][line(distance, side)] for distance in range(outer)])
        side_lines = sls_ref[kv]
        top = jnp.maximum(own_lines, side_lines)
        own_scale, side_scale = jnp.exp(own_lines - top), jnp.exp(side_lines - top)
        both = own_scale + side_scale
        mls_ref[kv] = top + jnp.log(both)
        for distance in order:
            begin(
                mix_scales,
                (kv, distance),
                mls_ref.at[kv, distance],
                gls_ref.at[kv, distance],
                mls_send.at[kv, distance],
                mls_recv.at[kv, distance],
                (line(distance, side), tensor),
            )
        shares[kv] = own_scale / both, side_scale / both

    def mixed(kv, distance):
        sides[kv, distance].wait_recv()
        own_shares, side_shares = shares[kv]
        return plus(
            weighted(part_refs[kv][line(distance, side)], own_shares[distance]),
            weighted(side_got[kv, distance], side_shares[distance]),
        )

    def send_mix(kv, distance):
        mix_ref[kv, distance] = jnp.concatenate(mixed(kv, distance), axis=0).astype(jnp.bfloat16)
        begin(
            mixes,
            (kv, distance),
            mix_ref.at[kv, distance],
            mix_got.at[kv, distance],
            mix_send.at[kv, distance],
            mix_recv.at[kv, distance],
            (line(distance, side), tensor),
        )

    def merged(kv):
        gls_ref[kv, 0] = mls_ref[kv, 0]
        for distance in order:
            mix_scales[kv, distance].wait_recv()
        lines = gls_ref[kv]
        lines = jnp.exp(lines - jnp.max(lines, axis=0, keepdims=True))
        share = lines / jnp.sum(lines, axis=0, keepdims=True)
        total = [block * share[0][sub : sub + 1] for sub, block in enumerate(mixed(kv, 0))]
        for distance in order:
            mixes[kv, distance].wait_recv()
            total = plus(total, weighted(mix_got[kv, distance], share[distance]))
        return jnp.concatenate(total, axis=0).astype(jnp.bfloat16)

    def twin_copy(kv, distance, which):
        block = att_ref.at[(pair + pairs - distance) % pairs * 2 + which, kv]
        return remote(block, block, near_send.at[kv, distance], near_recv.at[kv, distance], twin)

    def far_copy(kv, distance, source, target):
        block = att_ref.at[source, kv]
        return remote(
            block, block, far_send.at[kv, distance], far_recv.at[kv, distance], (me, target)
        )

    def share_out(kv, attention):
        att_ref[tensor, kv] = attention
        copies = [
            far_copy(kv, distance, tensor, far_pair(distance) * 2 + core)
            for distance in range(1, pairs)
        ]
        copies.append(twin_copy(kv, 0, core))
        for copy in copies:
            copy.start()
            started.append(copy)

    def pass_on(kv):
        for distance in range(1, pairs):
            source = far_pair(pairs - distance) * 2 + core
            far_copy(kv, distance, source, source).wait_recv()
            copy = twin_copy(kv, distance, core)
            copy.start()
            started.append(copy)

    def terms_of(kv, source):
        rest = (kv - 1) * per_kv * HEAD_DIM
        if kv == 0:
            weight = w_early[source]
        else:
            weight = w_late[source, rest : rest + per_kv * HEAD_DIM, :]
        return lax.dot_general(
            att_ref[source, kv],
            weight,
            (((0,), (0,)), ((), ())),
            preferred_element_type=jnp.float32,
        )

    def near_terms(kv):
        total = terms_of(kv, tensor)
        for distance in range(1, pairs):
            total = total + terms_of(kv, far_pair(distance) * 2 + core)
        return total

    def twin_terms(kv):
        total = None
        for distance in range(pairs):
            twin_copy(kv, distance, 1 - core).wait_recv()
            fresh = terms_of(kv, (pair + pairs - distance) % pairs * 2 + 1 - core)
            total = fresh if total is None else total + fresh
        return total

    last = kv_count - 1
    for kv in range(known):
        send_sides(kv)
    spread = spread_columns(w_hbm, per_kv * HEAD_DIM, w_late, tensor_count, w_send, w_recv)
    for copy in spread:
        copy.start()
    if early:
        fetch.wait()
        ls_refs[last][...] = jnp.zeros_like(ls_refs[last])
        steps = [
            (step, request)
            for step in range(early // STEP_PAGES)
            for request in range(REQUESTS)
        ]
        tasks = [(weigh, (kv,)) for kv in range(known)]
        tasks += [(send_mix, (kv, distance)) for kv in range(known) for distance in order]
        share_of = -(-len(tasks) // len(steps))
        for step, request in steps:
            late_ref[request] = (left_ref if step == 0 else late_ref)[request] + early_terms(
                lists,
                qt_ref,
                kc_ref,
                vc_ref,
                left_m_ref[request, 0:1, :],
                request,
                step,
                last,
                per_kv,
            )
            for run, given in tasks[:share_of]:
                run(*given)
            del tasks[:share_of]
        for request in range(REQUESTS):
            settle(
                late_ref[request],
                left_m_ref[request, 0:1, :],
                request,
                part_refs[last],
                ls_refs[last],
                per_kv,
            )
        send_sides(last)
        ready = known
    else:
        ready = 0
    for kv in range(ready, kv_count):
        weigh(kv)
        for distance in order:
            send_mix(kv, distance)
    result = None
    for kv in range(kv_count):
        share_out(kv, merged(kv))
        if kv == 1:
            for copy in spread:
                copy.wait()
        pass_on(kv)
        fresh = near_terms(kv) + twin_terms(kv)
        result = fresh if result is None else result + fresh
    out_ref[...] = result.astype(jnp.bfloat16)
    for copy in started:
        copy.wait_send()


def finish(parts, scales, leftovers, w_cols, out_weight, seq_count, tensor_count, early):
    q_rows, tok_rows = parts[0].shape[1:]
    kv_count = len(parts) + (1 if early else 0)
    out_cols = out_weight.shape[1] // tensor_count
    pairs = tensor_count // 2
    outer = seq_count // 2
    vmem = pl.BlockSpec(memory_space=pltpu.VMEM)
    w_block = (tensor_count, out_weight.shape[0] - w_cols.shape[1], out_cols)
    att_block = (tensor_count, kv_count, q_rows, tok_rows)
    part_buf = pltpu.VMEM((kv_count, outer, q_rows, tok_rows), jnp.bfloat16)
    scale_buf = pltpu.VMEM((kv_count, outer, LINES, tok_rows), jnp.float32)
    line_sems = pltpu.SemaphoreType.DMA((kv_count, outer))
    pair_sems = pltpu.SemaphoreType.DMA((kv_count, pairs))
    w_sems = pltpu.SemaphoreType.DMA((tensor_count,))
    operands = list(parts) + list(scales) + list(leftovers) + [w_cols, in_hbm(out_weight)]
    scratch = [part_buf, part_buf, scale_buf, part_buf, scale_buf, scale_buf]
    scratch += [pltpu.VMEM(w_block, jnp.bfloat16), pltpu.VMEM(att_block, jnp.bfloat16)]
    scratch += [line_sems] * 8 + [w_sems] * 2 + [pair_sems] * 4
    if early:
        scratch += [
            pltpu.VMEM(parts[0].shape, parts[0].dtype),
            pltpu.VMEM(scales[0].shape, scales[0].dtype),
            pltpu.VMEM(leftovers[0].shape, leftovers[0].dtype),
            pltpu.SMEM(leftovers[2].shape, leftovers[2].dtype),
            pltpu.SemaphoreType.DMA(()),
        ]
    return pl.pallas_call(
        functools.partial(finish_kernel, seq_count, tensor_count, kv_count, early),
        out_shape=jax.ShapeDtypeStruct((tok_rows, out_cols), jnp.bfloat16),
        in_specs=[vmem] * (len(operands) - 1) + [pl.BlockSpec(memory_space=pltpu.HBM)],
        out_specs=vmem,
        scratch_shapes=scratch,
        compiler_params=pltpu.CompilerParams(
            collective_id=1, has_side_effects=True, vmem_limit_bytes=32 << 20
        ),
    )(*operands)


def regroup(array, rows):
    count, width = array.shape[0], array.shape[-1]
    if width == rows:
        return array
    array = jnp.moveaxis(array, 0, -2)
    array = array.reshape(array.shape[:-2] + (count * width // rows, rows))
    return jnp.moveaxis(array, -2, 0)


def body(
    hidden_in,
    norm_gain,
    query_weight,
    key_weight,
    value_weight,
    out_weight,
    key_cache,
    value_cache,
    cached_lengths,
    group_ids,
    prompt_pages,
    own_pages,
):
    tok_rows = hidden_in.shape[0]
    seq_count = lax.axis_size("seq")
    kv_count = key_weight.shape[1] // HEAD_DIM
    split = tok_rows == BLOCK and kv_count > 1
    early = EARLY_STEPS * STEP_PAGES if split else 0
    later = LATE_STEPS * STEP_PAGES if split else 0
    tensor_count = lax.axis_size("tensor")
    queries_t, fresh_k, fresh_v, packed, keys, values, w_cols, *rest = gather(
        hidden_in,
        norm_gain,
        query_weight,
        key_weight,
        value_weight,
        key_cache,
        value_cache,
        cached_lengths,
        group_ids,
        prompt_pages,
        own_pages,
        out_weight,
        seq_count,
        tensor_count,
        early,
    )
    queries_t = regroup(queries_t, BLOCK)
    sums, peak = rest if early else (None, None)
    found = attend(
        packed, queries_t, fresh_k, fresh_v, keys, values, sums, peak, early, later
    )
    known = kv_count - 1 if early else kv_count
    parts = [regroup(array, tok_rows) for array in found[:known]]
    scales = [regroup(array, tok_rows) for array in found[known : 2 * known]]
    leftovers = list(found[2 * known :])
    if early:
        leftovers += [queries_t, keys, values]
    return finish(
        parts, scales, leftovers, w_cols, out_weight, seq_count, tensor_count, later
    )


def solution(mesh):
    in_specs = (
        P("seq", None),
        P(),
        P(None, "tensor"),
        P(None, "tensor"),
        P(None, "tensor"),
        P("tensor", None),
        P("seq", None, "tensor"),
        P("seq", None, "tensor"),
        P(),
        P(),
        P(),
        P(),
    )
    out_specs = P("seq", "tensor")
    return jax.shard_map(body, mesh=mesh, in_specs=in_specs, out_specs=out_specs, check_vma=False)
```

```python
import functools
import math

import jax
import jax.numpy as jnp
from jax import lax
from jax.experimental import pallas as pl
from jax.experimental.pallas import tpu as pltpu
from jax.sharding import PartitionSpec as P

HEAD_DIM = 128
PAGE_ROWS = 128
ADDED_TOKENS = 512
GROUPS = 2
PROMPT_PAGES = 128
STEP_PAGES = 8
TAIL_PAGES = 4
BLOCK = 128
EXTRA = 16
REQUESTS = 2
LIMIT = 1e30
EARLY_STEPS = 3
LATE_STEPS = 2
SAFE_POWER = 100.0
SCORE_SCALE = 1.0 / math.sqrt(HEAD_DIM)
EXP2_SCALE = SCORE_SCALE * math.log2(math.e)
EMPTY = -1e30
SHIFT = 60.0 / EXP2_SCALE
BLOCKS = ADDED_TOKENS // BLOCK
LINES = 8
MESH = pl.DeviceIdType.MESH


def in_hbm(array):
    return pltpu.with_memory_space_constraint(array, pltpu.HBM)


def dot_nt(left, right):
    return lax.dot_general(
        left, right, (((1,), (1,)), ((), ())), preferred_element_type=jnp.float32
    )


def cols(index):
    return slice(index * HEAD_DIM, (index + 1) * HEAD_DIM)


def joined_queries(qt_ref, request, kv, per_kv):
    return jnp.concatenate(
        [
            qt_ref[request * BLOCKS + block, kv, cols(sub), :]
            for sub in range(per_kv)
            for block in range(BLOCKS)
        ],
        axis=1,
    )


def joined_marks(qt_ref, request, kv, per_kv):
    rows = [
        qt_ref[request * BLOCKS + block, kv, per_kv * HEAD_DIM :, :].astype(jnp.float32)[
            sub : sub + 1
        ]
        for sub in range(per_kv)
        for block in range(BLOCKS)
    ]
    return jnp.concatenate(rows, axis=1) + SHIFT


def values_t(values):
    ones = jnp.ones((EXTRA, values.shape[0]), jnp.bfloat16)
    return jnp.concatenate([values.T, ones], axis=0)


def page_group(lists, cache_ref, request, start, pages, kv):
    last = cache_ref.shape[0] - 1
    slots = [jnp.clip(lists[request, start + page] >> 8, 0, last) for page in range(pages)]
    return jnp.concatenate([cache_ref[slot, :, cols(kv)] for slot in slots], axis=0)


def page_bias(lists, request, start, pages):
    place = lax.broadcasted_iota(jnp.int32, (PAGE_ROWS, 1), 0)
    return jnp.concatenate(
        [
            jnp.where(place < (lists[request, start + page] & 255), 0.0, EMPTY)
            for page in range(pages)
        ],
        axis=0,
    )


def terms(queries, mark, keys, values, bias):
    scores = jnp.dot(keys, queries, preferred_element_type=jnp.float32)
    if bias is not None:
        scores = scores + bias
    weights = jnp.exp2((scores - mark) * EXP2_SCALE).astype(jnp.bfloat16)
    return jnp.dot(values_t(values), weights, preferred_element_type=jnp.float32)


def early_terms(lists, qt_ref, kc_ref, vc_ref, mark, request, step, kv, per_kv):
    start = step * STEP_PAGES
    return terms(
        joined_queries(qt_ref, request, kv, per_kv),
        mark,
        page_group(lists, kc_ref, request, start, STEP_PAGES, kv),
        page_group(lists, vc_ref, request, start, STEP_PAGES, kv),
        page_bias(lists, request, start, STEP_PAGES),
    )


def settle(sums, top, request, part_ref, ls_ref, per_kv):
    den = sums[HEAD_DIM : HEAD_DIM + 1]
    alive = (den > 0.0) & (top > 0.5 * EMPTY)
    den = jnp.where(alive, den, 1.0)
    scale = jnp.where(alive, top * SCORE_SCALE + jnp.log(den), EMPTY)
    parts = (sums[:HEAD_DIM] * jnp.where(alive, 1.0 / den, 0.0)).astype(jnp.bfloat16)
    for sub in range(per_kv):
        for block in range(BLOCKS):
            place = sub * BLOCKS + block
            span = slice(place * BLOCK, (place + 1) * BLOCK)
            part_ref[request * BLOCKS + block, cols(sub), :] = parts[:, span]
            ls_ref[request * BLOCKS + block, sub : sub + 1, :] = scale[:, span]


def attend_kernel(per_kv, tok_rows, late, early, later, *refs):
    refs = list(refs)
    packed_ref, qt_ref, fk_ref, fv_ref, kc_ref, vc_ref = refs[:6]
    del refs[:6]
    if late:
        start_ref, peak_ref = refs[:2]
        del refs[:2]
    kv_count = kc_ref.shape[2] // HEAD_DIM
    done_kv = kv_count - 1 if late else kv_count
    part_refs, ls_refs = refs[:done_kv], refs[done_kv : 2 * done_kv]
    del refs[: 2 * done_kv]
    if late:
        left_ref, left_m_ref, left_list_ref = refs[:3]
        del refs[:3]
    lists, m_ref, acc_ref, list_sem = refs
    fetch = pltpu.make_async_copy(packed_ref, lists, list_sem)
    fetch.start()
    requests = acc_ref.shape[0]
    width = per_kv * ADDED_TOKENS
    for ls_ref in ls_refs:
        ls_ref[...] = jnp.zeros_like(ls_ref)
    for kv in range(kv_count):
        for request in range(requests):
            if late and kv == 0:
                acc_ref[request, kv] = start_ref[request]
            else:
                acc_ref[request, kv] = jnp.zeros_like(acc_ref[request, kv])
            m_ref[request, kv, 0:1, :] = joined_marks(qt_ref, request, kv, per_kv)
    if late:
        left_list_ref[...] = packed_ref[...]

    def add(request, kv, keys, values, bias):
        queries = joined_queries(qt_ref, request, kv, per_kv)
        acc_ref[request, kv] += terms(queries, m_ref[request, kv, 0:1, :], keys, values, bias)

    def add_running(request, kv, keys, values, bias):
        queries = joined_queries(qt_ref, request, kv, per_kv)
        scores = jnp.dot(keys, queries, preferred_element_type=jnp.float32) + bias
        old = m_ref[request, kv, 0:1, :]
        new = jnp.maximum(old, jnp.max(scores, axis=0, keepdims=True))
        m_ref[request, kv, 0:1, :] = new
        weights = jnp.exp2((scores - new) * EXP2_SCALE)
        acc_ref[request, kv] = acc_ref[request, kv] * jnp.exp2((old - new) * EXP2_SCALE) + jnp.dot(
            values_t(values), weights.astype(jnp.bfloat16), preferred_element_type=jnp.float32
        )

    first = lax.axis_index("seq") * tok_rows
    home = first // ADDED_TOKENS

    def add_fresh(update):
        row = lax.broadcasted_iota(jnp.int32, (tok_rows, width), 0) + (first - home * ADDED_TOKENS)
        col = lax.broadcasted_iota(jnp.int32, (tok_rows, width), 1) % ADDED_TOKENS
        bias = jnp.where(row <= col, 0.0, EMPTY)
        for kv in range(kv_count):
            update(home, kv, fk_ref[:, cols(kv)], fv_ref[:, cols(kv)], bias)

    def add_pages(update, request, start, pages, masked, kvs=range(kv_count)):
        bias = page_bias(lists, request, start, pages) if masked else None
        for kv in kvs:
            keys = page_group(lists, kc_ref, request, start, pages, kv)
            values = page_group(lists, vc_ref, request, start, pages, kv)
            update(request, kv, keys, values, bias)

    add_fresh(add)
    fetch.wait()

    def attend_request(request, carry):
        total = lists[requests + request, 0]
        count = jnp.maximum(total - early, 0)
        whole = jnp.maximum(count - 1, 0) // STEP_PAGES

        def step(index, carry):
            add_pages(add, request, early + index * STEP_PAGES, STEP_PAGES, False)
            return carry

        for start in range(later, early, STEP_PAGES):

            @pl.when(total > start)
            def _():
                add_pages(add, request, start, STEP_PAGES, True, range(done_kv, kv_count))

        lax.fori_loop(0, whole, step, 0)
        done = whole * STEP_PAGES
        rest = count - done

        @pl.when((rest > 0) & (rest <= TAIL_PAGES))
        def _():
            add_pages(add, request, early + done, TAIL_PAGES, True)

        @pl.when(rest > TAIL_PAGES)
        def _():
            add_pages(add, request, early + done, STEP_PAGES, True)

        safe = [
            acc_ref[request, kv, HEAD_DIM : HEAD_DIM + 1, :] < LIMIT for kv in range(kv_count)
        ]
        if late:
            floats = joined_queries(qt_ref, request, kv_count - 1, per_kv).astype(jnp.float32)
            norms = jnp.sum(floats * floats, axis=0, keepdims=True) * jnp.max(peak_ref[...])
            power = (jnp.sqrt(norms) - m_ref[request, kv_count - 1, 0:1, :]) * EXP2_SCALE
            safe.append(power < SAFE_POWER)
        unsafe = jnp.max(
            jnp.concatenate([jnp.where(flags, 0.0, 1.0) for flags in safe], axis=0)
        )

        @pl.when(unsafe > 0.0)
        def _():
            acc_ref[request] = jnp.zeros_like(acc_ref[request])
            m_ref[request] = jnp.full_like(m_ref[request], EMPTY)

            @pl.when(request == home)
            def _():
                add_fresh(add_running)

            def step(index, carry):
                add_pages(add_running, request, index * TAIL_PAGES, TAIL_PAGES, True)
                return carry

            lax.fori_loop(0, (total + TAIL_PAGES - 1) // TAIL_PAGES, step, 0)
            if late:
                row = lax.broadcasted_iota(jnp.int32, left_list_ref.shape, 0)
                left_list_ref[...] = jnp.where(row == request, 0, left_list_ref[...])

        for kv in range(done_kv):
            settle(
                acc_ref[request, kv],
                m_ref[request, kv, 0:1, :],
                request,
                part_refs[kv],
                ls_refs[kv],
                per_kv,
            )
        if late:
            left_ref[request] = acc_ref[request, done_kv]
            left_m_ref[request] = m_ref[request, done_kv]
        return carry

    lax.fori_loop(0, requests, attend_request, 0)


def attend(
    packed, queries_t, fresh_k, fresh_v, key_cache, value_cache, early_sums, peak, early, later
):
    blocks, kv_count, q_rows, _ = queries_t.shape
    late = early > 0
    done_kv = kv_count - 1 if late else kv_count
    q_rows -= EXTRA
    per_kv = q_rows // HEAD_DIM
    pages, _, kv_cols = key_cache.shape
    tok_rows = fresh_k.shape[0]
    requests = blocks // BLOCKS
    width = per_kv * ADDED_TOKENS
    vmem = pl.BlockSpec(memory_space=pltpu.VMEM)
    out_shape = [jax.ShapeDtypeStruct((blocks, q_rows, BLOCK), jnp.bfloat16)] * done_kv
    out_shape += [jax.ShapeDtypeStruct((blocks, LINES, BLOCK), jnp.float32)] * done_kv
    operands = [packed, queries_t, fresh_k, fresh_v, key_cache, value_cache]
    if late:
        out_shape += [
            jax.ShapeDtypeStruct((requests, HEAD_DIM + EXTRA, width), jnp.float32),
            jax.ShapeDtypeStruct((requests, LINES, width), jnp.float32),
            jax.ShapeDtypeStruct(packed.shape, packed.dtype),
        ]
        operands += [early_sums, peak]
    return pl.pallas_call(
        functools.partial(attend_kernel, per_kv, tok_rows, late, early, later),
        out_shape=tuple(out_shape),
        in_specs=[vmem] * len(operands),
        out_specs=(vmem,) * len(out_shape),
        scratch_shapes=[
            pltpu.SMEM(packed.shape, packed.dtype),
            pltpu.VMEM((requests, kv_count, LINES, width), jnp.float32),
            pltpu.VMEM((requests, kv_count, HEAD_DIM + EXTRA, width), jnp.float32),
            pltpu.SemaphoreType.DMA(()),
        ],
        compiler_params=pltpu.CompilerParams(vmem_limit_bytes=28 << 20),
        cost_estimate=pl.CostEstimate(
            flops=4 * pages * PAGE_ROWS * ADDED_TOKENS * q_rows * kv_count,
            bytes_accessed=4 * pages * PAGE_ROWS * kv_cols,
            transcendentals=pages * PAGE_ROWS * ADDED_TOKENS * per_kv * kv_count,
        ),
    )(*operands)


def page_lists(lengths_ref, groups_ref, prompt_ref, own_ref, packed_ref, pages_dev, me):
    count = PROMPT_PAGES + own_ref.shape[1]
    position = lax.broadcasted_iota(jnp.int32, (1, count), 1)
    owned, pages, lives = [], [], []
    for request in range(REQUESTS):
        prompt = prompt_ref[0:1, :]
        for group in range(1, GROUPS):
            prompt = jnp.where(groups_ref[request] == group, prompt_ref[group : group + 1, :], prompt)
        slots = jnp.concatenate([prompt, own_ref[request : request + 1, :]], axis=1)
        own_len = lengths_ref[request] - PROMPT_PAGES * PAGE_ROWS
        live = jnp.clip(own_len - (position - PROMPT_PAGES) * PAGE_ROWS, 0, PAGE_ROWS)
        live = jnp.where(position < PROMPT_PAGES, PAGE_ROWS, live)
        page = slots - me * pages_dev
        owned.append((page >= 0) & (page < pages_dev) & (live > 0))
        pages.append(page)
        lives.append(live)
    earlier = lax.broadcasted_iota(jnp.int32, (count, count), 0)
    earlier = earlier < lax.broadcasted_iota(jnp.int32, (count, count), 1)
    earlier = jnp.where(earlier, 1.0, 0.0).astype(jnp.bfloat16)
    place = lax.broadcasted_iota(jnp.int32, (PAGE_ROWS, count), 0).astype(jnp.float32)
    packed_ref[...] = jnp.zeros_like(packed_ref)
    for request in range(REQUESTS):
        mark = jnp.where(owned[request], 1.0, 0.0)
        marks = jnp.broadcast_to(mark, (EXTRA, count)).astype(jnp.bfloat16)
        before = jnp.dot(marks, earlier, preferred_element_type=jnp.float32)[0:1]
        before = jnp.where(owned[request], before, -1.0)
        onehot = jnp.where(before == place, 1.0, 0.0).astype(jnp.bfloat16)

        def pick(line):
            line = jnp.where(owned[request], line, 0).astype(jnp.float32)
            lines = jnp.broadcast_to(line, (EXTRA, count)).astype(jnp.bfloat16)
            return dot_nt(lines, onehot)[0:1]

        packed = pick(pages[request]) * 256.0 + pick(lives[request])
        packed_ref[request : request + 1, :] = packed.astype(jnp.int32)
        total = jnp.sum(mark, axis=1, keepdims=True)
        packed_ref[REQUESTS + request : REQUESTS + request + 1, :] = jnp.broadcast_to(
            total, (1, PAGE_ROWS)
        ).astype(jnp.int32)


def greet(peers):
    barrier = pltpu.get_barrier_semaphore()
    for peer in peers:
        pl.semaphore_signal(barrier, inc=1, device_id=peer, device_id_type=MESH)


def greeted(count):
    pl.semaphore_wait(pltpu.get_barrier_semaphore(), count)


def remote(source, target, send_sem, recv_sem, peer):
    return pltpu.make_async_remote_copy(
        src_ref=source,
        dst_ref=target,
        send_sem=send_sem,
        recv_sem=recv_sem,
        device_id=peer,
        device_id_type=MESH,
    )


def spread_columns(w_hbm, start, target, tensor_count, send_sem, recv_sem):
    me = lax.axis_index("seq")
    tensor = lax.axis_index("tensor")
    rows, columns = target.shape[1:]

    def block(owner):
        first = pl.multiple_of(owner * columns, columns)
        return w_hbm.at[pl.ds(start, rows), pl.ds(first, columns)]

    copies = [pltpu.make_async_copy(block(tensor), target.at[tensor], send_sem.at[0])]
    for distance in range(1, tensor_count):
        owner = (tensor + distance) % tensor_count
        copies.append(
            remote(
                block(owner),
                target.at[tensor],
                send_sem.at[distance],
                recv_sem.at[distance],
                (me, owner),
            )
        )
    return copies


def gather_kernel(seq_count, early, *refs):
    refs = list(refs)
    x_ref, gain_hbm, wq_ref, wk_ref, wv_ref, kc_hbm, vc_hbm, w_hbm = refs[:8]
    small_hbm = refs[8:12]
    qt_ref, fk_ref, fv_ref, packed_ref, kc_ref, vc_ref, w_cols = refs[12:19]
    del refs[:19]
    if early:
        sums_ref, peak_ref = refs[:2]
        del refs[:2]
    q_send, q_recv, qy_send, qy_recv, wq_buf, wk_buf, wv_buf, x_buf = refs[:8]
    load_sem, lists, gain_ref, lengths_ref, groups_ref, prompt_ref, own_ref = refs[8:15]
    w_send, w_recv = refs[15:]
    loads = [
        pltpu.make_async_copy(source, target, load_sem.at[index])
        for index, (source, target) in enumerate(
            (
                (x_ref, x_buf),
                (wk_ref, wk_buf),
                (wq_ref, wq_buf),
                (wv_ref, wv_buf),
                (kc_hbm, kc_ref),
                (vc_hbm, vc_ref),
                (packed_ref, lists),
                (gain_hbm, gain_ref),
                (small_hbm[0], lengths_ref),
                (small_hbm[1], groups_ref),
                (small_hbm[2], prompt_ref),
                (small_hbm[3], own_ref),
            )
        )
    ]
    small = loads[7:]
    for load in loads[:1] + small + loads[1:4]:
        load.start()
    me = lax.axis_index("seq")
    tensor = lax.axis_index("tensor")
    tensor_count = w_cols.shape[0]
    outer = seq_count // 2
    place, side = me // 2, me % 2
    twin = (place * 2 + 1 - side, tensor)
    kv_count = qt_ref.shape[1]
    per_kv = (qt_ref.shape[2] - EXTRA) // HEAD_DIM
    order = sorted(range(1, outer), key=lambda distance: -min(distance, outer - distance))

    def line_peer(distance):
        return (place + distance) % outer * 2 + side

    others = [(me, (tensor + distance) % tensor_count) for distance in range(1, tensor_count)]
    greet([twin] + [(line_peer(distance), tensor) for distance in range(1, outer)] + others)

    loads[0].wait()
    small[0].wait()
    floats = x_buf[...].astype(jnp.float32)
    mean = jnp.mean(floats * floats, axis=-1, keepdims=True)
    normed = (floats * lax.rsqrt(mean + 1e-05) * gain_ref[...]).astype(jnp.bfloat16)

    def project(weight):
        return jnp.dot(normed, weight, preferred_element_type=jnp.float32)

    loads[1].wait()
    keys = project(wk_buf[...])
    fk_ref[...] = keys.astype(jnp.bfloat16)
    keys_t = keys.T.astype(jnp.bfloat16)
    loads[2].wait()
    started = []

    def make(kv):
        span = per_kv * HEAD_DIM
        queries_t = project(wq_buf[:, kv * span : (kv + 1) * span]).T.astype(jnp.bfloat16)
        qt_ref[me, kv, :span, :] = queries_t
        right = keys_t[cols(kv)].astype(jnp.float32)
        marks = [
            jnp.sum(queries_t[cols(sub)].astype(jnp.float32) * right, axis=0, keepdims=True)
            for sub in range(per_kv)
        ]
        marks.append(jnp.zeros((EXTRA - per_kv, marks[0].shape[1]), jnp.float32))
        qt_ref[me, kv, span:, :] = jnp.concatenate(marks, axis=0).astype(jnp.bfloat16)

    def launch(kv):
        own = qt_ref.at[me, kv]
        copy = remote(own, own, qy_send.at[kv, 0], qy_recv.at[kv, 0], twin)
        copy.start()
        started.append(copy)
        for distance in order:
            peer = (line_peer(distance), tensor)
            copy = remote(own, own, q_send.at[kv, distance], q_recv.at[kv, distance], peer)
            copy.start()
            started.append(copy)

    def relay(kv, distance):
        block = qt_ref.at[line_peer(outer - distance), kv]
        remote(block, block, q_send.at[kv, distance], q_recv.at[kv, distance], twin).wait_recv()
        copy = remote(block, block, qy_send.at[kv, distance], qy_recv.at[kv, distance], twin)
        copy.start()
        started.append(copy)

    def arrive(kv):
        for distance in [0] + order:
            block = qt_ref.at[(place + outer - distance) % outer * 2 + 1 - side, kv]
            remote(block, block, qy_send.at[kv, distance], qy_recv.at[kv, distance], twin).wait_recv()

    make(0)
    greeted(outer + tensor_count - 1)
    launch(0)
    for load in loads[4:6]:
        load.start()
    spread = spread_columns(w_hbm, 0, w_cols, tensor_count, w_send, w_recv)
    for copy in spread:
        copy.start()
    for kv in range(1, kv_count):
        make(kv)
    loads[3].wait()
    fv_ref[...] = project(wv_buf[...]).astype(jnp.bfloat16)
    for load in small[1:]:
        load.wait()
    page_lists(lengths_ref, groups_ref, prompt_ref, own_ref, packed_ref, kc_ref.shape[0], me)
    for distance in order:
        relay(0, distance)
    for kv in range(1, kv_count):
        launch(kv)
    loads[6].start()
    for load in loads[4:7]:
        load.wait()
    waiting = [(kv, distance) for kv in range(1, kv_count) for distance in order]
    if early:
        peak = jnp.zeros((PAGE_ROWS, 1), jnp.float32)
        for page in range(kc_ref.shape[0]):
            floats = kc_ref[page, :, cols(kv_count - 1)].astype(jnp.float32)
            peak = jnp.maximum(peak, jnp.sum(floats * floats, axis=1, keepdims=True))
        peak_ref[...] = jnp.broadcast_to(peak, peak_ref.shape)
        arrive(0)
        marks = [joined_marks(qt_ref, request, 0, per_kv) for request in range(REQUESTS)]
        for step in range(early // STEP_PAGES):
            for request in range(REQUESTS):
                fresh = early_terms(
                    lists, qt_ref, kc_ref, vc_ref, marks[request], request, step, 0, per_kv
                )
                if step == 0:
                    sums_ref[request] = fresh
                else:
                    sums_ref[request] += fresh
                if waiting:
                    relay(*waiting.pop(0))
    else:
        arrive(0)
    for kv, distance in waiting:
        relay(kv, distance)
    for kv in range(1, kv_count):
        arrive(kv)
    for copy in spread:
        copy.wait()
    for copy in started:
        copy.wait_send()


def gather(
    hidden_in,
    norm_gain,
    query_weight,
    key_weight,
    value_weight,
    key_cache,
    value_cache,
    cached_lengths,
    group_ids,
    prompt_pages,
    own_pages,
    out_weight,
    seq_count,
    tensor_count,
    early,
):
    tok_rows = hidden_in.shape[0]
    q_cols, kv_cols = query_weight.shape[1], key_weight.shape[1]
    kv_count = kv_cols // HEAD_DIM
    per_kv = q_cols // kv_cols
    slots = pltpu.SemaphoreType.DMA((kv_count, seq_count // 2))
    vmem = pl.BlockSpec(memory_space=pltpu.VMEM)
    hbm = pl.BlockSpec(memory_space=pltpu.HBM)
    fresh = jax.ShapeDtypeStruct((tok_rows, kv_cols), jnp.bfloat16)
    rows = per_kv * HEAD_DIM + EXTRA
    out_shape = [
        jax.ShapeDtypeStruct((seq_count, kv_count, rows, tok_rows), jnp.bfloat16),
        fresh,
        fresh,
        jax.ShapeDtypeStruct((LINES, PAGE_ROWS), jnp.int32),
        jax.ShapeDtypeStruct(key_cache.shape, key_cache.dtype),
        jax.ShapeDtypeStruct(value_cache.shape, value_cache.dtype),
        jax.ShapeDtypeStruct(
            (tensor_count, per_kv * HEAD_DIM, out_weight.shape[1] // tensor_count), jnp.bfloat16
        ),
    ]
    if early:
        sums = (REQUESTS, HEAD_DIM + EXTRA, per_kv * ADDED_TOKENS)
        out_shape += [
            jax.ShapeDtypeStruct(sums, jnp.float32),
            jax.ShapeDtypeStruct((PAGE_ROWS, HEAD_DIM), jnp.float32),
        ]
    return pl.pallas_call(
        functools.partial(gather_kernel, seq_count, early),
        out_shape=tuple(out_shape),
        in_specs=[hbm] * 12,
        out_specs=(vmem,) * len(out_shape),
        scratch_shapes=[slots] * 4
        + [
            pltpu.VMEM(weight.shape, weight.dtype)
            for weight in (query_weight, key_weight, value_weight, hidden_in)
        ]
        + [
            pltpu.SemaphoreType.DMA((12,)),
            pltpu.SMEM((LINES, PAGE_ROWS), jnp.int32),
            pltpu.VMEM((1, norm_gain.shape[0]), norm_gain.dtype),
            pltpu.SMEM(cached_lengths.shape, jnp.int32),
            pltpu.SMEM(group_ids.shape, jnp.int32),
            pltpu.VMEM(prompt_pages.shape, jnp.int32),
            pltpu.VMEM(own_pages.shape, jnp.int32),
            pltpu.SemaphoreType.DMA((tensor_count,)),
            pltpu.SemaphoreType.DMA((tensor_count,)),
        ],
        compiler_params=pltpu.CompilerParams(
            collective_id=0, has_side_effects=True, vmem_limit_bytes=40 << 20
        ),
    )(
        in_hbm(hidden_in),
        in_hbm(norm_gain.reshape(1, -1)),
        in_hbm(query_weight),
        in_hbm(key_weight),
        in_hbm(value_weight),
        in_hbm(key_cache),
        in_hbm(value_cache),
        in_hbm(out_weight),
        in_hbm(cached_lengths),
        in_hbm(group_ids),
        in_hbm(prompt_pages),
        in_hbm(own_pages),
    )


def finish_kernel(seq_count, tensor_count, kv_count, early, *refs):
    refs = list(refs)
    known = kv_count - 1 if early else kv_count
    part_refs, ls_refs = refs[:known], refs[known : 2 * known]
    del refs[: 2 * known]
    if early:
        left_ref, left_m_ref, packed_ref, qt_ref, kc_ref, vc_ref = refs[:6]
        del refs[:6]
    w_early, w_hbm, out_ref = refs[:3]
    mix_ref, mix_got, mls_ref, side_got, sls_ref, gls_ref = refs[3:9]
    w_late, att_ref = refs[9:11]
    side_send, side_recv, sls_send, sls_recv, mix_send, mix_recv, mls_send, mls_recv = refs[11:19]
    w_send, w_recv, far_send, far_recv, near_send, near_recv = refs[19:25]
    del refs[:25]
    if early:
        late_ref, lists, list_sem = refs[2:]
        part_refs = part_refs + refs[:1]
        ls_refs = ls_refs + refs[1:2]
        fetch = pltpu.make_async_copy(packed_ref, lists, list_sem)
        fetch.start()
    tok_rows, out_cols = out_ref.shape
    per_kv = part_refs[0].shape[1] // HEAD_DIM
    me = lax.axis_index("seq")
    tensor = lax.axis_index("tensor")
    pair, core = tensor // 2, tensor % 2
    pairs = tensor_count // 2
    twin = (me, pair * 2 + 1 - core)
    outer = seq_count // 2
    place, side = me // 2, me % 2
    beside = (place * 2 + 1 - side, tensor)
    order = sorted(range(1, outer), key=lambda distance: -min(distance, outer - distance))

    def far_pair(distance):
        return (pair + distance) % pairs

    def line(distance, which):
        return (place + distance) % outer * 2 + which

    greet(
        [beside]
        + [(line(distance, side), tensor) for distance in range(1, outer)]
        + [twin]
        + [(me, far_pair(distance) * 2 + core) for distance in range(1, pairs)]
        + [(me, far_pair(distance) * 2 + 1 - core) for distance in range(1, pairs)]
    )
    greeted(outer + tensor_count - 1)
    started = []
    scales, sides, mixes, mix_scales, shares = {}, {}, {}, {}, {}

    def begin(table, key, *rest):
        table[key] = remote(*rest)
        table[key].start()
        started.append(table[key])

    def send_sides(kv):
        for distance in order + [0]:
            begin(
                scales,
                (kv, distance),
                ls_refs[kv].at[line(distance, 1 - side)],
                sls_ref.at[kv, distance],
                sls_send.at[kv, distance],
                sls_recv.at[kv, distance],
                beside,
            )
        for distance in order + [0]:
            begin(
                sides,
                (kv, distance),
                part_refs[kv].at[line(distance, 1 - side)],
                side_got.at[kv, distance],
                side_send.at[kv, distance],
                side_recv.at[kv, distance],
                beside,
            )

    def weighted(block, share):
        return [
            block[cols(sub)].astype(jnp.float32) * share[sub : sub + 1] for sub in range(per_kv)
        ]

    def plus(left, right):
        return [one + other for one, other in zip(left, right)]

    def weigh(kv):
        for distance in order + [0]:
            scales[kv, distance].wait_recv()
        own_lines = jnp.stack([ls_refs[kv][line(distance, side)] for distance in range(outer)])
        side_lines = sls_ref[kv]
        top = jnp.maximum(own_lines, side_lines)
        own_scale, side_scale = jnp.exp(own_lines - top), jnp.exp(side_lines - top)
        both = own_scale + side_scale
        mls_ref[kv] = top + jnp.log(both)
        for distance in order:
            begin(
                mix_scales,
                (kv, distance),
                mls_ref.at[kv, distance],
                gls_ref.at[kv, distance],
                mls_send.at[kv, distance],
                mls_recv.at[kv, distance],
                (line(distance, side), tensor),
            )
        shares[kv] = own_scale / both, side_scale / both

    def mixed(kv, distance):
        sides[kv, distance].wait_recv()
        own_shares, side_shares = shares[kv]
        return plus(
            weighted(part_refs[kv][line(distance, side)], own_shares[distance]),
            weighted(side_got[kv, distance], side_shares[distance]),
        )

    def send_mix(kv, distance):
        mix_ref[kv, distance] = jnp.concatenate(mixed(kv, distance), axis=0).astype(jnp.bfloat16)
        begin(
            mixes,
            (kv, distance),
            mix_ref.at[kv, distance],
            mix_got.at[kv, distance],
            mix_send.at[kv, distance],
            mix_recv.at[kv, distance],
            (line(distance, side), tensor),
        )

    def merged(kv):
        gls_ref[kv, 0] = mls_ref[kv, 0]
        for distance in order:
            mix_scales[kv, distance].wait_recv()
        lines = gls_ref[kv]
        lines = jnp.exp(lines - jnp.max(lines, axis=0, keepdims=True))
        share = lines / jnp.sum(lines, axis=0, keepdims=True)
        total = [block * share[0][sub : sub + 1] for sub, block in enumerate(mixed(kv, 0))]
        for distance in order:
            mixes[kv, distance].wait_recv()
            total = plus(total, weighted(mix_got[kv, distance], share[distance]))
        return jnp.concatenate(total, axis=0).astype(jnp.bfloat16)

    def twin_copy(kv, distance, which):
        block = att_ref.at[(pair + pairs - distance) % pairs * 2 + which, kv]
        return remote(block, block, near_send.at[kv, distance], near_recv.at[kv, distance], twin)

    def far_copy(kv, distance, source, target):
        block = att_ref.at[source, kv]
        return remote(
            block, block, far_send.at[kv, distance], far_recv.at[kv, distance], (me, target)
        )

    def share_out(kv, attention):
        att_ref[tensor, kv] = attention
        copies = [
            far_copy(kv, distance, tensor, far_pair(distance) * 2 + core)
            for distance in range(1, pairs)
        ]
        copies.append(twin_copy(kv, 0, core))
        for copy in copies:
            copy.start()
            started.append(copy)

    def pass_on(kv):
        for distance in range(1, pairs):
            source = far_pair(pairs - distance) * 2 + core
            far_copy(kv, distance, source, source).wait_recv()
            copy = twin_copy(kv, distance, core)
            copy.start()
            started.append(copy)

    def terms_of(kv, source):
        rest = (kv - 1) * per_kv * HEAD_DIM
        if kv == 0:
            weight = w_early[source]
        else:
            weight = w_late[source, rest : rest + per_kv * HEAD_DIM, :]
        return lax.dot_general(
            att_ref[source, kv],
            weight,
            (((0,), (0,)), ((), ())),
            preferred_element_type=jnp.float32,
        )

    def own_terms(kv):
        return terms_of(kv, tensor)

    def far_terms(kv):
        total = None
        for distance in range(1, pairs):
            fresh = terms_of(kv, far_pair(distance) * 2 + core)
            total = fresh if total is None else total + fresh
        return total

    def twin_terms(kv):
        total = None
        for distance in range(pairs):
            twin_copy(kv, distance, 1 - core).wait_recv()
            fresh = terms_of(kv, (pair + pairs - distance) % pairs * 2 + 1 - core)
            total = fresh if total is None else total + fresh
        return total

    last = kv_count - 1
    for kv in range(known):
        send_sides(kv)
    spread = spread_columns(w_hbm, per_kv * HEAD_DIM, w_late, tensor_count, w_send, w_recv)
    for copy in spread:
        copy.start()
    if early:
        fetch.wait()
        ls_refs[last][...] = jnp.zeros_like(ls_refs[last])
        steps = [
            (step, request)
            for step in range(early // STEP_PAGES)
            for request in range(REQUESTS)
        ]
        tasks = [(weigh, (kv,)) for kv in range(known)]
        tasks += [(send_mix, (kv, distance)) for kv in range(known) for distance in order]
        share_of = -(-len(tasks) // len(steps))
        for step, request in steps:
            late_ref[request] = (left_ref if step == 0 else late_ref)[request] + early_terms(
                lists,
                qt_ref,
                kc_ref,
                vc_ref,
                left_m_ref[request, 0:1, :],
                request,
                step,
                last,
                per_kv,
            )
            for run, given in tasks[:share_of]:
                run(*given)
            del tasks[:share_of]
        for request in range(REQUESTS):
            settle(
                late_ref[request],
                left_m_ref[request, 0:1, :],
                request,
                part_refs[last],
                ls_refs[last],
                per_kv,
            )
        send_sides(last)
        ready = known
    else:
        ready = 0
    for kv in range(ready, kv_count):
        weigh(kv)
        for distance in order:
            send_mix(kv, distance)
    for kv in range(last):
        share_out(kv, merged(kv))
        pass_on(kv)
    share_out(last, merged(last))
    for copy in spread:
        copy.wait()
    result = own_terms(last)
    for kv in range(last):
        result = result + own_terms(kv) + far_terms(kv) + twin_terms(kv)
    pass_on(last)
    result = result + far_terms(last) + twin_terms(last)
    out_ref[...] = result.astype(jnp.bfloat16)
    for copy in started:
        copy.wait_send()


def finish(parts, scales, leftovers, w_cols, out_weight, seq_count, tensor_count, early):
    q_rows, tok_rows = parts[0].shape[1:]
    kv_count = len(parts) + (1 if early else 0)
    out_cols = out_weight.shape[1] // tensor_count
    pairs = tensor_count // 2
    outer = seq_count // 2
    vmem = pl.BlockSpec(memory_space=pltpu.VMEM)
    w_block = (tensor_count, out_weight.shape[0] - w_cols.shape[1], out_cols)
    att_block = (tensor_count, kv_count, q_rows, tok_rows)
    part_buf = pltpu.VMEM((kv_count, outer, q_rows, tok_rows), jnp.bfloat16)
    scale_buf = pltpu.VMEM((kv_count, outer, LINES, tok_rows), jnp.float32)
    line_sems = pltpu.SemaphoreType.DMA((kv_count, outer))
    pair_sems = pltpu.SemaphoreType.DMA((kv_count, pairs))
    w_sems = pltpu.SemaphoreType.DMA((tensor_count,))
    operands = list(parts) + list(scales) + list(leftovers) + [w_cols, in_hbm(out_weight)]
    scratch = [part_buf, part_buf, scale_buf, part_buf, scale_buf, scale_buf]
    scratch += [pltpu.VMEM(w_block, jnp.bfloat16), pltpu.VMEM(att_block, jnp.bfloat16)]
    scratch += [line_sems] * 8 + [w_sems] * 2 + [pair_sems] * 4
    if early:
        scratch += [
            pltpu.VMEM(parts[0].shape, parts[0].dtype),
            pltpu.VMEM(scales[0].shape, scales[0].dtype),
            pltpu.VMEM(leftovers[0].shape, leftovers[0].dtype),
            pltpu.SMEM(leftovers[2].shape, leftovers[2].dtype),
            pltpu.SemaphoreType.DMA(()),
        ]
    return pl.pallas_call(
        functools.partial(finish_kernel, seq_count, tensor_count, kv_count, early),
        out_shape=jax.ShapeDtypeStruct((tok_rows, out_cols), jnp.bfloat16),
        in_specs=[vmem] * (len(operands) - 1) + [pl.BlockSpec(memory_space=pltpu.HBM)],
        out_specs=vmem,
        scratch_shapes=scratch,
        compiler_params=pltpu.CompilerParams(
            collective_id=1, has_side_effects=True, vmem_limit_bytes=32 << 20
        ),
    )(*operands)


def regroup(array, rows):
    count, width = array.shape[0], array.shape[-1]
    if width == rows:
        return array
    array = jnp.moveaxis(array, 0, -2)
    array = array.reshape(array.shape[:-2] + (count * width // rows, rows))
    return jnp.moveaxis(array, -2, 0)


def body(
    hidden_in,
    norm_gain,
    query_weight,
    key_weight,
    value_weight,
    out_weight,
    key_cache,
    value_cache,
    cached_lengths,
    group_ids,
    prompt_pages,
    own_pages,
):
    tok_rows = hidden_in.shape[0]
    seq_count = lax.axis_size("seq")
    kv_count = key_weight.shape[1] // HEAD_DIM
    split = tok_rows == BLOCK and kv_count > 1
    early = EARLY_STEPS * STEP_PAGES if split else 0
    later = LATE_STEPS * STEP_PAGES if split else 0
    tensor_count = lax.axis_size("tensor")
    queries_t, fresh_k, fresh_v, packed, keys, values, w_cols, *rest = gather(
        hidden_in,
        norm_gain,
        query_weight,
        key_weight,
        value_weight,
        key_cache,
        value_cache,
        cached_lengths,
        group_ids,
        prompt_pages,
        own_pages,
        out_weight,
        seq_count,
        tensor_count,
        early,
    )
    queries_t = regroup(queries_t, BLOCK)
    sums, peak = rest if early else (None, None)
    found = attend(
        packed, queries_t, fresh_k, fresh_v, keys, values, sums, peak, early, later
    )
    known = kv_count - 1 if early else kv_count
    parts = [regroup(array, tok_rows) for array in found[:known]]
    scales = [regroup(array, tok_rows) for array in found[known : 2 * known]]
    leftovers = list(found[2 * known :])
    if early:
        leftovers += [queries_t, keys, values]
    return finish(
        parts, scales, leftovers, w_cols, out_weight, seq_count, tensor_count, later
    )


def solution(mesh):
    in_specs = (
        P("seq", None),
        P(),
        P(None, "tensor"),
        P(None, "tensor"),
        P(None, "tensor"),
        P("tensor", None),
        P("seq", None, "tensor"),
        P("seq", None, "tensor"),
        P(),
        P(),
        P(),
        P(),
    )
    out_specs = P("seq", "tensor")
    return jax.shard_map(body, mesh=mesh, in_specs=in_specs, out_specs=out_specs, check_vma=False)
```

```python
import functools
import math

import jax
import jax.numpy as jnp
from jax import lax
from jax.experimental import pallas as pl
from jax.experimental.pallas import tpu as pltpu
from jax.sharding import PartitionSpec as P

HEAD_DIM = 128
PAGE_ROWS = 128
ADDED_TOKENS = 512
GROUPS = 2
PROMPT_PAGES = 128
STEP_PAGES = 8
TAIL_PAGES = 4
BLOCK = 128
EXTRA = 16
REQUESTS = 2
LIMIT = 1e30
EARLY_STEPS = 3
LATE_STEPS = 3
SAFE_POWER = 100.0
SCORE_SCALE = 1.0 / math.sqrt(HEAD_DIM)
EXP2_SCALE = SCORE_SCALE * math.log2(math.e)
EMPTY = -1e30
SHIFT = 60.0 / EXP2_SCALE
BLOCKS = ADDED_TOKENS // BLOCK
LINES = 8
MESH = pl.DeviceIdType.MESH


def in_hbm(array):
    return pltpu.with_memory_space_constraint(array, pltpu.HBM)


def dot_nt(left, right):
    return lax.dot_general(
        left, right, (((1,), (1,)), ((), ())), preferred_element_type=jnp.float32
    )


def cols(index):
    return slice(index * HEAD_DIM, (index + 1) * HEAD_DIM)


def joined_queries(qt_ref, request, kv, per_kv):
    return jnp.concatenate(
        [
            qt_ref[request * BLOCKS + block, kv, cols(sub), :]
            for sub in range(per_kv)
            for block in range(BLOCKS)
        ],
        axis=1,
    )


def joined_marks(qt_ref, request, kv, per_kv):
    rows = [
        qt_ref[request * BLOCKS + block, kv, per_kv * HEAD_DIM :, :].astype(jnp.float32)[
            sub : sub + 1
        ]
        for sub in range(per_kv)
        for block in range(BLOCKS)
    ]
    return jnp.concatenate(rows, axis=1) + SHIFT


def values_t(values):
    ones = jnp.ones((EXTRA, values.shape[0]), jnp.bfloat16)
    return jnp.concatenate([values.T, ones], axis=0)


def page_group(lists, cache_ref, request, start, pages, kv):
    last = cache_ref.shape[0] - 1
    slots = [jnp.clip(lists[request, start + page] >> 8, 0, last) for page in range(pages)]
    return jnp.concatenate([cache_ref[slot, :, cols(kv)] for slot in slots], axis=0)


def page_bias(lists, request, start, pages):
    place = lax.broadcasted_iota(jnp.int32, (PAGE_ROWS, 1), 0)
    return jnp.concatenate(
        [
            jnp.where(place < (lists[request, start + page] & 255), 0.0, EMPTY)
            for page in range(pages)
        ],
        axis=0,
    )


def terms(queries, mark, keys, values, bias):
    scores = jnp.dot(keys, queries, preferred_element_type=jnp.float32)
    if bias is not None:
        scores = scores + bias
    weights = jnp.exp2((scores - mark) * EXP2_SCALE).astype(jnp.bfloat16)
    return jnp.dot(values_t(values), weights, preferred_element_type=jnp.float32)


def early_terms(lists, qt_ref, kc_ref, vc_ref, mark, request, step, kv, per_kv):
    start = step * STEP_PAGES
    return terms(
        joined_queries(qt_ref, request, kv, per_kv),
        mark,
        page_group(lists, kc_ref, request, start, STEP_PAGES, kv),
        page_group(lists, vc_ref, request, start, STEP_PAGES, kv),
        page_bias(lists, request, start, STEP_PAGES),
    )


def settle(sums, top, request, part_ref, ls_ref, per_kv):
    den = sums[HEAD_DIM : HEAD_DIM + 1]
    alive = (den > 0.0) & (top > 0.5 * EMPTY)
    den = jnp.where(alive, den, 1.0)
    scale = jnp.where(alive, top * SCORE_SCALE + jnp.log(den), EMPTY)
    parts = (sums[:HEAD_DIM] * jnp.where(alive, 1.0 / den, 0.0)).astype(jnp.bfloat16)
    for sub in range(per_kv):
        for block in range(BLOCKS):
            place = sub * BLOCKS + block
            span = slice(place * BLOCK, (place + 1) * BLOCK)
            part_ref[request * BLOCKS + block, cols(sub), :] = parts[:, span]
            ls_ref[request * BLOCKS + block, sub : sub + 1, :] = scale[:, span]


def attend_kernel(per_kv, tok_rows, late, early, later, *refs):
    refs = list(refs)
    packed_ref, qt_ref, fk_ref, fv_ref, kc_ref, vc_ref = refs[:6]
    del refs[:6]
    if late:
        start_ref, peak_ref = refs[:2]
        del refs[:2]
    kv_count = kc_ref.shape[2] // HEAD_DIM
    done_kv = kv_count - 1 if late else kv_count
    part_refs, ls_refs = refs[:done_kv], refs[done_kv : 2 * done_kv]
    del refs[: 2 * done_kv]
    if late:
        left_ref, left_m_ref, left_list_ref = refs[:3]
        del refs[:3]
    lists, m_ref, acc_ref, list_sem = refs
    fetch = pltpu.make_async_copy(packed_ref, lists, list_sem)
    fetch.start()
    requests = acc_ref.shape[0]
    width = per_kv * ADDED_TOKENS
    for ls_ref in ls_refs:
        ls_ref[...] = jnp.zeros_like(ls_ref)
    for kv in range(kv_count):
        for request in range(requests):
            if late and kv == 0:
                acc_ref[request, kv] = start_ref[request]
            else:
                acc_ref[request, kv] = jnp.zeros_like(acc_ref[request, kv])
            m_ref[request, kv, 0:1, :] = joined_marks(qt_ref, request, kv, per_kv)
    if late:
        left_list_ref[...] = packed_ref[...]

    def add(request, kv, keys, values, bias):
        queries = joined_queries(qt_ref, request, kv, per_kv)
        acc_ref[request, kv] += terms(queries, m_ref[request, kv, 0:1, :], keys, values, bias)

    def add_running(request, kv, keys, values, bias):
        queries = joined_queries(qt_ref, request, kv, per_kv)
        scores = jnp.dot(keys, queries, preferred_element_type=jnp.float32) + bias
        old = m_ref[request, kv, 0:1, :]
        new = jnp.maximum(old, jnp.max(scores, axis=0, keepdims=True))
        m_ref[request, kv, 0:1, :] = new
        weights = jnp.exp2((scores - new) * EXP2_SCALE)
        acc_ref[request, kv] = acc_ref[request, kv] * jnp.exp2((old - new) * EXP2_SCALE) + jnp.dot(
            values_t(values), weights.astype(jnp.bfloat16), preferred_element_type=jnp.float32
        )

    first = lax.axis_index("seq") * tok_rows
    home = first // ADDED_TOKENS

    def add_fresh(update):
        row = lax.broadcasted_iota(jnp.int32, (tok_rows, width), 0) + (first - home * ADDED_TOKENS)
        col = lax.broadcasted_iota(jnp.int32, (tok_rows, width), 1) % ADDED_TOKENS
        bias = jnp.where(row <= col, 0.0, EMPTY)
        for kv in range(kv_count):
            update(home, kv, fk_ref[:, cols(kv)], fv_ref[:, cols(kv)], bias)

    def add_pages(update, request, start, pages, masked, kvs=range(kv_count)):
        bias = page_bias(lists, request, start, pages) if masked else None
        for kv in kvs:
            keys = page_group(lists, kc_ref, request, start, pages, kv)
            values = page_group(lists, vc_ref, request, start, pages, kv)
            update(request, kv, keys, values, bias)

    add_fresh(add)
    fetch.wait()

    def attend_request(request, carry):
        total = lists[requests + request, 0]
        count = jnp.maximum(total - early, 0)
        whole = jnp.maximum(count - 1, 0) // STEP_PAGES

        def step(index, carry):
            add_pages(add, request, early + index * STEP_PAGES, STEP_PAGES, False)
            return carry

        for start in range(later, early, STEP_PAGES):

            @pl.when(total > start)
            def _():
                add_pages(add, request, start, STEP_PAGES, True, range(done_kv, kv_count))

        lax.fori_loop(0, whole, step, 0)
        done = whole * STEP_PAGES
        rest = count - done

        @pl.when((rest > 0) & (rest <= TAIL_PAGES))
        def _():
            add_pages(add, request, early + done, TAIL_PAGES, True)

        @pl.when(rest > TAIL_PAGES)
        def _():
            add_pages(add, request, early + done, STEP_PAGES, True)

        safe = [
            acc_ref[request, kv, HEAD_DIM : HEAD_DIM + 1, :] < LIMIT for kv in range(kv_count)
        ]
        if late:
            floats = joined_queries(qt_ref, request, kv_count - 1, per_kv).astype(jnp.float32)
            norms = jnp.sum(floats * floats, axis=0, keepdims=True) * jnp.max(peak_ref[...])
            power = (jnp.sqrt(norms) - m_ref[request, kv_count - 1, 0:1, :]) * EXP2_SCALE
            safe.append(power < SAFE_POWER)
        unsafe = jnp.max(
            jnp.concatenate([jnp.where(flags, 0.0, 1.0) for flags in safe], axis=0)
        )

        @pl.when(unsafe > 0.0)
        def _():
            acc_ref[request] = jnp.zeros_like(acc_ref[request])
            m_ref[request] = jnp.full_like(m_ref[request], EMPTY)

            @pl.when(request == home)
            def _():
                add_fresh(add_running)

            def step(index, carry):
                add_pages(add_running, request, index * TAIL_PAGES, TAIL_PAGES, True)
                return carry

            lax.fori_loop(0, (total + TAIL_PAGES - 1) // TAIL_PAGES, step, 0)
            if late:
                row = lax.broadcasted_iota(jnp.int32, left_list_ref.shape, 0)
                left_list_ref[...] = jnp.where(row == request, 0, left_list_ref[...])

        for kv in range(done_kv):
            settle(
                acc_ref[request, kv],
                m_ref[request, kv, 0:1, :],
                request,
                part_refs[kv],
                ls_refs[kv],
                per_kv,
            )
        if late:
            left_ref[request] = acc_ref[request, done_kv]
            left_m_ref[request] = m_ref[request, done_kv]
        return carry

    lax.fori_loop(0, requests, attend_request, 0)


def attend(
    packed, queries_t, fresh_k, fresh_v, key_cache, value_cache, early_sums, peak, early, later
):
    blocks, kv_count, q_rows, _ = queries_t.shape
    late = early > 0
    done_kv = kv_count - 1 if late else kv_count
    q_rows -= EXTRA
    per_kv = q_rows // HEAD_DIM
    pages, _, kv_cols = key_cache.shape
    tok_rows = fresh_k.shape[0]
    requests = blocks // BLOCKS
    width = per_kv * ADDED_TOKENS
    vmem = pl.BlockSpec(memory_space=pltpu.VMEM)
    out_shape = [jax.ShapeDtypeStruct((blocks, q_rows, BLOCK), jnp.bfloat16)] * done_kv
    out_shape += [jax.ShapeDtypeStruct((blocks, LINES, BLOCK), jnp.float32)] * done_kv
    operands = [packed, queries_t, fresh_k, fresh_v, key_cache, value_cache]
    if late:
        out_shape += [
            jax.ShapeDtypeStruct((requests, HEAD_DIM + EXTRA, width), jnp.float32),
            jax.ShapeDtypeStruct((requests, LINES, width), jnp.float32),
            jax.ShapeDtypeStruct(packed.shape, packed.dtype),
        ]
        operands += [early_sums, peak]
    return pl.pallas_call(
        functools.partial(attend_kernel, per_kv, tok_rows, late, early, later),
        out_shape=tuple(out_shape),
        in_specs=[vmem] * len(operands),
        out_specs=(vmem,) * len(out_shape),
        scratch_shapes=[
            pltpu.SMEM(packed.shape, packed.dtype),
            pltpu.VMEM((requests, kv_count, LINES, width), jnp.float32),
            pltpu.VMEM((requests, kv_count, HEAD_DIM + EXTRA, width), jnp.float32),
            pltpu.SemaphoreType.DMA(()),
        ],
        compiler_params=pltpu.CompilerParams(vmem_limit_bytes=28 << 20),
        cost_estimate=pl.CostEstimate(
            flops=4 * pages * PAGE_ROWS * ADDED_TOKENS * q_rows * kv_count,
            bytes_accessed=4 * pages * PAGE_ROWS * kv_cols,
            transcendentals=pages * PAGE_ROWS * ADDED_TOKENS * per_kv * kv_count,
        ),
    )(*operands)


def page_lists(lengths_ref, groups_ref, prompt_ref, own_ref, packed_ref, pages_dev, me):
    count = PROMPT_PAGES + own_ref.shape[1]
    position = lax.broadcasted_iota(jnp.int32, (1, count), 1)
    owned, pages, lives = [], [], []
    for request in range(REQUESTS):
        prompt = prompt_ref[0:1, :]
        for group in range(1, GROUPS):
            prompt = jnp.where(groups_ref[request] == group, prompt_ref[group : group + 1, :], prompt)
        slots = jnp.concatenate([prompt, own_ref[request : request + 1, :]], axis=1)
        own_len = lengths_ref[request] - PROMPT_PAGES * PAGE_ROWS
        live = jnp.clip(own_len - (position - PROMPT_PAGES) * PAGE_ROWS, 0, PAGE_ROWS)
        live = jnp.where(position < PROMPT_PAGES, PAGE_ROWS, live)
        page = slots - me * pages_dev
        owned.append((page >= 0) & (page < pages_dev) & (live > 0))
        pages.append(page)
        lives.append(live)
    earlier = lax.broadcasted_iota(jnp.int32, (count, count), 0)
    earlier = earlier < lax.broadcasted_iota(jnp.int32, (count, count), 1)
    earlier = jnp.where(earlier, 1.0, 0.0).astype(jnp.bfloat16)
    place = lax.broadcasted_iota(jnp.int32, (PAGE_ROWS, count), 0).astype(jnp.float32)
    packed_ref[...] = jnp.zeros_like(packed_ref)
    for request in range(REQUESTS):
        mark = jnp.where(owned[request], 1.0, 0.0)
        marks = jnp.broadcast_to(mark, (EXTRA, count)).astype(jnp.bfloat16)
        before = jnp.dot(marks, earlier, preferred_element_type=jnp.float32)[0:1]
        before = jnp.where(owned[request], before, -1.0)
        onehot = jnp.where(before == place, 1.0, 0.0).astype(jnp.bfloat16)

        def pick(line):
            line = jnp.where(owned[request], line, 0).astype(jnp.float32)
            lines = jnp.broadcast_to(line, (EXTRA, count)).astype(jnp.bfloat16)
            return dot_nt(lines, onehot)[0:1]

        packed = pick(pages[request]) * 256.0 + pick(lives[request])
        packed_ref[request : request + 1, :] = packed.astype(jnp.int32)
        total = jnp.sum(mark, axis=1, keepdims=True)
        packed_ref[REQUESTS + request : REQUESTS + request + 1, :] = jnp.broadcast_to(
            total, (1, PAGE_ROWS)
        ).astype(jnp.int32)


def greet(peers):
    barrier = pltpu.get_barrier_semaphore()
    for peer in peers:
        pl.semaphore_signal(barrier, inc=1, device_id=peer, device_id_type=MESH)


def greeted(count):
    pl.semaphore_wait(pltpu.get_barrier_semaphore(), count)


def remote(source, target, send_sem, recv_sem, peer):
    return pltpu.make_async_remote_copy(
        src_ref=source,
        dst_ref=target,
        send_sem=send_sem,
        recv_sem=recv_sem,
        device_id=peer,
        device_id_type=MESH,
    )


def spread_columns(w_hbm, start, target, tensor_count, send_sem, recv_sem):
    me = lax.axis_index("seq")
    tensor = lax.axis_index("tensor")
    rows, columns = target.shape[1:]

    def block(owner):
        first = pl.multiple_of(owner * columns, columns)
        return w_hbm.at[pl.ds(start, rows), pl.ds(first, columns)]

    copies = [pltpu.make_async_copy(block(tensor), target.at[tensor], send_sem.at[0])]
    for distance in range(1, tensor_count):
        owner = (tensor + distance) % tensor_count
        copies.append(
            remote(
                block(owner),
                target.at[tensor],
                send_sem.at[distance],
                recv_sem.at[distance],
                (me, owner),
            )
        )
    return copies


def gather_kernel(seq_count, early, *refs):
    refs = list(refs)
    x_ref, gain_hbm, wq_ref, wk_ref, wv_ref, kc_hbm, vc_hbm, w_hbm = refs[:8]
    small_hbm = refs[8:12]
    qt_ref, fk_ref, fv_ref, packed_ref, kc_ref, vc_ref, w_cols = refs[12:19]
    del refs[:19]
    if early:
        sums_ref, peak_ref = refs[:2]
        del refs[:2]
    q_send, q_recv, qy_send, qy_recv, wq_buf, wk_buf, wv_buf, x_buf = refs[:8]
    load_sem, lists, gain_ref, lengths_ref, groups_ref, prompt_ref, own_ref = refs[8:15]
    w_send, w_recv = refs[15:]
    loads = [
        pltpu.make_async_copy(source, target, load_sem.at[index])
        for index, (source, target) in enumerate(
            (
                (x_ref, x_buf),
                (wk_ref, wk_buf),
                (wq_ref, wq_buf),
                (wv_ref, wv_buf),
                (kc_hbm, kc_ref),
                (vc_hbm, vc_ref),
                (packed_ref, lists),
                (gain_hbm, gain_ref),
                (small_hbm[0], lengths_ref),
                (small_hbm[1], groups_ref),
                (small_hbm[2], prompt_ref),
                (small_hbm[3], own_ref),
            )
        )
    ]
    small = loads[7:]
    for load in loads[:1] + small + loads[1:4]:
        load.start()
    me = lax.axis_index("seq")
    tensor = lax.axis_index("tensor")
    tensor_count = w_cols.shape[0]
    outer = seq_count // 2
    place, side = me // 2, me % 2
    twin = (place * 2 + 1 - side, tensor)
    kv_count = qt_ref.shape[1]
    per_kv = (qt_ref.shape[2] - EXTRA) // HEAD_DIM
    order = sorted(range(1, outer), key=lambda distance: -min(distance, outer - distance))

    def line_peer(distance):
        return (place + distance) % outer * 2 + side

    others = [(me, (tensor + distance) % tensor_count) for distance in range(1, tensor_count)]
    greet([twin] + [(line_peer(distance), tensor) for distance in range(1, outer)] + others)

    loads[0].wait()
    small[0].wait()
    floats = x_buf[...].astype(jnp.float32)
    mean = jnp.mean(floats * floats, axis=-1, keepdims=True)
    normed = (floats * lax.rsqrt(mean + 1e-05) * gain_ref[...]).astype(jnp.bfloat16)

    def project(weight):
        return jnp.dot(normed, weight, preferred_element_type=jnp.float32)

    loads[1].wait()
    keys = project(wk_buf[...])
    fk_ref[...] = keys.astype(jnp.bfloat16)
    keys_t = keys.T.astype(jnp.bfloat16)
    loads[2].wait()
    started = []

    def make(kv):
        span = per_kv * HEAD_DIM
        queries_t = project(wq_buf[:, kv * span : (kv + 1) * span]).T.astype(jnp.bfloat16)
        qt_ref[me, kv, :span, :] = queries_t
        right = keys_t[cols(kv)].astype(jnp.float32)
        marks = [
            jnp.sum(queries_t[cols(sub)].astype(jnp.float32) * right, axis=0, keepdims=True)
            for sub in range(per_kv)
        ]
        marks.append(jnp.zeros((EXTRA - per_kv, marks[0].shape[1]), jnp.float32))
        qt_ref[me, kv, span:, :] = jnp.concatenate(marks, axis=0).astype(jnp.bfloat16)

    def launch(kv):
        own = qt_ref.at[me, kv]
        copy = remote(own, own, qy_send.at[kv, 0], qy_recv.at[kv, 0], twin)
        copy.start()
        started.append(copy)
        for distance in order:
            peer = (line_peer(distance), tensor)
            copy = remote(own, own, q_send.at[kv, distance], q_recv.at[kv, distance], peer)
            copy.start()
            started.append(copy)

    def relay(kv, distance):
        block = qt_ref.at[line_peer(outer - distance), kv]
        remote(block, block, q_send.at[kv, distance], q_recv.at[kv, distance], twin).wait_recv()
        copy = remote(block, block, qy_send.at[kv, distance], qy_recv.at[kv, distance], twin)
        copy.start()
        started.append(copy)

    def arrive(kv):
        for distance in [0] + order:
            block = qt_ref.at[(place + outer - distance) % outer * 2 + 1 - side, kv]
            remote(block, block, qy_send.at[kv, distance], qy_recv.at[kv, distance], twin).wait_recv()

    make(0)
    greeted(outer + tensor_count - 1)
    launch(0)
    for load in loads[4:6]:
        load.start()
    spread = spread_columns(w_hbm, 0, w_cols, tensor_count, w_send, w_recv)
    for copy in spread:
        copy.start()
    for kv in range(1, kv_count):
        make(kv)
    loads[3].wait()
    fv_ref[...] = project(wv_buf[...]).astype(jnp.bfloat16)
    for load in small[1:]:
        load.wait()
    page_lists(lengths_ref, groups_ref, prompt_ref, own_ref, packed_ref, kc_ref.shape[0], me)
    for distance in order:
        relay(0, distance)
    for kv in range(1, kv_count):
        launch(kv)
    loads[6].start()
    for load in loads[4:7]:
        load.wait()
    waiting = [(kv, distance) for kv in range(1, kv_count) for distance in order]
    if early:
        peak = jnp.zeros((PAGE_ROWS, 1), jnp.float32)
        for page in range(kc_ref.shape[0]):
            floats = kc_ref[page, :, cols(kv_count - 1)].astype(jnp.float32)
            peak = jnp.maximum(peak, jnp.sum(floats * floats, axis=1, keepdims=True))
        peak_ref[...] = jnp.broadcast_to(peak, peak_ref.shape)
        arrive(0)
        marks = [joined_marks(qt_ref, request, 0, per_kv) for request in range(REQUESTS)]
        for step in range(early // STEP_PAGES):
            for request in range(REQUESTS):
                fresh = early_terms(
                    lists, qt_ref, kc_ref, vc_ref, marks[request], request, step, 0, per_kv
                )
                if step == 0:
                    sums_ref[request] = fresh
                else:
                    sums_ref[request] += fresh
                if waiting:
                    relay(*waiting.pop(0))
    else:
        arrive(0)
    for kv, distance in waiting:
        relay(kv, distance)
    for kv in range(1, kv_count):
        arrive(kv)
    for copy in spread:
        copy.wait()
    for copy in started:
        copy.wait_send()


def gather(
    hidden_in,
    norm_gain,
    query_weight,
    key_weight,
    value_weight,
    key_cache,
    value_cache,
    cached_lengths,
    group_ids,
    prompt_pages,
    own_pages,
    out_weight,
    seq_count,
    tensor_count,
    early,
):
    tok_rows = hidden_in.shape[0]
    q_cols, kv_cols = query_weight.shape[1], key_weight.shape[1]
    kv_count = kv_cols // HEAD_DIM
    per_kv = q_cols // kv_cols
    slots = pltpu.SemaphoreType.DMA((kv_count, seq_count // 2))
    vmem = pl.BlockSpec(memory_space=pltpu.VMEM)
    hbm = pl.BlockSpec(memory_space=pltpu.HBM)
    fresh = jax.ShapeDtypeStruct((tok_rows, kv_cols), jnp.bfloat16)
    rows = per_kv * HEAD_DIM + EXTRA
    out_shape = [
        jax.ShapeDtypeStruct((seq_count, kv_count, rows, tok_rows), jnp.bfloat16),
        fresh,
        fresh,
        jax.ShapeDtypeStruct((LINES, PAGE_ROWS), jnp.int32),
        jax.ShapeDtypeStruct(key_cache.shape, key_cache.dtype),
        jax.ShapeDtypeStruct(value_cache.shape, value_cache.dtype),
        jax.ShapeDtypeStruct(
            (tensor_count, per_kv * HEAD_DIM, out_weight.shape[1] // tensor_count), jnp.bfloat16
        ),
    ]
    if early:
        sums = (REQUESTS, HEAD_DIM + EXTRA, per_kv * ADDED_TOKENS)
        out_shape += [
            jax.ShapeDtypeStruct(sums, jnp.float32),
            jax.ShapeDtypeStruct((PAGE_ROWS, HEAD_DIM), jnp.float32),
        ]
    return pl.pallas_call(
        functools.partial(gather_kernel, seq_count, early),
        out_shape=tuple(out_shape),
        in_specs=[hbm] * 12,
        out_specs=(vmem,) * len(out_shape),
        scratch_shapes=[slots] * 4
        + [
            pltpu.VMEM(weight.shape, weight.dtype)
            for weight in (query_weight, key_weight, value_weight, hidden_in)
        ]
        + [
            pltpu.SemaphoreType.DMA((12,)),
            pltpu.SMEM((LINES, PAGE_ROWS), jnp.int32),
            pltpu.VMEM((1, norm_gain.shape[0]), norm_gain.dtype),
            pltpu.SMEM(cached_lengths.shape, jnp.int32),
            pltpu.SMEM(group_ids.shape, jnp.int32),
            pltpu.VMEM(prompt_pages.shape, jnp.int32),
            pltpu.VMEM(own_pages.shape, jnp.int32),
            pltpu.SemaphoreType.DMA((tensor_count,)),
            pltpu.SemaphoreType.DMA((tensor_count,)),
        ],
        compiler_params=pltpu.CompilerParams(
            collective_id=0, has_side_effects=True, vmem_limit_bytes=40 << 20
        ),
    )(
        in_hbm(hidden_in),
        in_hbm(norm_gain.reshape(1, -1)),
        in_hbm(query_weight),
        in_hbm(key_weight),
        in_hbm(value_weight),
        in_hbm(key_cache),
        in_hbm(value_cache),
        in_hbm(out_weight),
        in_hbm(cached_lengths),
        in_hbm(group_ids),
        in_hbm(prompt_pages),
        in_hbm(own_pages),
    )


def finish_kernel(seq_count, tensor_count, kv_count, early, *refs):
    refs = list(refs)
    known = kv_count - 1 if early else kv_count
    part_refs, ls_refs = refs[:known], refs[known : 2 * known]
    del refs[: 2 * known]
    if early:
        left_ref, left_m_ref, packed_ref, qt_ref, kc_ref, vc_ref = refs[:6]
        del refs[:6]
    w_early, w_hbm, out_ref = refs[:3]
    mix_ref, mix_got, mls_ref, side_got, sls_ref, gls_ref = refs[3:9]
    w_late, att_ref = refs[9:11]
    side_send, side_recv, sls_send, sls_recv, mix_send, mix_recv, mls_send, mls_recv = refs[11:19]
    w_send, w_recv, far_send, far_recv, near_send, near_recv = refs[19:25]
    del refs[:25]
    if early:
        late_ref, lists, list_sem = refs[2:]
        part_refs = part_refs + refs[:1]
        ls_refs = ls_refs + refs[1:2]
        fetch = pltpu.make_async_copy(packed_ref, lists, list_sem)
        fetch.start()
    tok_rows, out_cols = out_ref.shape
    per_kv = part_refs[0].shape[1] // HEAD_DIM
    me = lax.axis_index("seq")
    tensor = lax.axis_index("tensor")
    pair, core = tensor // 2, tensor % 2
    pairs = tensor_count // 2
    twin = (me, pair * 2 + 1 - core)
    outer = seq_count // 2
    place, side = me // 2, me % 2
    beside = (place * 2 + 1 - side, tensor)
    order = sorted(range(1, outer), key=lambda distance: -min(distance, outer - distance))

    def far_pair(distance):
        return (pair + distance) % pairs

    def line(distance, which):
        return (place + distance) % outer * 2 + which

    greet(
        [beside]
        + [(line(distance, side), tensor) for distance in range(1, outer)]
        + [twin]
        + [(me, far_pair(distance) * 2 + core) for distance in range(1, pairs)]
        + [(me, far_pair(distance) * 2 + 1 - core) for distance in range(1, pairs)]
    )
    greeted(outer + tensor_count - 1)
    started = []
    scales, sides, mixes, mix_scales, shares = {}, {}, {}, {}, {}

    def begin(table, key, *rest):
        table[key] = remote(*rest)
        table[key].start()
        started.append(table[key])

    def send_sides(kv):
        for distance in order + [0]:
            begin(
                scales,
                (kv, distance),
                ls_refs[kv].at[line(distance, 1 - side)],
                sls_ref.at[kv, distance],
                sls_send.at[kv, distance],
                sls_recv.at[kv, distance],
                beside,
            )
        for distance in order + [0]:
            begin(
                sides,
                (kv, distance),
                part_refs[kv].at[line(distance, 1 - side)],
                side_got.at[kv, distance],
                side_send.at[kv, distance],
                side_recv.at[kv, distance],
                beside,
            )

    def weighted(block, share):
        return [
            block[cols(sub)].astype(jnp.float32) * share[sub : sub + 1] for sub in range(per_kv)
        ]

    def plus(left, right):
        return [one + other for one, other in zip(left, right)]

    def weigh(kv):
        for distance in order + [0]:
            scales[kv, distance].wait_recv()
        own_lines = jnp.stack([ls_refs[kv][line(distance, side)] for distance in range(outer)])
        side_lines = sls_ref[kv]
        top = jnp.maximum(own_lines, side_lines)
        own_scale, side_scale = jnp.exp(own_lines - top), jnp.exp(side_lines - top)
        both = own_scale + side_scale
        mls_ref[kv] = top + jnp.log(both)
        for distance in order:
            begin(
                mix_scales,
                (kv, distance),
                mls_ref.at[kv, distance],
                gls_ref.at[kv, distance],
                mls_send.at[kv, distance],
                mls_recv.at[kv, distance],
                (line(distance, side), tensor),
            )
        shares[kv] = own_scale / both, side_scale / both

    def mixed(kv, distance):
        sides[kv, distance].wait_recv()
        own_shares, side_shares = shares[kv]
        return plus(
            weighted(part_refs[kv][line(distance, side)], own_shares[distance]),
            weighted(side_got[kv, distance], side_shares[distance]),
        )

    def send_mix(kv, distance):
        mix_ref[kv, distance] = jnp.concatenate(mixed(kv, distance), axis=0).astype(jnp.bfloat16)
        begin(
            mixes,
            (kv, distance),
            mix_ref.at[kv, distance],
            mix_got.at[kv, distance],
            mix_send.at[kv, distance],
            mix_recv.at[kv, distance],
            (line(distance, side), tensor),
        )

    def merged(kv):
        gls_ref[kv, 0] = mls_ref[kv, 0]
        for distance in order:
            mix_scales[kv, distance].wait_recv()
        lines = gls_ref[kv]
        lines = jnp.exp(lines - jnp.max(lines, axis=0, keepdims=True))
        share = lines / jnp.sum(lines, axis=0, keepdims=True)
        total = [block * share[0][sub : sub + 1] for sub, block in enumerate(mixed(kv, 0))]
        for distance in order:
            mixes[kv, distance].wait_recv()
            total = plus(total, weighted(mix_got[kv, distance], share[distance]))
        return jnp.concatenate(total, axis=0).astype(jnp.bfloat16)

    def twin_copy(kv, distance, which):
        block = att_ref.at[(pair + pairs - distance) % pairs * 2 + which, kv]
        return remote(block, block, near_send.at[kv, distance], near_recv.at[kv, distance], twin)

    def far_copy(kv, distance, source, target):
        block = att_ref.at[source, kv]
        return remote(
            block, block, far_send.at[kv, distance], far_recv.at[kv, distance], (me, target)
        )

    def share_out(kv, attention):
        att_ref[tensor, kv] = attention
        copies = [
            far_copy(kv, distance, tensor, far_pair(distance) * 2 + core)
            for distance in range(1, pairs)
        ]
        copies.append(twin_copy(kv, 0, core))
        for copy in copies:
            copy.start()
            started.append(copy)

    def pass_on(kv):
        for distance in range(1, pairs):
            source = far_pair(pairs - distance) * 2 + core
            far_copy(kv, distance, source, source).wait_recv()
            copy = twin_copy(kv, distance, core)
            copy.start()
            started.append(copy)

    def terms_of(kv, source):
        rest = (kv - 1) * per_kv * HEAD_DIM
        if kv == 0:
            weight = w_early[source]
        else:
            weight = w_late[source, rest : rest + per_kv * HEAD_DIM, :]
        return lax.dot_general(
            att_ref[source, kv],
            weight,
            (((0,), (0,)), ((), ())),
            preferred_element_type=jnp.float32,
        )

    def own_terms(kv):
        return terms_of(kv, tensor)

    def far_terms(kv):
        total = None
        for distance in range(1, pairs):
            fresh = terms_of(kv, far_pair(distance) * 2 + core)
            total = fresh if total is None else total + fresh
        return total

    def twin_terms(kv):
        total = None
        for distance in range(pairs):
            twin_copy(kv, distance, 1 - core).wait_recv()
            fresh = terms_of(kv, (pair + pairs - distance) % pairs * 2 + 1 - core)
            total = fresh if total is None else total + fresh
        return total

    last = kv_count - 1
    for kv in range(known):
        send_sides(kv)
    spread = spread_columns(w_hbm, per_kv * HEAD_DIM, w_late, tensor_count, w_send, w_recv)
    for copy in spread:
        copy.start()
    if early:
        fetch.wait()
        ls_refs[last][...] = jnp.zeros_like(ls_refs[last])
        steps = [
            (step, request)
            for step in range(early // STEP_PAGES)
            for request in range(REQUESTS)
        ]
        tasks = [(weigh, (kv,)) for kv in range(known)]
        tasks += [(send_mix, (kv, distance)) for kv in range(known) for distance in order]
        share_of = -(-len(tasks) // len(steps))
        for step, request in steps:
            late_ref[request] = (left_ref if step == 0 else late_ref)[request] + early_terms(
                lists,
                qt_ref,
                kc_ref,
                vc_ref,
                left_m_ref[request, 0:1, :],
                request,
                step,
                last,
                per_kv,
            )
            for run, given in tasks[:share_of]:
                run(*given)
            del tasks[:share_of]
        for request in range(REQUESTS):
            settle(
                late_ref[request],
                left_m_ref[request, 0:1, :],
                request,
                part_refs[last],
                ls_refs[last],
                per_kv,
            )
        send_sides(last)
        ready = known
    else:
        ready = 0
    for kv in range(ready, kv_count):
        weigh(kv)
        for distance in order:
            send_mix(kv, distance)
    for kv in range(last):
        share_out(kv, merged(kv))
        pass_on(kv)
    share_out(last, merged(last))
    for copy in spread:
        copy.wait()
    result = own_terms(last)
    for kv in range(last):
        result = result + own_terms(kv) + far_terms(kv) + twin_terms(kv)
    pass_on(last)
    result = result + far_terms(last) + twin_terms(last)
    out_ref[...] = result.astype(jnp.bfloat16)
    for copy in started:
        copy.wait_send()


def finish(parts, scales, leftovers, w_cols, out_weight, seq_count, tensor_count, early):
    q_rows, tok_rows = parts[0].shape[1:]
    kv_count = len(parts) + (1 if early else 0)
    out_cols = out_weight.shape[1] // tensor_count
    pairs = tensor_count // 2
    outer = seq_count // 2
    vmem = pl.BlockSpec(memory_space=pltpu.VMEM)
    w_block = (tensor_count, out_weight.shape[0] - w_cols.shape[1], out_cols)
    att_block = (tensor_count, kv_count, q_rows, tok_rows)
    part_buf = pltpu.VMEM((kv_count, outer, q_rows, tok_rows), jnp.bfloat16)
    scale_buf = pltpu.VMEM((kv_count, outer, LINES, tok_rows), jnp.float32)
    line_sems = pltpu.SemaphoreType.DMA((kv_count, outer))
    pair_sems = pltpu.SemaphoreType.DMA((kv_count, pairs))
    w_sems = pltpu.SemaphoreType.DMA((tensor_count,))
    operands = list(parts) + list(scales) + list(leftovers) + [w_cols, in_hbm(out_weight)]
    scratch = [part_buf, part_buf, scale_buf, part_buf, scale_buf, scale_buf]
    scratch += [pltpu.VMEM(w_block, jnp.bfloat16), pltpu.VMEM(att_block, jnp.bfloat16)]
    scratch += [line_sems] * 8 + [w_sems] * 2 + [pair_sems] * 4
    if early:
        scratch += [
            pltpu.VMEM(parts[0].shape, parts[0].dtype),
            pltpu.VMEM(scales[0].shape, scales[0].dtype),
            pltpu.VMEM(leftovers[0].shape, leftovers[0].dtype),
            pltpu.SMEM(leftovers[2].shape, leftovers[2].dtype),
            pltpu.SemaphoreType.DMA(()),
        ]
    return pl.pallas_call(
        functools.partial(finish_kernel, seq_count, tensor_count, kv_count, early),
        out_shape=jax.ShapeDtypeStruct((tok_rows, out_cols), jnp.bfloat16),
        in_specs=[vmem] * (len(operands) - 1) + [pl.BlockSpec(memory_space=pltpu.HBM)],
        out_specs=vmem,
        scratch_shapes=scratch,
        compiler_params=pltpu.CompilerParams(
            collective_id=1, has_side_effects=True, vmem_limit_bytes=32 << 20
        ),
    )(*operands)


def regroup(array, rows):
    count, width = array.shape[0], array.shape[-1]
    if width == rows:
        return array
    array = jnp.moveaxis(array, 0, -2)
    array = array.reshape(array.shape[:-2] + (count * width // rows, rows))
    return jnp.moveaxis(array, -2, 0)


def body(
    hidden_in,
    norm_gain,
    query_weight,
    key_weight,
    value_weight,
    out_weight,
    key_cache,
    value_cache,
    cached_lengths,
    group_ids,
    prompt_pages,
    own_pages,
):
    tok_rows = hidden_in.shape[0]
    seq_count = lax.axis_size("seq")
    kv_count = key_weight.shape[1] // HEAD_DIM
    split = tok_rows == BLOCK and kv_count > 1
    early = EARLY_STEPS * STEP_PAGES if split else 0
    later = LATE_STEPS * STEP_PAGES if split else 0
    tensor_count = lax.axis_size("tensor")
    queries_t, fresh_k, fresh_v, packed, keys, values, w_cols, *rest = gather(
        hidden_in,
        norm_gain,
        query_weight,
        key_weight,
        value_weight,
        key_cache,
        value_cache,
        cached_lengths,
        group_ids,
        prompt_pages,
        own_pages,
        out_weight,
        seq_count,
        tensor_count,
        early,
    )
    queries_t = regroup(queries_t, BLOCK)
    sums, peak = rest if early else (None, None)
    found = attend(
        packed, queries_t, fresh_k, fresh_v, keys, values, sums, peak, early, later
    )
    known = kv_count - 1 if early else kv_count
    parts = [regroup(array, tok_rows) for array in found[:known]]
    scales = [regroup(array, tok_rows) for array in found[known : 2 * known]]
    leftovers = list(found[2 * known :])
    if early:
        leftovers += [queries_t, keys, values]
    return finish(
        parts, scales, leftovers, w_cols, out_weight, seq_count, tensor_count, later
    )


def solution(mesh):
    in_specs = (
        P("seq", None),
        P(),
        P(None, "tensor"),
        P(None, "tensor"),
        P(None, "tensor"),
        P("tensor", None),
        P("seq", None, "tensor"),
        P("seq", None, "tensor"),
        P(),
        P(),
        P(),
        P(),
    )
    out_specs = P("seq", "tensor")
    return jax.shard_map(body, mesh=mesh, in_specs=in_specs, out_specs=out_specs, check_vma=False)
```

```python
import functools
import math

import jax
import jax.numpy as jnp
from jax import lax
from jax.experimental import pallas as pl
from jax.experimental.pallas import tpu as pltpu
from jax.sharding import PartitionSpec as P

HEAD_DIM = 128
PAGE_ROWS = 128
ADDED_TOKENS = 512
GROUPS = 2
PROMPT_PAGES = 128
STEP_PAGES = 8
TAIL_PAGES = 4
BLOCK = 128
EXTRA = 16
REQUESTS = 2
LIMIT = 1e30
EARLY_STEPS = 3
LATE_STEPS = 3
SAFE_POWER = 100.0
SCORE_SCALE = 1.0 / math.sqrt(HEAD_DIM)
EXP2_SCALE = SCORE_SCALE * math.log2(math.e)
EMPTY = -1e30
SHIFT = 60.0 / EXP2_SCALE
BLOCKS = ADDED_TOKENS // BLOCK
LINES = 8
MESH = pl.DeviceIdType.MESH


def in_hbm(array):
    return pltpu.with_memory_space_constraint(array, pltpu.HBM)


def dot_nt(left, right):
    return lax.dot_general(
        left, right, (((1,), (1,)), ((), ())), preferred_element_type=jnp.float32
    )


def cols(index):
    return slice(index * HEAD_DIM, (index + 1) * HEAD_DIM)


def joined_queries(qt_ref, request, kv, per_kv):
    return jnp.concatenate(
        [
            qt_ref[request * BLOCKS + block, kv, cols(sub), :]
            for sub in range(per_kv)
            for block in range(BLOCKS)
        ],
        axis=1,
    )


def joined_marks(qt_ref, request, kv, per_kv):
    rows = [
        qt_ref[request * BLOCKS + block, kv, per_kv * HEAD_DIM :, :].astype(jnp.float32)[
            sub : sub + 1
        ]
        for sub in range(per_kv)
        for block in range(BLOCKS)
    ]
    return jnp.concatenate(rows, axis=1) + SHIFT


def values_t(values):
    ones = jnp.ones((EXTRA, values.shape[0]), jnp.bfloat16)
    return jnp.concatenate([values.T, ones], axis=0)


def page_group(lists, cache_ref, request, start, pages, kv):
    last = cache_ref.shape[0] - 1
    slots = [jnp.clip(lists[request, start + page] >> 8, 0, last) for page in range(pages)]
    return jnp.concatenate([cache_ref[slot, :, cols(kv)] for slot in slots], axis=0)


def page_bias(lists, request, start, pages):
    place = lax.broadcasted_iota(jnp.int32, (PAGE_ROWS, 1), 0)
    return jnp.concatenate(
        [
            jnp.where(place < (lists[request, start + page] & 255), 0.0, EMPTY)
            for page in range(pages)
        ],
        axis=0,
    )


def terms(queries, mark, keys, values, bias):
    scores = jnp.dot(keys, queries, preferred_element_type=jnp.float32)
    if bias is not None:
        scores = scores + bias
    weights = jnp.exp2((scores - mark) * EXP2_SCALE).astype(jnp.bfloat16)
    return jnp.dot(values_t(values), weights, preferred_element_type=jnp.float32)


def early_terms(lists, qt_ref, kc_ref, vc_ref, mark, request, step, kv, per_kv):
    start = step * STEP_PAGES
    return terms(
        joined_queries(qt_ref, request, kv, per_kv),
        mark,
        page_group(lists, kc_ref, request, start, STEP_PAGES, kv),
        page_group(lists, vc_ref, request, start, STEP_PAGES, kv),
        page_bias(lists, request, start, STEP_PAGES),
    )


def settle(sums, top, request, part_ref, ls_ref, per_kv):
    den = sums[HEAD_DIM : HEAD_DIM + 1]
    alive = (den > 0.0) & (top > 0.5 * EMPTY)
    den = jnp.where(alive, den, 1.0)
    scale = jnp.where(alive, top * SCORE_SCALE + jnp.log(den), EMPTY)
    parts = (sums[:HEAD_DIM] * jnp.where(alive, 1.0 / den, 0.0)).astype(jnp.bfloat16)
    for sub in range(per_kv):
        for block in range(BLOCKS):
            place = sub * BLOCKS + block
            span = slice(place * BLOCK, (place + 1) * BLOCK)
            part_ref[request * BLOCKS + block, cols(sub), :] = parts[:, span]
            ls_ref[request * BLOCKS + block, sub : sub + 1, :] = scale[:, span]


def attend_kernel(per_kv, tok_rows, late, early, later, *refs):
    refs = list(refs)
    packed_ref, qt_ref, fk_ref, fv_ref, kc_ref, vc_ref = refs[:6]
    del refs[:6]
    if late:
        start_ref, peak_ref = refs[:2]
        del refs[:2]
    kv_count = kc_ref.shape[2] // HEAD_DIM
    done_kv = kv_count - 1 if late else kv_count
    part_refs, ls_refs = refs[:done_kv], refs[done_kv : 2 * done_kv]
    del refs[: 2 * done_kv]
    if late:
        left_ref, left_m_ref, left_list_ref = refs[:3]
        del refs[:3]
    lists, m_ref, acc_ref, list_sem = refs
    fetch = pltpu.make_async_copy(packed_ref, lists, list_sem)
    fetch.start()
    requests = acc_ref.shape[0]
    width = per_kv * ADDED_TOKENS
    for ls_ref in ls_refs:
        ls_ref[...] = jnp.zeros_like(ls_ref)
    for kv in range(kv_count):
        for request in range(requests):
            if late and kv == 0:
                acc_ref[request, kv] = start_ref[request]
            else:
                acc_ref[request, kv] = jnp.zeros_like(acc_ref[request, kv])
            m_ref[request, kv, 0:1, :] = joined_marks(qt_ref, request, kv, per_kv)
    if late:
        left_list_ref[...] = packed_ref[...]

    def add(request, kv, keys, values, bias):
        queries = joined_queries(qt_ref, request, kv, per_kv)
        acc_ref[request, kv] += terms(queries, m_ref[request, kv, 0:1, :], keys, values, bias)

    def add_running(request, kv, keys, values, bias):
        queries = joined_queries(qt_ref, request, kv, per_kv)
        scores = jnp.dot(keys, queries, preferred_element_type=jnp.float32) + bias
        old = m_ref[request, kv, 0:1, :]
        new = jnp.maximum(old, jnp.max(scores, axis=0, keepdims=True))
        m_ref[request, kv, 0:1, :] = new
        weights = jnp.exp2((scores - new) * EXP2_SCALE)
        acc_ref[request, kv] = acc_ref[request, kv] * jnp.exp2((old - new) * EXP2_SCALE) + jnp.dot(
            values_t(values), weights.astype(jnp.bfloat16), preferred_element_type=jnp.float32
        )

    first = lax.axis_index("seq") * tok_rows
    home = first // ADDED_TOKENS

    def add_fresh(update):
        row = lax.broadcasted_iota(jnp.int32, (tok_rows, width), 0) + (first - home * ADDED_TOKENS)
        col = lax.broadcasted_iota(jnp.int32, (tok_rows, width), 1) % ADDED_TOKENS
        bias = jnp.where(row <= col, 0.0, EMPTY)
        for kv in range(kv_count):
            update(home, kv, fk_ref[:, cols(kv)], fv_ref[:, cols(kv)], bias)

    def add_pages(update, request, start, pages, masked, kvs=range(kv_count)):
        bias = page_bias(lists, request, start, pages) if masked else None
        for kv in kvs:
            keys = page_group(lists, kc_ref, request, start, pages, kv)
            values = page_group(lists, vc_ref, request, start, pages, kv)
            update(request, kv, keys, values, bias)

    add_fresh(add)
    fetch.wait()

    def attend_request(request, carry):
        total = lists[requests + request, 0]
        count = jnp.maximum(total - early, 0)
        whole = jnp.maximum(count - 1, 0) // STEP_PAGES

        def step(index, carry):
            add_pages(add, request, early + index * STEP_PAGES, STEP_PAGES, False)
            return carry

        for start in range(later, early, STEP_PAGES):

            @pl.when(total > start)
            def _():
                add_pages(add, request, start, STEP_PAGES, True, range(done_kv, kv_count))

        lax.fori_loop(0, whole, step, 0)
        done = whole * STEP_PAGES
        rest = count - done

        @pl.when((rest > 0) & (rest <= TAIL_PAGES))
        def _():
            add_pages(add, request, early + done, TAIL_PAGES, True)

        @pl.when(rest > TAIL_PAGES)
        def _():
            add_pages(add, request, early + done, STEP_PAGES, True)

        safe = [
            acc_ref[request, kv, HEAD_DIM : HEAD_DIM + 1, :] < LIMIT for kv in range(kv_count)
        ]
        if late:
            floats = joined_queries(qt_ref, request, kv_count - 1, per_kv).astype(jnp.float32)
            norms = jnp.sum(floats * floats, axis=0, keepdims=True)
            norms = norms * jnp.max(peak_ref[...], axis=0, keepdims=True)[:, 0:1]
            power = (jnp.sqrt(norms) - m_ref[request, kv_count - 1, 0:1, :]) * EXP2_SCALE
            safe.append(power < SAFE_POWER)
        unsafe = jnp.max(
            jnp.concatenate([jnp.where(flags, 0.0, 1.0) for flags in safe], axis=0)
        )

        @pl.when(unsafe > 0.0)
        def _():
            acc_ref[request] = jnp.zeros_like(acc_ref[request])
            m_ref[request] = jnp.full_like(m_ref[request], EMPTY)

            @pl.when(request == home)
            def _():
                add_fresh(add_running)

            def step(index, carry):
                add_pages(add_running, request, index * TAIL_PAGES, TAIL_PAGES, True)
                return carry

            lax.fori_loop(0, (total + TAIL_PAGES - 1) // TAIL_PAGES, step, 0)
            if late:
                row = lax.broadcasted_iota(jnp.int32, left_list_ref.shape, 0)
                left_list_ref[...] = jnp.where(row == request, 0, left_list_ref[...])

        for kv in range(done_kv):
            settle(
                acc_ref[request, kv],
                m_ref[request, kv, 0:1, :],
                request,
                part_refs[kv],
                ls_refs[kv],
                per_kv,
            )
        if late:
            left_ref[request] = acc_ref[request, done_kv]
            left_m_ref[request] = m_ref[request, done_kv]
        return carry

    lax.fori_loop(0, requests, attend_request, 0)


def attend(
    packed, queries_t, fresh_k, fresh_v, key_cache, value_cache, early_sums, peak, early, later
):
    blocks, kv_count, q_rows, _ = queries_t.shape
    late = early > 0
    done_kv = kv_count - 1 if late else kv_count
    q_rows -= EXTRA
    per_kv = q_rows // HEAD_DIM
    pages, _, kv_cols = key_cache.shape
    tok_rows = fresh_k.shape[0]
    requests = blocks // BLOCKS
    width = per_kv * ADDED_TOKENS
    vmem = pl.BlockSpec(memory_space=pltpu.VMEM)
    out_shape = [jax.ShapeDtypeStruct((blocks, q_rows, BLOCK), jnp.bfloat16)] * done_kv
    out_shape += [jax.ShapeDtypeStruct((blocks, LINES, BLOCK), jnp.float32)] * done_kv
    operands = [packed, queries_t, fresh_k, fresh_v, key_cache, value_cache]
    if late:
        out_shape += [
            jax.ShapeDtypeStruct((requests, HEAD_DIM + EXTRA, width), jnp.float32),
            jax.ShapeDtypeStruct((requests, LINES, width), jnp.float32),
            jax.ShapeDtypeStruct(packed.shape, packed.dtype),
        ]
        operands += [early_sums, peak]
    return pl.pallas_call(
        functools.partial(attend_kernel, per_kv, tok_rows, late, early, later),
        out_shape=tuple(out_shape),
        in_specs=[vmem] * len(operands),
        out_specs=(vmem,) * len(out_shape),
        scratch_shapes=[
            pltpu.SMEM(packed.shape, packed.dtype),
            pltpu.VMEM((requests, kv_count, LINES, width), jnp.float32),
            pltpu.VMEM((requests, kv_count, HEAD_DIM + EXTRA, width), jnp.float32),
            pltpu.SemaphoreType.DMA(()),
        ],
        compiler_params=pltpu.CompilerParams(vmem_limit_bytes=28 << 20),
        cost_estimate=pl.CostEstimate(
            flops=4 * pages * PAGE_ROWS * ADDED_TOKENS * q_rows * kv_count,
            bytes_accessed=4 * pages * PAGE_ROWS * kv_cols,
            transcendentals=pages * PAGE_ROWS * ADDED_TOKENS * per_kv * kv_count,
        ),
    )(*operands)


def page_lists(lengths_ref, groups_ref, prompt_ref, own_ref, packed_ref, pages_dev, me):
    count = PROMPT_PAGES + own_ref.shape[1]
    position = lax.broadcasted_iota(jnp.int32, (1, count), 1)
    owned, pages, lives = [], [], []
    for request in range(REQUESTS):
        prompt = prompt_ref[0:1, :]
        for group in range(1, GROUPS):
            prompt = jnp.where(groups_ref[request] == group, prompt_ref[group : group + 1, :], prompt)
        slots = jnp.concatenate([prompt, own_ref[request : request + 1, :]], axis=1)
        own_len = lengths_ref[request] - PROMPT_PAGES * PAGE_ROWS
        live = jnp.clip(own_len - (position - PROMPT_PAGES) * PAGE_ROWS, 0, PAGE_ROWS)
        live = jnp.where(position < PROMPT_PAGES, PAGE_ROWS, live)
        page = slots - me * pages_dev
        owned.append((page >= 0) & (page < pages_dev) & (live > 0))
        pages.append(page)
        lives.append(live)
    earlier = lax.broadcasted_iota(jnp.int32, (count, count), 0)
    earlier = earlier < lax.broadcasted_iota(jnp.int32, (count, count), 1)
    earlier = jnp.where(earlier, 1.0, 0.0).astype(jnp.bfloat16)
    place = lax.broadcasted_iota(jnp.int32, (PAGE_ROWS, count), 0).astype(jnp.float32)
    packed_ref[...] = jnp.zeros_like(packed_ref)
    for request in range(REQUESTS):
        mark = jnp.where(owned[request], 1.0, 0.0)
        marks = jnp.broadcast_to(mark, (EXTRA, count)).astype(jnp.bfloat16)
        before = jnp.dot(marks, earlier, preferred_element_type=jnp.float32)[0:1]
        before = jnp.where(owned[request], before, -1.0)
        onehot = jnp.where(before == place, 1.0, 0.0).astype(jnp.bfloat16)

        def pick(line):
            line = jnp.where(owned[request], line, 0).astype(jnp.float32)
            lines = jnp.broadcast_to(line, (EXTRA, count)).astype(jnp.bfloat16)
            return dot_nt(lines, onehot)[0:1]

        packed = pick(pages[request]) * 256.0 + pick(lives[request])
        packed_ref[request : request + 1, :] = packed.astype(jnp.int32)
        total = jnp.sum(mark, axis=1, keepdims=True)
        packed_ref[REQUESTS + request : REQUESTS + request + 1, :] = jnp.broadcast_to(
            total, (1, PAGE_ROWS)
        ).astype(jnp.int32)


def greet(peers):
    barrier = pltpu.get_barrier_semaphore()
    for peer in peers:
        pl.semaphore_signal(barrier, inc=1, device_id=peer, device_id_type=MESH)


def greeted(count):
    pl.semaphore_wait(pltpu.get_barrier_semaphore(), count)


def remote(source, target, send_sem, recv_sem, peer):
    return pltpu.make_async_remote_copy(
        src_ref=source,
        dst_ref=target,
        send_sem=send_sem,
        recv_sem=recv_sem,
        device_id=peer,
        device_id_type=MESH,
    )


def spread_columns(w_hbm, start, target, tensor_count, send_sem, recv_sem):
    me = lax.axis_index("seq")
    tensor = lax.axis_index("tensor")
    rows, columns = target.shape[1:]

    def block(owner):
        first = pl.multiple_of(owner * columns, columns)
        return w_hbm.at[pl.ds(start, rows), pl.ds(first, columns)]

    copies = [pltpu.make_async_copy(block(tensor), target.at[tensor], send_sem.at[0])]
    for distance in range(1, tensor_count):
        owner = (tensor + distance) % tensor_count
        copies.append(
            remote(
                block(owner),
                target.at[tensor],
                send_sem.at[distance],
                recv_sem.at[distance],
                (me, owner),
            )
        )
    return copies


def gather_kernel(seq_count, early, *refs):
    refs = list(refs)
    x_ref, gain_hbm, wq_ref, wk_ref, wv_ref, kc_hbm, vc_hbm, w_hbm = refs[:8]
    small_hbm = refs[8:12]
    qt_ref, fk_ref, fv_ref, packed_ref, kc_ref, vc_ref, w_cols = refs[12:19]
    del refs[:19]
    if early:
        sums_ref, peak_ref = refs[:2]
        del refs[:2]
    q_send, q_recv, qy_send, qy_recv, wq_buf, wk_buf, wv_buf, x_buf = refs[:8]
    load_sem, lists, gain_ref, lengths_ref, groups_ref, prompt_ref, own_ref = refs[8:15]
    w_send, w_recv = refs[15:]
    loads = [
        pltpu.make_async_copy(source, target, load_sem.at[index])
        for index, (source, target) in enumerate(
            (
                (x_ref, x_buf),
                (wk_ref, wk_buf),
                (wq_ref, wq_buf),
                (wv_ref, wv_buf),
                (kc_hbm, kc_ref),
                (vc_hbm, vc_ref),
                (packed_ref, lists),
                (gain_hbm, gain_ref),
                (small_hbm[0], lengths_ref),
                (small_hbm[1], groups_ref),
                (small_hbm[2], prompt_ref),
                (small_hbm[3], own_ref),
            )
        )
    ]
    small = loads[7:]
    for load in loads[:1] + small + loads[1:4]:
        load.start()
    me = lax.axis_index("seq")
    tensor = lax.axis_index("tensor")
    tensor_count = w_cols.shape[0]
    outer = seq_count // 2
    place, side = me // 2, me % 2
    twin = (place * 2 + 1 - side, tensor)
    kv_count = qt_ref.shape[1]
    per_kv = (qt_ref.shape[2] - EXTRA) // HEAD_DIM
    order = sorted(range(1, outer), key=lambda distance: -min(distance, outer - distance))

    def line_peer(distance):
        return (place + distance) % outer * 2 + side

    others = [(me, (tensor + distance) % tensor_count) for distance in range(1, tensor_count)]
    greet([twin] + [(line_peer(distance), tensor) for distance in range(1, outer)] + others)

    loads[0].wait()
    small[0].wait()
    floats = x_buf[...].astype(jnp.float32)
    mean = jnp.mean(floats * floats, axis=-1, keepdims=True)
    normed = (floats * lax.rsqrt(mean + 1e-05) * gain_ref[...]).astype(jnp.bfloat16)

    def project(weight):
        return jnp.dot(normed, weight, preferred_element_type=jnp.float32)

    loads[1].wait()
    keys = project(wk_buf[...])
    fk_ref[...] = keys.astype(jnp.bfloat16)
    keys_t = keys.T.astype(jnp.bfloat16)
    loads[2].wait()
    started = []

    def make(kv):
        span = per_kv * HEAD_DIM
        queries_t = project(wq_buf[:, kv * span : (kv + 1) * span]).T.astype(jnp.bfloat16)
        qt_ref[me, kv, :span, :] = queries_t
        right = keys_t[cols(kv)].astype(jnp.float32)
        marks = [
            jnp.sum(queries_t[cols(sub)].astype(jnp.float32) * right, axis=0, keepdims=True)
            for sub in range(per_kv)
        ]
        marks.append(jnp.zeros((EXTRA - per_kv, marks[0].shape[1]), jnp.float32))
        qt_ref[me, kv, span:, :] = jnp.concatenate(marks, axis=0).astype(jnp.bfloat16)

    def launch(kv):
        own = qt_ref.at[me, kv]
        copy = remote(own, own, qy_send.at[kv, 0], qy_recv.at[kv, 0], twin)
        copy.start()
        started.append(copy)
        for distance in order:
            peer = (line_peer(distance), tensor)
            copy = remote(own, own, q_send.at[kv, distance], q_recv.at[kv, distance], peer)
            copy.start()
            started.append(copy)

    def relay(kv, distance):
        block = qt_ref.at[line_peer(outer - distance), kv]
        remote(block, block, q_send.at[kv, distance], q_recv.at[kv, distance], twin).wait_recv()
        copy = remote(block, block, qy_send.at[kv, distance], qy_recv.at[kv, distance], twin)
        copy.start()
        started.append(copy)

    def arrive(kv):
        for distance in [0] + order:
            block = qt_ref.at[(place + outer - distance) % outer * 2 + 1 - side, kv]
            remote(block, block, qy_send.at[kv, distance], qy_recv.at[kv, distance], twin).wait_recv()

    make(0)
    greeted(outer + tensor_count - 1)
    launch(0)
    for load in loads[4:6]:
        load.start()
    spread = spread_columns(w_hbm, 0, w_cols, tensor_count, w_send, w_recv)
    for copy in spread:
        copy.start()
    for kv in range(1, kv_count):
        make(kv)
    loads[3].wait()
    fv_ref[...] = project(wv_buf[...]).astype(jnp.bfloat16)
    for load in small[1:]:
        load.wait()
    page_lists(lengths_ref, groups_ref, prompt_ref, own_ref, packed_ref, kc_ref.shape[0], me)
    for distance in order:
        relay(0, distance)
    for kv in range(1, kv_count):
        launch(kv)
    loads[6].start()
    for load in loads[4:7]:
        load.wait()
    waiting = [(kv, distance) for kv in range(1, kv_count) for distance in order]
    if early:
        peak = jnp.zeros((PAGE_ROWS, 1), jnp.float32)
        for page in range(kc_ref.shape[0]):
            floats = kc_ref[page, :, cols(kv_count - 1)].astype(jnp.float32)
            peak = jnp.maximum(peak, jnp.sum(floats * floats, axis=1, keepdims=True))
        peak_ref[...] = jnp.broadcast_to(peak, peak_ref.shape)
        arrive(0)
        marks = [joined_marks(qt_ref, request, 0, per_kv) for request in range(REQUESTS)]
        for step in range(early // STEP_PAGES):
            for request in range(REQUESTS):
                fresh = early_terms(
                    lists, qt_ref, kc_ref, vc_ref, marks[request], request, step, 0, per_kv
                )
                if step == 0:
                    sums_ref[request] = fresh
                else:
                    sums_ref[request] += fresh
                if waiting:
                    relay(*waiting.pop(0))
    else:
        arrive(0)
    for kv, distance in waiting:
        relay(kv, distance)
    for kv in range(1, kv_count):
        arrive(kv)
    for copy in spread:
        copy.wait()
    for copy in started:
        copy.wait_send()


def gather(
    hidden_in,
    norm_gain,
    query_weight,
    key_weight,
    value_weight,
    key_cache,
    value_cache,
    cached_lengths,
    group_ids,
    prompt_pages,
    own_pages,
    out_weight,
    seq_count,
    tensor_count,
    early,
):
    tok_rows = hidden_in.shape[0]
    q_cols, kv_cols = query_weight.shape[1], key_weight.shape[1]
    kv_count = kv_cols // HEAD_DIM
    per_kv = q_cols // kv_cols
    slots = pltpu.SemaphoreType.DMA((kv_count, seq_count // 2))
    vmem = pl.BlockSpec(memory_space=pltpu.VMEM)
    hbm = pl.BlockSpec(memory_space=pltpu.HBM)
    fresh = jax.ShapeDtypeStruct((tok_rows, kv_cols), jnp.bfloat16)
    rows = per_kv * HEAD_DIM + EXTRA
    out_shape = [
        jax.ShapeDtypeStruct((seq_count, kv_count, rows, tok_rows), jnp.bfloat16),
        fresh,
        fresh,
        jax.ShapeDtypeStruct((LINES, PAGE_ROWS), jnp.int32),
        jax.ShapeDtypeStruct(key_cache.shape, key_cache.dtype),
        jax.ShapeDtypeStruct(value_cache.shape, value_cache.dtype),
        jax.ShapeDtypeStruct(
            (tensor_count, per_kv * HEAD_DIM, out_weight.shape[1] // tensor_count), jnp.bfloat16
        ),
    ]
    if early:
        sums = (REQUESTS, HEAD_DIM + EXTRA, per_kv * ADDED_TOKENS)
        out_shape += [
            jax.ShapeDtypeStruct(sums, jnp.float32),
            jax.ShapeDtypeStruct((PAGE_ROWS, HEAD_DIM), jnp.float32),
        ]
    return pl.pallas_call(
        functools.partial(gather_kernel, seq_count, early),
        out_shape=tuple(out_shape),
        in_specs=[hbm] * 12,
        out_specs=(vmem,) * len(out_shape),
        scratch_shapes=[slots] * 4
        + [
            pltpu.VMEM(weight.shape, weight.dtype)
            for weight in (query_weight, key_weight, value_weight, hidden_in)
        ]
        + [
            pltpu.SemaphoreType.DMA((12,)),
            pltpu.SMEM((LINES, PAGE_ROWS), jnp.int32),
            pltpu.VMEM((1, norm_gain.shape[0]), norm_gain.dtype),
            pltpu.SMEM(cached_lengths.shape, jnp.int32),
            pltpu.SMEM(group_ids.shape, jnp.int32),
            pltpu.VMEM(prompt_pages.shape, jnp.int32),
            pltpu.VMEM(own_pages.shape, jnp.int32),
            pltpu.SemaphoreType.DMA((tensor_count,)),
            pltpu.SemaphoreType.DMA((tensor_count,)),
        ],
        compiler_params=pltpu.CompilerParams(
            collective_id=0, has_side_effects=True, vmem_limit_bytes=40 << 20
        ),
    )(
        in_hbm(hidden_in),
        in_hbm(norm_gain.reshape(1, -1)),
        in_hbm(query_weight),
        in_hbm(key_weight),
        in_hbm(value_weight),
        in_hbm(key_cache),
        in_hbm(value_cache),
        in_hbm(out_weight),
        in_hbm(cached_lengths),
        in_hbm(group_ids),
        in_hbm(prompt_pages),
        in_hbm(own_pages),
    )


def finish_kernel(seq_count, tensor_count, kv_count, early, *refs):
    refs = list(refs)
    known = kv_count - 1 if early else kv_count
    part_refs, ls_refs = refs[:known], refs[known : 2 * known]
    del refs[: 2 * known]
    if early:
        left_ref, left_m_ref, packed_ref, qt_ref, kc_ref, vc_ref = refs[:6]
        del refs[:6]
    w_early, w_hbm, out_ref = refs[:3]
    mix_ref, mix_got, mls_ref, side_got, sls_ref, gls_ref = refs[3:9]
    w_late, att_ref = refs[9:11]
    side_send, side_recv, sls_send, sls_recv, mix_send, mix_recv, mls_send, mls_recv = refs[11:19]
    w_send, w_recv, far_send, far_recv, near_send, near_recv = refs[19:25]
    del refs[:25]
    if early:
        late_ref, lists, list_sem = refs[2:]
        part_refs = part_refs + refs[:1]
        ls_refs = ls_refs + refs[1:2]
        fetch = pltpu.make_async_copy(packed_ref, lists, list_sem)
        fetch.start()
    tok_rows, out_cols = out_ref.shape
    per_kv = part_refs[0].shape[1] // HEAD_DIM
    me = lax.axis_index("seq")
    tensor = lax.axis_index("tensor")
    pair, core = tensor // 2, tensor % 2
    pairs = tensor_count // 2
    twin = (me, pair * 2 + 1 - core)
    outer = seq_count // 2
    place, side = me // 2, me % 2
    beside = (place * 2 + 1 - side, tensor)
    order = sorted(range(1, outer), key=lambda distance: -min(distance, outer - distance))

    def far_pair(distance):
        return (pair + distance) % pairs

    def line(distance, which):
        return (place + distance) % outer * 2 + which

    greet(
        [beside]
        + [(line(distance, side), tensor) for distance in range(1, outer)]
        + [twin]
        + [(me, far_pair(distance) * 2 + core) for distance in range(1, pairs)]
        + [(me, far_pair(distance) * 2 + 1 - core) for distance in range(1, pairs)]
    )
    greeted(outer + tensor_count - 1)
    started = []
    scales, sides, mixes, mix_scales, shares = {}, {}, {}, {}, {}

    def begin(table, key, *rest):
        table[key] = remote(*rest)
        table[key].start()
        started.append(table[key])

    def send_sides(kv):
        for distance in order + [0]:
            begin(
                scales,
                (kv, distance),
                ls_refs[kv].at[line(distance, 1 - side)],
                sls_ref.at[kv, distance],
                sls_send.at[kv, distance],
                sls_recv.at[kv, distance],
                beside,
            )
        for distance in order + [0]:
            begin(
                sides,
                (kv, distance),
                part_refs[kv].at[line(distance, 1 - side)],
                side_got.at[kv, distance],
                side_send.at[kv, distance],
                side_recv.at[kv, distance],
                beside,
            )

    def weighted(block, share):
        return [
            block[cols(sub)].astype(jnp.float32) * share[sub : sub + 1] for sub in range(per_kv)
        ]

    def plus(left, right):
        return [one + other for one, other in zip(left, right)]

    def weigh(kv):
        for distance in order + [0]:
            scales[kv, distance].wait_recv()
        own_lines = jnp.stack([ls_refs[kv][line(distance, side)] for distance in range(outer)])
        side_lines = sls_ref[kv]
        top = jnp.maximum(own_lines, side_lines)
        own_scale, side_scale = jnp.exp(own_lines - top), jnp.exp(side_lines - top)
        both = own_scale + side_scale
        mls_ref[kv] = top + jnp.log(both)
        for distance in order:
            begin(
                mix_scales,
                (kv, distance),
                mls_ref.at[kv, distance],
                gls_ref.at[kv, distance],
                mls_send.at[kv, distance],
                mls_recv.at[kv, distance],
                (line(distance, side), tensor),
            )
        shares[kv] = own_scale / both, side_scale / both

    def mixed(kv, distance):
        sides[kv, distance].wait_recv()
        own_shares, side_shares = shares[kv]
        return plus(
            weighted(part_refs[kv][line(distance, side)], own_shares[distance]),
            weighted(side_got[kv, distance], side_shares[distance]),
        )

    def send_mix(kv, distance):
        mix_ref[kv, distance] = jnp.concatenate(mixed(kv, distance), axis=0).astype(jnp.bfloat16)
        begin(
            mixes,
            (kv, distance),
            mix_ref.at[kv, distance],
            mix_got.at[kv, distance],
            mix_send.at[kv, distance],
            mix_recv.at[kv, distance],
            (line(distance, side), tensor),
        )

    def merged(kv):
        gls_ref[kv, 0] = mls_ref[kv, 0]
        for distance in order:
            mix_scales[kv, distance].wait_recv()
        lines = gls_ref[kv]
        lines = jnp.exp(lines - jnp.max(lines, axis=0, keepdims=True))
        share = lines / jnp.sum(lines, axis=0, keepdims=True)
        total = [block * share[0][sub : sub + 1] for sub, block in enumerate(mixed(kv, 0))]
        for distance in order:
            mixes[kv, distance].wait_recv()
            total = plus(total, weighted(mix_got[kv, distance], share[distance]))
        return jnp.concatenate(total, axis=0).astype(jnp.bfloat16)

    def twin_copy(kv, distance, which):
        block = att_ref.at[(pair + pairs - distance) % pairs * 2 + which, kv]
        return remote(block, block, near_send.at[kv, distance], near_recv.at[kv, distance], twin)

    def far_copy(kv, distance, source, target):
        block = att_ref.at[source, kv]
        return remote(
            block, block, far_send.at[kv, distance], far_recv.at[kv, distance], (me, target)
        )

    def share_out(kv, attention):
        att_ref[tensor, kv] = attention
        copies = [
            far_copy(kv, distance, tensor, far_pair(distance) * 2 + core)
            for distance in range(1, pairs)
        ]
        copies.append(twin_copy(kv, 0, core))
        for copy in copies:
            copy.start()
            started.append(copy)

    def pass_on(kv):
        for distance in range(1, pairs):
            source = far_pair(pairs - distance) * 2 + core
            far_copy(kv, distance, source, source).wait_recv()
            copy = twin_copy(kv, distance, core)
            copy.start()
            started.append(copy)

    def terms_of(kv, source):
        rest = (kv - 1) * per_kv * HEAD_DIM
        if kv == 0:
            weight = w_early[source]
        else:
            weight = w_late[source, rest : rest + per_kv * HEAD_DIM, :]
        return lax.dot_general(
            att_ref[source, kv],
            weight,
            (((0,), (0,)), ((), ())),
            preferred_element_type=jnp.float32,
        )

    def own_terms(kv):
        return terms_of(kv, tensor)

    def far_terms(kv):
        total = None
        for distance in range(1, pairs):
            fresh = terms_of(kv, far_pair(distance) * 2 + core)
            total = fresh if total is None else total + fresh
        return total

    def twin_terms(kv):
        total = None
        for distance in range(pairs):
            twin_copy(kv, distance, 1 - core).wait_recv()
            fresh = terms_of(kv, (pair + pairs - distance) % pairs * 2 + 1 - core)
            total = fresh if total is None else total + fresh
        return total

    last = kv_count - 1
    for kv in range(known):
        send_sides(kv)
    spread = spread_columns(w_hbm, per_kv * HEAD_DIM, w_late, tensor_count, w_send, w_recv)
    for copy in spread:
        copy.start()
    if early:
        fetch.wait()
        ls_refs[last][...] = jnp.zeros_like(ls_refs[last])
        steps = [
            (step, request)
            for step in range(early // STEP_PAGES)
            for request in range(REQUESTS)
        ]
        tasks = [(weigh, (kv,)) for kv in range(known)]
        tasks += [(send_mix, (kv, distance)) for kv in range(known) for distance in order]
        share_of = -(-len(tasks) // len(steps))
        for step, request in steps:
            late_ref[request] = (left_ref if step == 0 else late_ref)[request] + early_terms(
                lists,
                qt_ref,
                kc_ref,
                vc_ref,
                left_m_ref[request, 0:1, :],
                request,
                step,
                last,
                per_kv,
            )
            for run, given in tasks[:share_of]:
                run(*given)
            del tasks[:share_of]
        for request in range(REQUESTS):
            settle(
                late_ref[request],
                left_m_ref[request, 0:1, :],
                request,
                part_refs[last],
                ls_refs[last],
                per_kv,
            )
        send_sides(last)
        ready = known
    else:
        ready = 0
    for kv in range(ready, kv_count):
        weigh(kv)
        for distance in order:
            send_mix(kv, distance)
    for kv in range(last):
        share_out(kv, merged(kv))
        pass_on(kv)
    share_out(last, merged(last))
    for copy in spread:
        copy.wait()
    result = own_terms(last)
    for kv in range(last):
        result = result + own_terms(kv) + far_terms(kv) + twin_terms(kv)
    pass_on(last)
    result = result + far_terms(last) + twin_terms(last)
    out_ref[...] = result.astype(jnp.bfloat16)
    for copy in started:
        copy.wait_send()


def finish(parts, scales, leftovers, w_cols, out_weight, seq_count, tensor_count, early):
    q_rows, tok_rows = parts[0].shape[1:]
    kv_count = len(parts) + (1 if early else 0)
    out_cols = out_weight.shape[1] // tensor_count
    pairs = tensor_count // 2
    outer = seq_count // 2
    vmem = pl.BlockSpec(memory_space=pltpu.VMEM)
    w_block = (tensor_count, out_weight.shape[0] - w_cols.shape[1], out_cols)
    att_block = (tensor_count, kv_count, q_rows, tok_rows)
    part_buf = pltpu.VMEM((kv_count, outer, q_rows, tok_rows), jnp.bfloat16)
    scale_buf = pltpu.VMEM((kv_count, outer, LINES, tok_rows), jnp.float32)
    line_sems = pltpu.SemaphoreType.DMA((kv_count, outer))
    pair_sems = pltpu.SemaphoreType.DMA((kv_count, pairs))
    w_sems = pltpu.SemaphoreType.DMA((tensor_count,))
    operands = list(parts) + list(scales) + list(leftovers) + [w_cols, in_hbm(out_weight)]
    scratch = [part_buf, part_buf, scale_buf, part_buf, scale_buf, scale_buf]
    scratch += [pltpu.VMEM(w_block, jnp.bfloat16), pltpu.VMEM(att_block, jnp.bfloat16)]
    scratch += [line_sems] * 8 + [w_sems] * 2 + [pair_sems] * 4
    if early:
        scratch += [
            pltpu.VMEM(parts[0].shape, parts[0].dtype),
            pltpu.VMEM(scales[0].shape, scales[0].dtype),
            pltpu.VMEM(leftovers[0].shape, leftovers[0].dtype),
            pltpu.SMEM(leftovers[2].shape, leftovers[2].dtype),
            pltpu.SemaphoreType.DMA(()),
        ]
    return pl.pallas_call(
        functools.partial(finish_kernel, seq_count, tensor_count, kv_count, early),
        out_shape=jax.ShapeDtypeStruct((tok_rows, out_cols), jnp.bfloat16),
        in_specs=[vmem] * (len(operands) - 1) + [pl.BlockSpec(memory_space=pltpu.HBM)],
        out_specs=vmem,
        scratch_shapes=scratch,
        compiler_params=pltpu.CompilerParams(
            collective_id=1, has_side_effects=True, vmem_limit_bytes=32 << 20
        ),
    )(*operands)


def regroup(array, rows):
    count, width = array.shape[0], array.shape[-1]
    if width == rows:
        return array
    array = jnp.moveaxis(array, 0, -2)
    array = array.reshape(array.shape[:-2] + (count * width // rows, rows))
    return jnp.moveaxis(array, -2, 0)


def body(
    hidden_in,
    norm_gain,
    query_weight,
    key_weight,
    value_weight,
    out_weight,
    key_cache,
    value_cache,
    cached_lengths,
    group_ids,
    prompt_pages,
    own_pages,
):
    tok_rows = hidden_in.shape[0]
    seq_count = lax.axis_size("seq")
    kv_count = key_weight.shape[1] // HEAD_DIM
    split = tok_rows == BLOCK and kv_count > 1
    early = EARLY_STEPS * STEP_PAGES if split else 0
    later = LATE_STEPS * STEP_PAGES if split else 0
    tensor_count = lax.axis_size("tensor")
    queries_t, fresh_k, fresh_v, packed, keys, values, w_cols, *rest = gather(
        hidden_in,
        norm_gain,
        query_weight,
        key_weight,
        value_weight,
        key_cache,
        value_cache,
        cached_lengths,
        group_ids,
        prompt_pages,
        own_pages,
        out_weight,
        seq_count,
        tensor_count,
        early,
    )
    queries_t = regroup(queries_t, BLOCK)
    sums, peak = rest if early else (None, None)
    found = attend(
        packed, queries_t, fresh_k, fresh_v, keys, values, sums, peak, early, later
    )
    known = kv_count - 1 if early else kv_count
    parts = [regroup(array, tok_rows) for array in found[:known]]
    scales = [regroup(array, tok_rows) for array in found[known : 2 * known]]
    leftovers = list(found[2 * known :])
    if early:
        leftovers += [queries_t, keys, values]
    return finish(
        parts, scales, leftovers, w_cols, out_weight, seq_count, tensor_count, later
    )


def solution(mesh):
    in_specs = (
        P("seq", None),
        P(),
        P(None, "tensor"),
        P(None, "tensor"),
        P(None, "tensor"),
        P("tensor", None),
        P("seq", None, "tensor"),
        P("seq", None, "tensor"),
        P(),
        P(),
        P(),
        P(),
    )
    out_specs = P("seq", "tensor")
    return jax.shard_map(body, mesh=mesh, in_specs=in_specs, out_specs=out_specs, check_vma=False)
```
